32 devices in a mesh: dp: 4 (over z), ctx: 4 (over x, core), tp: 2 (over y).
Axes of the slice: x: 2, y: 2, z: 4, core: 2. Of those that a mesh axis runs over, the one named last changes fastest.
Arguments:
- hidden_in: bfloat16 [8, 1536, 1024], P('dp', 'ctx'), may hold values from -6 to 6
- positions: int32 [8, 1536], P('dp', 'ctx'), may hold values from 0 to 2046, as said below
- valid_mask: int32 [8, 1536], P('dp', 'ctx'), may hold values from 0 to 1, as said below
- teacher: bfloat16 [8, 1536, 1024], P('dp', 'ctx'), may hold values from -6 to 6
- cotangent: bfloat16 [8, 1536, 1024], P('dp', 'ctx'), may hold values from -6 to 6
- mixer_gain: float32 [1024], replicated, may hold values from 0.5 to 1.5
- query_weight: bfloat16 [1024, 512], P(('dp', 'ctx'), 'tp'), may hold values from -0.1875 to 0.1875
- keyvalue_projection_weight: bfloat16 [1024, 2, 128], P(('dp', 'ctx'), None, 'tp'), may hold values from -0.1875 to 0.1875
- attnout_weight: bfloat16 [512, 1024], P('tp', ('dp', 'ctx')), may hold values from -3 to 3
- stream_weight: bfloat16 [1024, 2, 1536], P(('dp', 'ctx'), None, 'tp'), may hold values from -0.1875 to 0.1875
- state_weight: bfloat16 [1024, 256], P(('dp', 'ctx')), may hold values from -0.1875 to 0.1875
- step_weight: bfloat16 [1024, 24], P(('dp', 'ctx'), 'tp'), may hold values from -0.1875 to 0.1875
- conv_stream: float32 [4, 1536], P(None, 'tp'), may hold values from -3 to 3
- bias_stream: float32 [1536], P('tp'), may hold values from -3 to 3
- conv_state: float32 [4, 256], replicated, may hold values from -3 to 3
- bias_state: float32 [256], replicated, may hold values from -3 to 3
- step_bias: float32 [24], P('tp'), may hold values from -7 to -4
- decay_log: float32 [24], P('tp'), may hold values from -2 to 1
- skip_scale: float32 [24], P('tp'), may hold values from 0.5 to 1.5
- mambaout_weight: bfloat16 [1536, 1024], P('tp', ('dp', 'ctx')), may hold values from -0.03125 to 0.03125
- ffn_gain: float32 [1024], replicated, may hold values from 0.5 to 1.5
- gateup_weight: bfloat16 [1024, 2, 2048], P(('dp', 'ctx'), None, 'tp'), may hold values from -0.1875 to 0.1875
- down_weight: bfloat16 [2048, 1024], P('tp', ('dp', 'ctx')), may hold values from -0.125 to 0.125
Outputs:
- block_out: bfloat16 [8, 1536, 1024], P('dp', 'ctx')
- loss: float32 [], replicated
- input_grad: bfloat16 [8, 1536, 1024], P('dp', 'ctx')
- mixgain_grad: float32 [1024], replicated
- query_grad: float32 [1024, 512], P(('dp', 'ctx'), 'tp')
- keyval_grad: float32 [1024, 2, 128], P(('dp', 'ctx'), None, 'tp')
- attnout_grad: float32 [512, 1024], P('tp', ('dp', 'ctx'))
- stream_grad: float32 [1024, 2, 1536], P(('dp', 'ctx'), None, 'tp')
- state_grad: float32 [1024, 256], P(('dp', 'ctx'))
- step_grad: float32 [1024, 24], P(('dp', 'ctx'), 'tp')
- convstream_grad: float32 [4, 1536], P(None, 'tp')
- biasstream_grad: float32 [1536], P('tp')
- convstate_grad: float32 [4, 256], replicated
- biasstate_grad: float32 [256], replicated
- stepbias_grad: float32 [24], P('tp')
- decay_grad: float32 [24], P('tp')
- skip_grad: float32 [24], P('tp')
- mambaout_grad: float32 [1536, 1024], P('tp', ('dp', 'ctx'))
- ffngain_grad: float32 [1024], replicated
- gateup_grad: float32 [1024, 2, 2048], P(('dp', 'ctx'), None, 'tp')
- down_grad: float32 [2048, 1024], P('tp', ('dp', 'ctx'))
The draws below stay inside these ranges and needn't reach their ends.
Inputs may be any that keep to these rules, and one draw needn't show every extreme that they name: Within each sequence the positions rise by one from token to token, starting at an offset of 0 to 511; some sequence starts at 0 and some at 511. `valid_mask`: 1 marks a valid token; the first token of every sequence is valid.
All inputs are finite; a program needn't handle non-finite values.
Results may differ from the reference program's by a relative error of at most 0.015.
Values may be sent and summed in bfloat16 or wider, within the bound.
No kernel may reach another device: no remote copies, remote signals or barrier semaphores. Data moves between devices by JAX's collectives and lax.ppermute only.
A program may use at most 192 MiB of HBM per device.

```python
import jax
import jax.numpy as jnp
from jax import lax

MODEL_WIDTH = 1024
HQ = 8
KEYVALUE_HEADS = 2
HEAD_SIZE = 64
MH = 24
MP = 64
NS = 128
KC = 4
FF = 2048
SPAN = 128
QBLK = 512
LENGTH = 1536
SEQS = 8


def draw_positions(key, part):
    offsets = jax.random.randint(key, (SEQS, 1), 0, 512, dtype=jnp.int32)
    offsets = offsets.at[0, 0].set(0).at[SEQS - 1, 0].set(511)
    return offsets + jnp.arange(LENGTH, dtype=jnp.int32)[None, :]


def draw_valid_mask(key, part):
    places = jnp.arange(SEQS * LENGTH, dtype=jnp.int32).reshape(SEQS, LENGTH)
    keep_levels = 250 + 700 * places // (SEQS * LENGTH)
    random_rolls = jax.random.randint(key, (SEQS, LENGTH), 0, 1000, dtype=jnp.int32)
    first_token = jnp.arange(LENGTH, dtype=jnp.int32)[None, :] == 0
    return jnp.where(first_token | (random_rolls < keep_levels), 1, 0).astype(jnp.int32)


def block_levels(stream_key, dims, split, low, top_value):
    def one(axis_at, shards_of):
        heights = jax.random.uniform(jax.random.fold_in(jax.random.fold_in(stream_key, 6), axis_at), (shards_of,), jnp.float32, low / len(split), top_value / len(split))
        return jnp.repeat(jnp.exp(heights), dims[axis_at] // shards_of).reshape((-1,) + (1,) * (len(dims) - axis_at - 1))

    level = one(*split[0])
    for cut in split[1:]:
        level = level * one(*cut)
    return level


def centred(rng, dims, spread, bound, cuts=(), held_as=jnp.bfloat16):
    drawn = spread * jax.random.normal(rng, dims, jnp.float32)
    if cuts:
        drawn = drawn * block_levels(rng, dims, cuts, -0.22, 0.18)
    return jnp.clip(drawn, -bound, bound).astype(held_as)


def setup_inputs(seed: int = 0) -> dict:
    seeds = jax.random.split(jax.random.key(seed), 24)
    hidden_in = centred(seeds[0], (SEQS, LENGTH, MODEL_WIDTH), 1.0, 6.0, ((0, 4), (1, 4)))
    positions = draw_positions(jax.random.fold_in(seeds[23], 71), 0)
    valid_mask = draw_valid_mask(jax.random.fold_in(seeds[23], 71), 0)
    teacher = centred(seeds[3], (SEQS, LENGTH, MODEL_WIDTH), 1.0, 6.0, ((0, 4), (1, 4)))
    cotangent = centred(seeds[4], (SEQS, LENGTH, MODEL_WIDTH), 1.0, 6.0, ((0, 4), (1, 4)))
    mixer_gain = jnp.clip(1.0 + 0.1 * jax.random.normal(seeds[5], (MODEL_WIDTH,), jnp.float32), 0.5, 1.5)
    query_weight = centred(seeds[6], (MODEL_WIDTH, HQ * HEAD_SIZE), MODEL_WIDTH ** -0.5, 0.1875, ((0, 16), (1, 2)))
    keyvalue_projection_weight = centred(seeds[7], (MODEL_WIDTH, 2, KEYVALUE_HEADS * HEAD_SIZE), MODEL_WIDTH ** -0.5, 0.1875, ((0, 16), (2, 2)))
    attnout_weight = centred(seeds[8], (HQ * HEAD_SIZE, MODEL_WIDTH), 4 ** -0.5, 3.0, ((0, 2), (1, 16)))
    stream_weight = centred(seeds[9], (MODEL_WIDTH, 2, MH * MP), MODEL_WIDTH ** -0.5, 0.1875, ((0, 16), (2, 2)))
    state_weight = centred(seeds[10], (MODEL_WIDTH, 2 * NS), MODEL_WIDTH ** -0.5, 0.1875, ((0, 16),))
    step_weight = centred(seeds[11], (MODEL_WIDTH, MH), MODEL_WIDTH ** -0.5, 0.1875, ((0, 16), (1, 2)))
    conv_stream = centred(seeds[12], (KC, MH * MP), 0.5, 3.0, ((1, 2),), jnp.float32)
    bias_stream = centred(seeds[13], (MH * MP,), 0.5, 3.0, ((0, 2),), jnp.float32)
    conv_state = centred(seeds[14], (KC, 2 * NS), 0.5, 3.0, (), jnp.float32)
    bias_state = centred(seeds[15], (2 * NS,), 0.5, 3.0, (), jnp.float32)
    step_bias = jnp.clip(-7.0 + 3.0 * jax.random.uniform(seeds[16], (MH,), jnp.float32) ** block_levels(seeds[16], (MH,), ((0, 2),), -0.2, 0.2), -7.0, -4.0)
    decay_log = jnp.clip(-2.0 + 3.0 * jax.random.uniform(seeds[17], (MH,), jnp.float32) ** block_levels(seeds[17], (MH,), ((0, 2),), -0.2, 0.2), -2.0, 1.0)
    skip_scale = jnp.clip(0.5 + 1.0 * jax.random.uniform(seeds[18], (MH,), jnp.float32) ** block_levels(seeds[18], (MH,), ((0, 2),), -0.2, 0.2), 0.5, 1.5)
    mambaout_weight = centred(seeds[19], (MH * MP, MODEL_WIDTH), (25 * MH * MP) ** -0.5, 0.03125, ((0, 2), (1, 16)))
    ffn_gain = jnp.clip(1.0 + 0.1 * jax.random.normal(seeds[20], (MODEL_WIDTH,), jnp.float32), 0.5, 1.5)
    gateup_weight = centred(seeds[21], (MODEL_WIDTH, 2, FF), MODEL_WIDTH ** -0.5, 0.1875, ((0, 16), (2, 2)))
    down_weight = centred(seeds[22], (FF, MODEL_WIDTH), FF ** -0.5, 0.125, ((0, 2), (1, 16)))
    return dict(hidden_in=hidden_in, positions=positions, valid_mask=valid_mask, teacher=teacher, cotangent=cotangent, mixer_gain=mixer_gain, query_weight=query_weight, keyvalue_projection_weight=keyvalue_projection_weight, attnout_weight=attnout_weight, stream_weight=stream_weight, state_weight=state_weight, step_weight=step_weight, conv_stream=conv_stream, bias_stream=bias_stream, conv_state=conv_state, bias_state=bias_state, step_bias=step_bias, decay_log=decay_log, skip_scale=skip_scale, mambaout_weight=mambaout_weight, ffn_gain=ffn_gain, gateup_weight=gateup_weight, down_weight=down_weight)


eps_norm = 1e-05
rope_base = 100000000000.0
highest = lax.Precision.HIGHEST

@jax.custom_vjp
def low(v):
    return lax.optimization_barrier(v.astype(jnp.bfloat16)).astype(jnp.float32)

@jax.custom_vjp
def low_back(v):
    return v

def low_keep(v):
    return (low(v), None)

def low_pass(kept, grad):
    return (grad,)

def back_keep(v):
    return (v, None)

def back_low(kept, grad):
    return (low(grad),)
low.defvjp(low_keep, low_pass)
low_back.defvjp(back_keep, back_low)

def matmul_high(left, right):
    return jnp.dot(left, right, precision=highest, preferred_element_type=jnp.float32)

def rms_norm(values, gain):
    return values * lax.rsqrt(lax.optimization_barrier(jnp.mean(values * values, -1, keepdims=True)) + eps_norm) * gain

def rotary(values, places):
    half = values.shape[-1] // 2
    freqs = rope_base ** (-2.0 * jnp.arange(half, dtype=jnp.float32) / values.shape[-1])
    angles = places.astype(jnp.float32)[..., None] * freqs
    cosine = jnp.cos(angles)[..., None, :]
    sine = jnp.sin(angles)[..., None, :]
    first = values[..., :half]
    second = values[..., half:]
    return jnp.concatenate([first * cosine - second * sine, second * cosine + first * sine], -1)

def causal_conv(pre, prev, taps, bias):
    sequence_length = pre.shape[-2]
    extended = jnp.concatenate([prev, pre], -2)
    total = bias + taps[0] * extended[..., 0:sequence_length, :]
    for offset in range(1, taps.shape[0]):
        total = total + taps[offset] * extended[..., offset:offset + sequence_length, :]
    return jax.nn.silu(total)

def block_terms(stream, steps, rate, entry_map, read_map):
    sequence_length = stream.shape[0]
    logs = jnp.cumsum(-steps * rate, axis=0)
    gaps = logs.T[:, :, None] - logs.T[:, None, :]
    places = jnp.arange(sequence_length, dtype=jnp.int32)
    causal = places[:, None] >= places[None, :]
    decay = jnp.where(causal, jnp.exp(jnp.where(causal, gaps, 0.0)), 0.0)
    inner = jnp.dot(read_map, entry_map.T, precision=highest, preferred_element_type=jnp.float32)
    weighted = steps[:, :, None] * stream
    local_out = jnp.einsum('hts,ts,shp->thp', decay, inner, weighted, precision=highest)
    tail = jnp.exp(logs[-1][None, :] - logs)
    local_state = jnp.einsum('sh,shp,sn->hpn', tail, weighted, entry_map, precision=highest)
    return (local_out, local_state, jnp.exp(logs[-1]), logs)

def state_terms(logs, read_map, carried):
    return jnp.einsum('tn,hpn->thp', read_map, carried, precision=highest) * jnp.exp(logs)[:, :, None]

def scan_mixer(stream, steps, rate, entry_map, read_map):
    sequence_length, heads, width = stream.shape
    blocks = sequence_length // SPAN

    def advance(carried, pieces):
        piece_stream, piece_steps, piece_entry, piece_read = pieces
        local_out, local_state, total, logs = block_terms(piece_stream, piece_steps, rate, piece_entry, piece_read)
        return (total[:, None, None] * carried + local_state, local_out + state_terms(logs, piece_read, carried))
    start = jnp.zeros((heads, width, entry_map.shape[-1]), jnp.float32)
    _, outputs = lax.scan(jax.checkpoint(advance), start, (stream.reshape(blocks, SPAN, heads, width), steps.reshape(blocks, SPAN, heads), entry_map.reshape(blocks, SPAN, -1), read_map.reshape(blocks, SPAN, -1)))
    return outputs.reshape(sequence_length, heads, width)

def attention(queries, keys, values):
    sequence_length, heads, width = queries.shape
    group = heads // keys.shape[1]
    keys_wide = jnp.repeat(keys, group, axis=1)
    values_wide = jnp.repeat(values, group, axis=1)
    scale = width ** (-0.5)
    blocks = sequence_length // QBLK

    def one_block(pieces):
        query_block, start = pieces
        scores = low_back(jnp.einsum('ihd,jhd->hij', query_block, keys_wide, precision=highest)) * scale
        rows = start + jnp.arange(QBLK, dtype=jnp.int32)
        allowed = jnp.arange(sequence_length, dtype=jnp.int32)[None, :] <= rows[:, None]
        scores = jnp.where(allowed[None], scores, -1e+30)
        top_score = lax.optimization_barrier(jnp.max(scores, -1, keepdims=True))
        expo = jnp.exp(scores - top_score)
        probs = low(expo / lax.optimization_barrier(jnp.sum(expo, -1, keepdims=True)))
        return jnp.einsum('hij,jhd->ihd', probs, values_wide, precision=highest)
    starts = jnp.arange(blocks, dtype=jnp.int32) * QBLK
    outputs = lax.map(jax.checkpoint(one_block), (queries.reshape(blocks, QBLK, heads, width), starts))
    return outputs.reshape(sequence_length, heads * width)

def layer(hidden, places, params):
    mixer_gain, query_weight, keyvalue_projection_weight, attnout_weight, stream_weight, state_weight, step_weight, conv_stream, bias_stream, conv_state, bias_state, step_bias, decay_log, skip_scale, mambaout_weight, ffn_gain, gateup_weight, down_weight = params
    sequence_length = hidden.shape[0]
    normed = low(rms_norm(hidden, mixer_gain))
    query_pre = low_back(matmul_high(normed, query_weight)).reshape(sequence_length, HQ, HEAD_SIZE)
    keyvalue_projected = low_back(jnp.einsum('ld,dcj->lcj', normed, keyvalue_projection_weight, precision=highest))
    key_before_rotation = keyvalue_projected[:, 0].reshape(sequence_length, KEYVALUE_HEADS, HEAD_SIZE)
    value_projected = keyvalue_projected[:, 1].reshape(sequence_length, KEYVALUE_HEADS, HEAD_SIZE)
    queries = low(rotary(query_pre, places))
    keys = low(rotary(key_before_rotation, places))
    values = low(value_projected)
    attended = low(low_back(attention(queries, keys, values)))
    streams = low_back(jnp.einsum('ld,dcj->lcj', normed, stream_weight, precision=highest))
    gate_z = streams[:, 0]
    stream_pre = streams[:, 1]
    state_pre = matmul_high(normed, state_weight)
    step_raw = low_back(matmul_high(normed, step_weight))
    stream_act = causal_conv(stream_pre, jnp.zeros((KC - 1, stream_pre.shape[1]), jnp.float32), conv_stream, bias_stream)
    state_act = causal_conv(state_pre, jnp.zeros((KC - 1, state_pre.shape[1]), jnp.float32), conv_state, bias_state)
    stream_heads = stream_act.reshape(sequence_length, MH, MP)
    steps = jax.nn.softplus(step_raw + step_bias)
    rate = jnp.exp(decay_log)
    mixer_out = scan_mixer(stream_heads, steps, rate, state_act[:, :NS], state_act[:, NS:])
    gated = (mixer_out + skip_scale[:, None] * stream_heads) * jax.nn.silu(gate_z.reshape(sequence_length, MH, MP))
    gated = low(gated.reshape(sequence_length, MH * MP))
    mixed = low_back(matmul_high(attended, attnout_weight) + matmul_high(gated, mambaout_weight))
    resid = hidden + mixed
    normed_two = low(rms_norm(resid, ffn_gain))
    gateup = low_back(jnp.einsum('ld,dcf->lcf', normed_two, gateup_weight, precision=highest))
    inner = low(jax.nn.silu(gateup[:, 0]) * gateup[:, 1])
    return resid + low_back(matmul_high(inner, down_weight))

def reference(hidden_in, positions, valid_mask, teacher, cotangent, mixer_gain, query_weight, keyvalue_projection_weight, attnout_weight, stream_weight, state_weight, step_weight, conv_stream, bias_stream, conv_state, bias_state, step_bias, decay_log, skip_scale, mambaout_weight, ffn_gain, gateup_weight, down_weight):
    params = tuple((item.astype(jnp.float32) for item in (mixer_gain, query_weight, keyvalue_projection_weight, attnout_weight, stream_weight, state_weight, step_weight, conv_stream, bias_stream, conv_state, bias_state, step_bias, decay_log, skip_scale, mambaout_weight, ffn_gain, gateup_weight, down_weight)))
    valid_count = jnp.sum(valid_mask).astype(jnp.float32)
    mask_float = valid_mask.astype(jnp.float32)
    target_all = teacher.astype(jnp.float32)
    cot_all = cotangent.astype(jnp.float32)
    hidden_all = hidden_in.astype(jnp.float32)

    def objective(hidden, weights):

        def per_seq(total, pieces):
            hidden_seq, places, mask_seq, target_seq, cot_seq = pieces
            out_seq = layer(hidden_seq, places, weights)
            diff = out_seq - target_seq
            squares = jnp.sum(mask_seq[:, None] * diff * diff)
            value = jnp.sum(out_seq * cot_seq) + squares / (valid_count * MODEL_WIDTH)
            return (total + value, (out_seq, squares))
        total, extras = lax.scan(jax.checkpoint(per_seq), jnp.zeros((), jnp.float32), (hidden, positions, mask_float, target_all, cot_all))
        return (total, extras)
    value, pullback, extras = jax.vjp(objective, hidden_all, params, has_aux=True)
    outputs, squares = extras
    hidden_grad, grads = pullback(jnp.ones((), jnp.float32))
    loss = jnp.sum(squares) / (valid_count * MODEL_WIDTH)
    return (outputs.astype(jnp.bfloat16), loss, hidden_grad.astype(jnp.bfloat16), grads[0], grads[1], grads[2], grads[3], grads[4], grads[5], grads[6], grads[7], grads[8], grads[9], grads[10], grads[11], grads[12], grads[13], grads[14], grads[15], grads[16], grads[17])
```

```python
import jax
import jax.numpy as jnp
from jax import lax
from jax.sharding import PartitionSpec as P

HEAD_SIZE = 64
MP = 64
NS = 128
KC = 4
CBLK = 128


eps_norm = 1e-05
rope_base = 100000000000.0
highest = lax.Precision.HIGHEST


def passed_along(block, axis, distance):
    devices = range(lax.axis_size(axis))
    route = [(i - distance, i) for i in devices if i - distance in devices]
    return lax.ppermute(block, axis, route)


def prefix_2(part, axis, combine, identity, reverse):
    count = lax.axis_size(axis)
    place = lax.axis_index(axis)
    ahead = count - 1 - place if reverse else place
    gathered = jax.tree.map(lambda a: lax.all_gather(a, axis), part)
    state = jax.tree.map(lambda a, e: jnp.zeros_like(a) + jnp.asarray(e, a.dtype), part, identity)

    def one(turn, state):
        source = count - 1 - turn if reverse else turn
        return combine(
            state, jax.tree.map(lambda a: lax.dynamic_index_in_dim(a, source, 0, False), gathered)
        )

    return lax.fori_loop(0, ahead, one, state)


def rms_norm(values, gain):
    return values * lax.rsqrt(jnp.mean(values * values, -1, keepdims=True) + eps_norm) * gain


def rotary(values, places):
    half = values.shape[-1] // 2
    freqs = rope_base ** (-2.0 * jnp.arange(half, dtype=jnp.float32) / values.shape[-1])
    angles = places.astype(jnp.float32)[..., None] * freqs
    cosine = jnp.cos(angles)[..., None, :]
    sine = jnp.sin(angles)[..., None, :]
    first = values[..., :half]
    second = values[..., half:]
    return jnp.concatenate([first * cosine - second * sine, second * cosine + first * sine], -1)


def causal_conv(pre, prev, taps, bias):
    sequence_length = pre.shape[-2]
    extended = jnp.concatenate([prev, pre], -2)
    total = bias + taps[0] * extended[..., 0:sequence_length, :]
    for offset in range(1, taps.shape[0]):
        total = total + taps[offset] * extended[..., offset : offset + sequence_length, :]
    return jax.nn.silu(total)


def running_sum(terms):
    places = jnp.arange(terms.shape[0], dtype=jnp.int32)
    lower = (places[:, None] >= places[None, :]).astype(jnp.float32)
    return jnp.dot(lower, terms, precision=highest)


def pair_sum(parts):
    if lax.axis_size("tp") != 2:
        return jax.tree.map(lambda a: lax.psum(a, "tp"), parts)
    low = jax.tree.map(lambda a: a.astype(jnp.bfloat16), parts)
    other = jax.tree.map(lambda a: lax.ppermute(a, "tp", [(0, 1), (1, 0)]), low)
    return jax.tree.map(lambda a, b: a.astype(jnp.float32) + b.astype(jnp.float32), low, other)


def block_terms(stream, steps, rate, entry_map, read_map):
    sequence_length = stream.shape[0]
    logs = running_sum(-steps * rate)
    gaps = logs.T[:, :, None] - logs.T[:, None, :]
    places = jnp.arange(sequence_length, dtype=jnp.int32)
    causal = places[:, None] >= places[None, :]
    decay = jnp.where(causal, jnp.exp(jnp.where(causal, gaps, 0.0)), 0.0)
    inner = jnp.dot(read_map, entry_map.T, precision=highest, preferred_element_type=jnp.float32)
    weighted = steps[:, :, None] * stream
    local_out = jnp.einsum("hts,ts,shp->thp", decay, inner, weighted, precision=highest)
    tail = jnp.exp(logs[-1][None, :] - logs)
    local_state = jnp.einsum("sh,shp,sn->hpn", tail, weighted, entry_map, precision=highest)
    return (local_out, local_state, jnp.exp(logs[-1]), logs)


def state_terms(logs, read_map, carried):
    return (
        jnp.einsum("tn,hpn->thp", read_map, carried, precision=highest) * jnp.exp(logs)[:, :, None]
    )


def local_part(stream_act, state_act, step_raw, step_bias, decay_log):
    seq_count, tokens, channels = stream_act.shape
    heads_here = step_raw.shape[-1]
    stream_heads = stream_act.reshape(seq_count, tokens, heads_here, MP)
    steps = jax.nn.softplus(step_raw + step_bias)
    rate = jnp.exp(decay_log)
    local_out, local_state, totals, logs = jax.vmap(block_terms, in_axes=(0, 0, None, 0, 0))(
        stream_heads, steps, rate, state_act[..., :NS], state_act[..., NS:]
    )
    return (local_out, local_state, totals)


def finish(
    gate_z, stream_act, state_act, step_raw, step_bias, decay_log, skip_scale, local_out, carried
):
    seq_count, tokens, channels = stream_act.shape
    heads_here = step_raw.shape[-1]
    stream_heads = stream_act.reshape(seq_count, tokens, heads_here, MP)
    steps = jax.nn.softplus(step_raw + step_bias)
    logs = jax.vmap(running_sum)(-steps * jnp.exp(decay_log))
    incoming = jax.vmap(state_terms)(logs, state_act[..., NS:], carried)
    mixer_out = local_out + incoming
    gated = (mixer_out + skip_scale[:, None] * stream_heads) * jax.nn.silu(
        gate_z.reshape(seq_count, tokens, heads_here, MP)
    )
    return gated.reshape(seq_count, tokens, channels)


def chain(earlier, later):
    return (earlier[0] * later[0], later[0][..., None, None] * earlier[1] + later[1])


def swiglu(pair):
    return jax.nn.silu(pair[:, :, 0]) * pair[:, :, 1]


def per_device(
    hidden_in,
    positions,
    valid_mask,
    teacher,
    cotangent,
    mixer_gain,
    query_weight,
    keyvalue_projection_weight,
    attnout_weight,
    stream_weight,
    state_weight,
    step_weight,
    conv_stream,
    bias_stream,
    conv_state,
    bias_state,
    step_bias,
    decay_log,
    skip_scale,
    mambaout_weight,
    ffn_gain,
    gateup_weight,
    down_weight,
):
    low, f32 = jnp.bfloat16, jnp.float32
    seq_count, tokens, width = hidden_in.shape
    owners = ("dp", "ctx")
    rows = query_weight.shape[0]
    q_cols = query_weight.shape[1]
    kv_cols = keyvalue_projection_weight.shape[2]
    channels = stream_weight.shape[2]
    bc_cols = state_weight.shape[1]
    heads = step_weight.shape[1]
    hidden_units = gateup_weight.shape[2]
    step_cols = 128

    tallies = jnp.sum(valid_mask.reshape(seq_count * tokens // CBLK, CBLK), -1).astype(low)
    spare = jnp.zeros((rows, step_cols - heads), low)
    spare = spare.at[0, : tallies.shape[0]].set(tallies)
    mixer_shard = jnp.concatenate(
        [
            stream_weight.reshape(rows, 2 * channels),
            state_weight,
            query_weight,
            keyvalue_projection_weight.reshape(rows, 2 * kv_cols),
            step_weight,
            spare,
        ],
        1,
    )
    mixer_full = lax.all_gather(mixer_shard, owners, axis=0, tiled=True)
    out_shard = jnp.concatenate([attnout_weight.T, mambaout_weight.T], 1)
    ffn_shard = jnp.concatenate([gateup_weight.reshape(rows, 2 * hidden_units), out_shard], 1)
    ffn_full = lax.all_gather(ffn_shard, owners, axis=0, tiled=True)
    gateup_full = ffn_full[:, : 2 * hidden_units]
    out_full_w = ffn_full[:, 2 * hidden_units :]
    down_full = lax.all_gather(down_weight.T, owners, axis=0, tiled=True)

    edges = [0]
    for size in (channels, channels, bc_cols, q_cols, kv_cols, kv_cols, heads):
        edges.append(edges[-1] + size)
    all_cols = mixer_full.shape[1]

    counts = mixer_full.reshape(-1, rows, all_cols)[:, 0, edges[7] : edges[7] + tallies.shape[0]]
    valid_total = jnp.sum(counts.astype(f32))
    ctx_index = lax.axis_index("ctx")
    rim = KC - 1
    hidden = hidden_in.astype(f32)
    normed = rms_norm(hidden, mixer_gain).astype(low)
    query_heads = q_cols // HEAD_SIZE
    kv_heads = kv_cols // HEAD_SIZE
    group = query_heads // kv_heads
    pre = jnp.einsum("std,dc->stc", normed, mixer_full, preferred_element_type=f32)
    gate_z, stream_pre, state_pre, query_pre, key_pre, value_projected, step_raw = (
        pre[..., edges[i] : edges[i + 1]] for i in range(7)
    )
    query_pre = query_pre.reshape(seq_count, tokens, query_heads, HEAD_SIZE)
    key_before_rotation = key_pre.reshape(seq_count, tokens, kv_heads, HEAD_SIZE)
    queries = rotary(query_pre, positions).astype(low)
    keys_mine = (
        rotary(key_before_rotation, positions)
        .astype(low)
        .reshape(seq_count, tokens, kv_heads * HEAD_SIZE)
    )
    keyval_send = jnp.concatenate([keys_mine, value_projected.astype(low)], -1)
    tails = passed_along((stream_pre[:, tokens - rim :], state_pre[:, tokens - rim :]), "ctx", 1)
    keyval_all = lax.all_gather(keyval_send, "ctx", axis=1, tiled=True)
    all_tokens = keyval_all.shape[1]
    key_all = keyval_all[..., : kv_heads * HEAD_SIZE].reshape(
        seq_count, all_tokens, kv_heads, HEAD_SIZE
    )
    value_all = keyval_all[..., kv_heads * HEAD_SIZE :].reshape(
        seq_count, all_tokens, kv_heads, HEAD_SIZE
    )
    stream_act = causal_conv(stream_pre, tails[0], conv_stream, bias_stream)
    state_act = causal_conv(state_pre, tails[1], conv_state, bias_state)
    local_out, local_state, totals = local_part(
        stream_act, state_act, step_raw, step_bias, decay_log
    )
    identity = (jnp.ones_like(totals), jnp.zeros_like(local_state))
    prefix = prefix_2((totals, local_state), "ctx", chain, identity, False)
    carried = prefix[1]
    gated = finish(
        gate_z,
        stream_act,
        state_act,
        step_raw,
        step_bias,
        decay_log,
        skip_scale,
        local_out,
        carried,
    )
    gated_low = gated.astype(low)
    scale = HEAD_SIZE ** (-0.5)
    query_index = ctx_index * tokens + jnp.arange(tokens, dtype=jnp.int32)
    allowed = jnp.arange(all_tokens, dtype=jnp.int32)[None, :] <= query_index[:, None]
    query_groups = queries.reshape(seq_count, tokens, kv_heads, group, HEAD_SIZE)

    def seq_scores(query_seq, key_seq):
        scores = (
            jnp.einsum("qkgd,jkd->kgqj", query_seq, key_seq, preferred_element_type=jnp.float32)
            * scale
        )
        return jnp.where(allowed, scores, -1e30)

    def attend(pieces):
        query_seq, key_seq, value_seq = pieces
        scores = seq_scores(query_seq, key_seq)
        top_score = jnp.max(scores, -1, keepdims=True)
        expo = jnp.exp(scores - top_score)
        denom = jnp.sum(expo, -1, keepdims=True)
        probs = (expo / denom).astype(jnp.bfloat16)
        outputs = jnp.einsum("kgqj,jkd->qkgd", probs, value_seq, preferred_element_type=jnp.float32)
        return (outputs, top_score + jnp.log(denom))

    attended, log_total = lax.map(attend, (query_groups, key_all, value_all))
    attended_low = attended.reshape(seq_count, tokens, q_cols).astype(low)
    mixers = jnp.concatenate([attended_low, gated_low], -1)

    mask_float = valid_mask.astype(f32)[..., None]
    loss_scale = 1.0 / (valid_total * width)
    squares_local = jnp.zeros((), f32)
    seqs = range(seq_count)
    resid, normed_two, gateup, inner, out_full = [], [], [], [], []
    mixed = [
        pair_sum(jnp.einsum("ti,di->td", mixers[s], out_full_w, preferred_element_type=f32))
        for s in seqs
    ]
    for s in seqs:
        resid.append(hidden[s] + mixed[s])
        normed_two.append(rms_norm(resid[s], ffn_gain).astype(low))
        gateup.append(jnp.dot(normed_two[s], gateup_full, preferred_element_type=f32))
        inner.append(
            (jax.nn.silu(gateup[s][:, :hidden_units]) * gateup[s][:, hidden_units:]).astype(low)
        )
    down = [
        pair_sum(jnp.einsum("tf,df->td", inner[s], down_full, preferred_element_type=f32))
        for s in seqs
    ]
    out_grad, down_in, gateup_low = [], [], []

    def swiglu_flat(both):
        return jax.nn.silu(both[:, :hidden_units]) * both[:, hidden_units:]

    for s in seqs:
        out_full.append(resid[s] + down[s])
        diff = out_full[s] - teacher[s].astype(f32)
        squares_local = squares_local + jnp.sum(mask_float[s] * diff * diff)
        out_grad.append(cotangent[s].astype(f32) + mask_float[s] * 2.0 * diff * loss_scale)
        down_in.append(out_grad[s].astype(low))
        inner_grad = jnp.einsum("td,df->tf", down_in[s], down_full, preferred_element_type=f32)
        gateup_low.append(jax.vjp(swiglu_flat, gateup[s])[1](inner_grad)[0].astype(low))
    normed_two_part = [
        jnp.einsum("tc,dc->td", gateup_low[s], gateup_full, preferred_element_type=f32)
        for s in seqs
    ]
    normed_two_grad = [pair_sum(normed_two_part[s]) for s in seqs]
    block_out = jnp.stack(out_full).astype(low)

    def wgrad(left, right):
        return jnp.einsum("td,tc->dc", left, right, preferred_element_type=f32).astype(low)

    join = lambda parts: jnp.concatenate(parts, 0)
    ffn_terms = jnp.concatenate(
        [
            wgrad(join(normed_two), join(gateup_low)),
            wgrad(join(down_in), join(inner)),
        ],
        1,
    )
    ffn_reduced = lax.psum_scatter(ffn_terms, owners, scatter_dimension=0, tiled=True)

    resid_grad, ffn_gain_grad = [], 0.0
    for s in seqs:
        back = jax.vjp(rms_norm, resid[s], ffn_gain)[1](normed_two_grad[s])
        resid_grad.append(out_grad[s] + back[0])
        ffn_gain_grad = ffn_gain_grad + back[1]
    resid_grad = jnp.stack(resid_grad)
    mixed_low = resid_grad.astype(low)
    out_wgrad = wgrad(
        mixed_low.reshape(-1, width), mixers.reshape(-1, q_cols + channels)
    )
    mixers_grad = jnp.einsum("std,di->sti", mixed_low, out_full_w, preferred_element_type=f32)
    attended_grad = (
        mixers_grad[..., :q_cols]
        .astype(low)
        .reshape(seq_count, tokens, kv_heads, group, HEAD_SIZE)
    )
    gated_grad = mixers_grad[..., q_cols:]

    def attend_back(pieces):
        query_seq, key_seq, value_seq, out_grad_seq, log_seq = pieces
        probs_full = jnp.exp(seq_scores(query_seq, key_seq) - log_seq)
        prob_grad = jnp.einsum(
            "qkgd,jkd->kgqj", out_grad_seq, value_seq, preferred_element_type=jnp.float32
        )
        centre = jnp.sum(probs_full * prob_grad, -1, keepdims=True)
        score_grad = (probs_full * (prob_grad - centre)).astype(jnp.bfloat16)
        query_part = (
            jnp.einsum("kgqj,jkd->qkgd", score_grad, key_seq, preferred_element_type=jnp.float32)
            * scale
        )
        key_part = (
            jnp.einsum("kgqj,qkgd->jkd", score_grad, query_seq, preferred_element_type=jnp.float32)
            * scale
        )
        value_part = jnp.einsum(
            "kgqj,qkgd->jkd",
            probs_full.astype(jnp.bfloat16),
            out_grad_seq,
            preferred_element_type=jnp.float32,
        )
        joined = jnp.concatenate(
            [
                key_part.reshape(all_tokens, kv_heads * HEAD_SIZE),
                value_part.reshape(all_tokens, kv_heads * HEAD_SIZE),
            ],
            -1,
        )
        return (query_part, joined)

    query_grad_rot, keyval_grad_all = lax.map(
        attend_back, (query_groups, key_all, value_all, attended_grad, log_total)
    )
    keyval_grad_mine = lax.psum_scatter(
        keyval_grad_all.astype(low), "ctx", scatter_dimension=1, tiled=True
    ).astype(f32)
    _, query_rope_back = jax.vjp(lambda values: rotary(values, positions), query_pre)
    query_in_grad = query_rope_back(
        query_grad_rot.reshape(seq_count, tokens, query_heads, HEAD_SIZE)
    )[0].reshape(seq_count, tokens, q_cols)
    _, key_rope_back = jax.vjp(lambda values: rotary(values, positions), key_before_rotation)
    key_in_grad = key_rope_back(
        keyval_grad_mine[..., :kv_cols].reshape(seq_count, tokens, kv_heads, HEAD_SIZE)
    )[0].reshape(seq_count, tokens, kv_cols)
    value_in_grad = keyval_grad_mine[..., kv_cols:]
    _, finish_back = jax.vjp(
        finish,
        gate_z,
        stream_act,
        state_act,
        step_raw,
        step_bias,
        decay_log,
        skip_scale,
        local_out,
        carried,
    )
    (
        gate_grad,
        stream_grad_one,
        state_grad_one,
        step_grad_one,
        stepbias_one,
        decay_one,
        skip_grad_all,
        local_out_grad,
        carried_grad,
    ) = finish_back(gated_grad)
    after_prefix = prefix_2((totals, carried_grad), "ctx", chain, identity, True)
    later_grad = after_prefix[1]
    totals_grad = jnp.sum(later_grad * carried, (-2, -1))
    _, local_back = jax.vjp(local_part, stream_act, state_act, step_raw, step_bias, decay_log)
    stream_grad_two, state_grad_two, step_grad_two, stepbias_two, decay_two = local_back(
        (local_out_grad, later_grad, totals_grad)
    )
    _, stream_conv_back = jax.vjp(causal_conv, stream_pre, tails[0], conv_stream, bias_stream)
    stream_pre_grad, stream_tail_grad, conv_stream_grad, bias_stream_grad = stream_conv_back(
        stream_grad_one + stream_grad_two
    )
    _, state_conv_back = jax.vjp(causal_conv, state_pre, tails[1], conv_state, bias_state)
    state_pre_grad, state_tail_grad, conv_state_grad, bias_state_grad = state_conv_back(
        state_grad_one + state_grad_two
    )
    back_tails = passed_along((stream_tail_grad, state_tail_grad), "ctx", -1)
    stream_pre_grad = jnp.concatenate(
        [stream_pre_grad[:, : tokens - rim], stream_pre_grad[:, tokens - rim :] + back_tails[0]], 1
    )
    state_pre_grad = jnp.concatenate(
        [state_pre_grad[:, : tokens - rim], state_pre_grad[:, tokens - rim :] + back_tails[1]], 1
    )
    step_grad = step_grad_one + step_grad_two
    pre_grad = jnp.concatenate(
        [
            part.astype(low)
            for part in (
                gate_grad,
                stream_pre_grad,
                state_pre_grad,
                query_in_grad,
                key_in_grad,
                value_in_grad,
                step_grad,
                jnp.zeros((seq_count, tokens, step_cols - heads), f32),
            )
        ],
        -1,
    )
    mixer_terms = jnp.concatenate(
        [
            wgrad(normed.reshape(-1, width), pre_grad.reshape(-1, all_cols)),
            out_wgrad,
        ],
        1,
    )
    mixer_reduced = lax.psum_scatter(mixer_terms, owners, scatter_dimension=0, tiled=True)
    normed_part = jnp.einsum("stc,dc->std", pre_grad, mixer_full, preferred_element_type=f32)
    _, norm_one_back = jax.vjp(rms_norm, hidden, mixer_gain)
    mixer_gain_grad = norm_one_back(normed_part)[1]
    hidden_norm_grad = norm_one_back(
        jnp.stack([pair_sum(normed_part[s]) for s in seqs])
    )[0]
    input_grad = (resid_grad + hidden_norm_grad).astype(low)

    tp_index = lax.axis_index("tp")
    tp_count = lax.axis_size("tp")

    def widen(piece, axis_dim):
        shape_full = list(piece.shape)
        shape_full[axis_dim] = piece.shape[axis_dim] * tp_count
        blank = jnp.zeros(tuple(shape_full), f32)
        return lax.dynamic_update_slice_in_dim(
            blank, piece, tp_index * piece.shape[axis_dim], axis_dim
        )

    def narrow(whole, axis_dim, piece_size):
        return lax.dynamic_slice_in_dim(whole, tp_index * piece_size, piece_size, axis_dim)

    summed = lax.psum(
        (
            mixer_gain_grad,
            ffn_gain_grad / tp_count,
            widen(conv_stream_grad, 1),
            widen(bias_stream_grad, 0),
            conv_state_grad,
            bias_state_grad,
            widen(stepbias_one + stepbias_two, 0),
            widen(decay_one + decay_two, 0),
            widen(skip_grad_all, 0),
            squares_local / tp_count,
        ),
        ("dp", "ctx", "tp"),
    )
    loss = summed[9] * loss_scale
    reduced = mixer_reduced.astype(f32)
    ffn_reduced = ffn_reduced.astype(f32)
    piece = [reduced[:, edges[i] : edges[i + 1]] for i in range(7)]
    state_reduced = pair_sum(piece[2])
    out_reduced = reduced[:, all_cols:]
    return (
        block_out,
        loss,
        input_grad,
        summed[0],
        piece[3],
        jnp.stack([piece[4], piece[5]], 1),
        out_reduced[:, :q_cols].T,
        reduced[:, : 2 * channels].reshape(rows, 2, channels),
        state_reduced,
        piece[6],
        narrow(summed[2], 1, channels),
        narrow(summed[3], 0, channels),
        summed[4],
        summed[5],
        narrow(summed[6], 0, heads),
        narrow(summed[7], 0, heads),
        narrow(summed[8], 0, heads),
        out_reduced[:, q_cols:].T,
        summed[1],
        ffn_reduced[:, : 2 * hidden_units].reshape(rows, 2, hidden_units),
        ffn_reduced[:, 2 * hidden_units :].T,
    )


def solution(mesh):
    return jax.shard_map(
        per_device,
        mesh=mesh,
        in_specs=(
            P("dp", "ctx", None),
            P("dp", "ctx"),
            P("dp", "ctx"),
            P("dp", "ctx", None),
            P("dp", "ctx", None),
            P(),
            P(("dp", "ctx"), "tp"),
            P(("dp", "ctx"), None, "tp"),
            P("tp", ("dp", "ctx")),
            P(("dp", "ctx"), None, "tp"),
            P(("dp", "ctx"), None),
            P(("dp", "ctx"), "tp"),
            P(None, "tp"),
            P("tp"),
            P(),
            P(),
            P("tp"),
            P("tp"),
            P("tp"),
            P("tp", ("dp", "ctx")),
            P(),
            P(("dp", "ctx"), None, "tp"),
            P("tp", ("dp", "ctx")),
        ),
        out_specs=(
            P("dp", "ctx", None),
            P(),
            P("dp", "ctx", None),
            P(),
            P(("dp", "ctx"), "tp"),
            P(("dp", "ctx"), None, "tp"),
            P("tp", ("dp", "ctx")),
            P(("dp", "ctx"), None, "tp"),
            P(("dp", "ctx"), None),
            P(("dp", "ctx"), "tp"),
            P(None, "tp"),
            P("tp"),
            P(),
            P(),
            P("tp"),
            P("tp"),
            P("tp"),
            P("tp", ("dp", "ctx")),
            P(),
            P(("dp", "ctx"), None, "tp"),
            P("tp", ("dp", "ctx")),
        ),
        check_vma=False,
    )
```

```python
import functools

import jax
import jax.numpy as jnp
from jax import lax
from jax.experimental import pallas as pl
from jax.experimental.pallas import tpu as pltpu
from jax.sharding import PartitionSpec as P

HEAD_SIZE = 64
MP = 64
NS = 128
KC = 4
CBLK = 128
VMEM_BYTES = 56 * 1024 * 1024

low = jnp.bfloat16
f32 = jnp.float32
highest = lax.Precision.HIGHEST
NEG = -1e30
eps_norm = 1e-05
rope_base = 100000000000.0


def vmem_params():
    return pltpu.CompilerParams(
        dimension_semantics=("arbitrary",), vmem_limit_bytes=VMEM_BYTES
    )


def mm(left, right):
    return jnp.dot(left, right, preferred_element_type=f32)


def mm_nt(left, right):
    return lax.dot_general(left, right, (((1,), (1,)), ((), ())), preferred_element_type=f32)


def mm_tn(left, right):
    return lax.dot_general(left, right, (((0,), (0,)), ((), ())), preferred_element_type=f32)


def iota(shape, axis):
    return lax.broadcasted_iota(jnp.int32, shape, axis)


def sigmoid(v):
    return 1.0 / (1.0 + jnp.exp(-v))


def softplus(v):
    return jnp.maximum(v, 0.0) + jnp.log1p(jnp.exp(-jnp.abs(v)))


def silu_grad(v, sig):
    return sig * (1.0 + v * (1.0 - sig))


def halves(v):
    high = v.astype(low)
    return high, (v - high.astype(f32)).astype(low)


def head_map(channels):
    shape = (128, channels)
    return jnp.where(iota(shape, 1) // MP == iota(shape, 0), 1.0, 0.0).astype(low)


def expand(per_head, spread):
    high, rest = halves(per_head)
    return mm(high, spread) + mm(rest, spread)


def collect(per_channel, spread):
    high, rest = halves(per_channel)
    return mm_nt(high, spread) + mm_nt(rest, spread)


def rotate(u, cosine, sine):
    first = (iota(u.shape, 1) // 32) % 2 == 0
    return u * cosine + jnp.where(first, pltpu.roll(u, 96, 1), pltpu.roll(u, 32, 1)) * sine


def prep_body(q_ref, kv_ref, cos_ref, sin_ref, q_out, kv_out):
    cosine, sine = cos_ref[...], sin_ref[...]
    scale = HEAD_SIZE ** (-0.5)
    for j in range(q_ref.shape[1] // 128):
        cols = slice(128 * j, 128 * j + 128)
        q_out[:, cols] = rotate(q_ref[:, cols], cosine, sine).astype(low) * jnp.asarray(scale, low)
    kv = kv_ref[...]
    keep = iota(kv.shape, 1) < HEAD_SIZE
    kv_out[...] = jnp.where(keep, rotate(kv, cosine, sine), kv).astype(low)


def attend_body(at_ref, q_ref, *refs, hops):
    kv_refs, (o_ref, lse_ref) = refs[:hops], refs[hops:]
    at = at_ref[0]
    tokens = q_ref.shape[0]
    lane = iota((tokens, 128), 1)
    lo = lane < HEAD_SIZE
    causal = iota((tokens, tokens), 0) >= iota((tokens, tokens), 1)
    lse_all = jnp.zeros((tokens, 128), f32)
    for j in range(q_ref.shape[1] // 128):
        pair = q_ref[:, 128 * j : 128 * j + 128].astype(f32)
        sides = []
        for side in range(2):
            query = pair if side == 0 else pltpu.roll(pair, HEAD_SIZE, 1)
            query = jnp.where(lo, query, 0.0).astype(low)
            scores = []
            for d in range(hops):
                score = mm_nt(query, kv_refs[d][...])
                scores.append(
                    jnp.where(causal if d == 0 else at >= d, score, NEG)
                )
            top = functools.reduce(
                jnp.maximum, [jnp.max(s, -1, keepdims=True) for s in scores]
            )
            total, mixed = 0.0, 0.0
            for d in range(hops):
                expo = jnp.exp(scores[d] - top)
                total = total + jnp.sum(expo, -1, keepdims=True)
                mixed = mixed + mm(expo.astype(low), kv_refs[d][...])
            sides.append(mixed * (1.0 / total))
            lse_all = jnp.where(lane == 2 * j + side, top + jnp.log(total), lse_all)
        o_ref[:, 128 * j : 128 * j + 128] = jnp.where(
            lo, pltpu.roll(sides[0], HEAD_SIZE, 1), sides[1]
        ).astype(low)
    lse_ref[...] = lse_all


def attend_back_body(at_ref, q_ref, go_ref, o_ref, lse_ref, cos_ref, sin_ref, *refs, hops):
    kv_refs, (gq_ref,), gkv_refs = refs[:hops], refs[hops : hops + 1], refs[hops + 1 :]
    at = at_ref[0]
    tokens = q_ref.shape[0]
    lane = iota((tokens, 128), 1)
    lo = lane < HEAD_SIZE
    causal = iota((tokens, tokens), 0) >= iota((tokens, tokens), 1)
    cosine, sine = cos_ref[...], sin_ref[...]
    lse_all = lse_ref[...]
    scale = HEAD_SIZE ** (-0.5)
    gkv = [jnp.zeros((tokens, 128), f32) for _ in range(hops)]
    for j in range(q_ref.shape[1] // 128):
        cols = slice(128 * j, 128 * j + 128)
        pair = q_ref[:, cols].astype(f32)
        go_pair = go_ref[:, cols].astype(low).astype(f32)
        weighed = go_pair * o_ref[:, cols].astype(f32)
        sides = []
        for side in range(2):
            query = pair if side == 0 else pltpu.roll(pair, HEAD_SIZE, 1)
            query = jnp.where(lo, query, 0.0).astype(low)
            grad = pltpu.roll(go_pair, HEAD_SIZE, 1) if side == 0 else go_pair
            grad = jnp.where(lo, 0.0, grad).astype(low)
            centre = jnp.sum(jnp.where(lo == (side == 0), weighed, 0.0), -1, keepdims=True)
            lse = jnp.sum(jnp.where(lane == 2 * j + side, lse_all, 0.0), -1, keepdims=True)
            gq = 0.0
            for d in range(hops):
                kv = kv_refs[d][...]
                score = mm_nt(query, kv)
                prob = jnp.exp(jnp.where(causal if d == 0 else at >= d, score, NEG) - lse)
                gprob = mm_nt(grad, kv)
                gscore = (prob * (gprob - centre)).astype(low)
                gq = gq + mm(gscore, kv)
                gkv[d] = gkv[d] + mm_tn(gscore, query) + mm_tn(prob.astype(low), grad)
            sides.append(gq * scale)
        joined = jnp.where(lo, sides[0], pltpu.roll(sides[1], HEAD_SIZE, 1))
        gq_ref[:, cols] = rotate(joined, cosine, -sine).astype(low)
    for d in range(hops):
        gkv_refs[d][...] = gkv[d].astype(low)


def keyval_sum_body(cos_ref, sin_ref, *refs):
    parts, (out_ref,) = refs[:-1], refs[-1:]
    total = parts[0][...].astype(f32)
    for part in parts[1:]:
        total = total + part[...].astype(f32)
    keep = iota(total.shape, 1) < HEAD_SIZE
    rotated = rotate(total, cos_ref[...], -sin_ref[...])
    out_ref[...] = jnp.where(keep, rotated, total).astype(low)


def decay_pair(logs, logs_t, first, keep):
    both = []
    for head in (first, first + 1):
        gap = logs[:, head : head + 1] - logs_t[head : head + 1, :]
        both.append(jnp.exp(jnp.where(keep, gap, NEG)))
    return both


def step_terms(step_ref, rows, heads_ref, heads):
    raw = step_ref[rows, :] + heads_ref[0:1, :]
    live = iota(raw.shape, 1) < heads
    steps = jnp.where(live, softplus(raw), 0.0)
    return jnp.where(live, raw, 0.0), steps


def lower_triangle(size):
    return iota((size, size), 0) >= iota((size, size), 1)


def scan_body(
    x_ref, bc_ref, step_ref, xt_ref, bct_ref, taps_ref, taps_bc_ref, heads_ref,
    v_ref, vbc_ref, y_ref, logs_ref, states_ref, send_ref,
    xe, bce, *, heads,
):
    tokens, channels = x_ref.shape
    xe[0:8, :] = xt_ref[...]
    xe[8:, :] = x_ref[...]
    bce[0:8, :] = bct_ref[...]
    bce[8:, :] = bc_ref[...]
    spread = head_map(channels)
    keep = lower_triangle(CBLK)
    triangle = jnp.where(keep, 1.0, 0.0)
    lo = iota((CBLK, 128), 1) < MP
    rate = heads_ref[1:2, :]
    state = None
    carry = jnp.zeros((1, 128), f32)
    total_decay = None
    for c in range(tokens // CBLK):
        rows = slice(CBLK * c, CBLK * c + CBLK)

        def conv(ext, taps):
            start = CBLK * c + 8 - (KC - 1)
            total = taps[KC : KC + 1, :] + taps[0:1, :] * ext[start : start + CBLK, :]
            for k in range(1, KC):
                total = total + taps[k : k + 1, :] * ext[start + k : start + k + CBLK, :]
            return total

        v = conv(xe, taps_ref)
        v_ref[rows, :] = v
        xs = v * sigmoid(v)
        vbc = conv(bce, taps_bc_ref)
        vbc_ref[rows, :] = vbc
        bc = (vbc * sigmoid(vbc)).astype(low)
        entry, read = bc[:, :NS], bc[:, NS:]
        _, steps = step_terms(step_ref, rows, heads_ref, heads)
        logs = jnp.dot(triangle, -steps * rate, precision=highest, preferred_element_type=f32)
        logs_t = logs.T
        total = logs[CBLK - 1 : CBLK, :]
        logs_ref[rows, :] = logs + carry
        carry = carry + total
        decays = expand(jnp.exp(logs), spread)
        steps_wide = expand(steps, spread)
        tails_wide = expand(jnp.exp(total - logs) * steps, spread)
        weighted = (xs * steps_wide).astype(low)
        inner = mm_nt(read, entry)
        if state is not None:
            incoming = decays * mm(read, state.astype(low))
        for j in range(channels // 128):
            cols = slice(128 * j, 128 * j + 128)
            left, right = decay_pair(logs, logs_t, 2 * j, keep)
            stacked = jnp.concatenate([(inner * left).astype(low), (inner * right).astype(low)], 0)
            result = mm(stacked, weighted[:, cols])
            out = jnp.where(lo, result[:CBLK], result[CBLK:])
            if state is not None:
                out = out + incoming[:, cols]
            y_ref[rows, cols] = out
        added = mm_tn(entry, (xs * tails_wide).astype(low))
        last = decays[CBLK - 1 : CBLK, :]
        state = added if state is None else last * state + added
        total_decay = last if total_decay is None else total_decay * last
        states_ref[NS * c : NS * c + NS, :] = state
    send_ref[0:NS, :] = state.astype(low)
    send_ref[NS:, :] = jnp.broadcast_to(total_decay, (send_ref.shape[0] - NS, channels)).astype(low)


def chained(refs):
    state = None
    for ref in reversed(refs):
        own = ref[0:NS, :].astype(f32)
        if state is None:
            state = own
        else:
            state = own + ref[NS : NS + 1, :].astype(f32) * state
    return state


def gate_body(z_ref, y_ref, v_ref, vbc_ref, logs_ref, heads_ref, *refs):
    earlier, (gated_ref, y_out, carried_ref) = refs[:-3], refs[-3:]
    tokens, channels = y_ref.shape
    spread = head_map(channels)
    skip = expand(heads_ref[...], spread)[2:3, :]
    carried = chained(earlier) if earlier else jnp.zeros((NS, channels), f32)
    carried_ref[...] = carried
    carried_low = carried.astype(low)
    for c in range(tokens // CBLK):
        rows = slice(CBLK * c, CBLK * c + CBLK)
        vc = vbc_ref[rows, NS:]
        read = (vc * sigmoid(vc)).astype(low)
        y = y_ref[rows, :] + expand(jnp.exp(logs_ref[rows, :]), spread) * mm(read, carried_low)
        y_out[rows, :] = y
        v = v_ref[rows, :]
        z = z_ref[rows, :]
        gated_ref[rows, :] = ((y + skip * (v * sigmoid(v))) * (z * sigmoid(z))).astype(low)


def gate_back_body(
    g_ref, z_ref, y_ref, v_ref, vbc_ref, logs_ref, heads_ref, sent_ref,
    dy_ref, dz_ref, send_ref, dskip_ref,
):
    tokens, channels = y_ref.shape
    spread = head_map(channels)
    skip = expand(heads_ref[...], spread)[2:3, :]
    state, dskip = 0.0, 0.0
    for c in range(tokens // CBLK):
        rows = slice(CBLK * c, CBLK * c + CBLK)
        vc = vbc_ref[rows, NS:]
        read = (vc * sigmoid(vc)).astype(low)
        v = v_ref[rows, :]
        xs = v * sigmoid(v)
        z = z_ref[rows, :]
        sig = sigmoid(z)
        grad = g_ref[rows, :].astype(f32)
        dy = grad * (z * sig)
        dz_ref[rows, :] = (grad * (y_ref[rows, :] + skip * xs) * silu_grad(z, sig)).astype(low)
        dy_ref[rows, :] = dy
        dskip = dskip + jnp.sum(dy * xs, 0, keepdims=True)
        faded = (dy * expand(jnp.exp(logs_ref[rows, :]), spread)).astype(low)
        state = state + mm_tn(read, faded)
    send_ref[0:NS, :] = state.astype(low)
    send_ref[NS:, :] = sent_ref[NS:, :]
    dskip_ref[...] = jnp.broadcast_to(dskip, dskip_ref.shape)


def scan_back_body(
    dy_ref, y_ref, v_ref, vbc_ref, x_ref, bc_ref, step_ref, xt_ref, bct_ref,
    taps_ref, taps_bc_ref, heads_ref, logs_ref, states_ref, carried_ref, *refs, heads,
):
    later, refs = refs[:-10], refs[-10:]
    dx_ref, dbc_ref, dstep_ref, edge_ref, head_ref, gx_ref, gbc_ref, gh_ref, dve, dbce = refs
    tokens, channels = y_ref.shape
    chunks = tokens // CBLK
    spread = head_map(channels)
    keep = lower_triangle(CBLK)
    triangle = jnp.where(keep, 1.0, 0.0)
    lo = iota((CBLK, 128), 1) < MP
    rate = heads_ref[1:2, :]
    skip = expand(heads_ref[...], spread)[2:3, :]
    dstate = chained(later) if later else jnp.zeros((NS, channels), f32)
    dve[0:8, :] = jnp.zeros((8, channels), f32)
    dve[8 + tokens :, :] = jnp.zeros((8, channels), f32)
    dbce[0:8, :] = jnp.zeros((8, 2 * NS), f32)
    dbce[8 + tokens :, :] = jnp.zeros((8, 2 * NS), f32)
    dbias, ddecay = 0.0, 0.0
    for c in reversed(range(chunks)):
        rows = slice(CBLK * c, CBLK * c + CBLK)
        v = v_ref[rows, :]
        sig = sigmoid(v)
        xs = v * sig
        vbc = vbc_ref[rows, :]
        sig_bc = sigmoid(vbc)
        bc = (vbc * sig_bc).astype(low)
        entry, read = bc[:, :NS], bc[:, NS:]
        raw, steps = step_terms(step_ref, rows, heads_ref, heads)
        logs = jnp.dot(triangle, -steps * rate, precision=highest, preferred_element_type=f32)
        logs_t = logs.T
        total = logs[CBLK - 1 : CBLK, :]
        decays = expand(jnp.exp(logs), spread)
        steps_wide = expand(steps, spread)
        tails_wide = expand(jnp.exp(total - logs), spread)
        last = decays[CBLK - 1 : CBLK, :]
        if c == 0:
            state = carried_ref[...]
        else:
            before = expand(jnp.exp(logs_ref[CBLK * c - 8 : CBLK * c, :]), spread)[7:8, :]
            state = states_ref[NS * (c - 1) : NS * c, :] + before * carried_ref[...]
        dy = dy_ref[rows, :]
        dy_low = dy.astype(low)
        w = xs * steps_wide
        w_low = w.astype(low)
        inner = mm_nt(read, entry)
        state_low = state.astype(low)
        dstate_low = dstate.astype(low)
        dw_later = tails_wide * mm(entry, dstate_low)
        faded = (dy * decays).astype(low)
        dread = mm_nt(faded, state_low)
        dentry = mm_nt((w * tails_wide).astype(low), dstate_low)
        dinner = 0.0
        pieces = []
        for j in range(channels // 128):
            cols = slice(128 * j, 128 * j + 128)
            left, right = decay_pair(logs, logs_t, 2 * j, keep)
            dy_pair, w_pair = dy_low[:, cols], w_low[:, cols]
            weights = jnp.concatenate([(inner * left).astype(low), (inner * right).astype(low)], 1)
            result = mm_tn(weights, dy_pair)
            pieces.append(jnp.where(lo, result[:CBLK], result[CBLK:]) + dw_later[:, cols])
            zero = jnp.zeros_like(dy_pair)
            parted = jnp.concatenate([jnp.where(lo, dy_pair, zero), jnp.where(lo, zero, dy_pair)], 0)
            dweights = mm_nt(parted, w_pair)
            dinner = dinner + dweights[:CBLK] * left + dweights[CBLK:] * right
        dw = jnp.concatenate(pieces, 1)
        dinner_low = dinner.astype(low)
        dread = dread + mm(dinner_low, entry)
        dentry = dentry + mm_tn(dinner_low, read)
        dlogs = collect(dy * y_ref[rows, :] - w * dw, spread)
        dtotal = jnp.sum(w * dw_later, 0, keepdims=True) + last * jnp.sum(
            dstate * state, 0, keepdims=True
        )
        dtotal = collect(jnp.broadcast_to(dtotal, (8, channels)), spread)[0:1, :]
        dfall = (
            lax.dot_general(
                triangle, dlogs, (((0,), (0,)), ((), ())),
                precision=highest, preferred_element_type=f32,
            )
            + dtotal
        )
        dsteps = collect(xs * dw, spread) - rate * dfall
        ddecay = ddecay - rate * jnp.sum(steps * dfall, 0, keepdims=True)
        live = iota(raw.shape, 1) < heads
        draw = jnp.where(live, dsteps * sigmoid(raw), 0.0)
        dbias = dbias + jnp.sum(draw, 0, keepdims=True)
        dstep_ref[rows, :] = draw.astype(low)
        dve[8 + CBLK * c : 8 + CBLK * c + CBLK, :] = (steps_wide * dw + skip * dy) * silu_grad(v, sig)
        dbce[8 + CBLK * c : 8 + CBLK * c + CBLK, :] = jnp.concatenate(
            [dentry, dread], 1
        ) * silu_grad(vbc, sig_bc)
        dstate = last * dstate + mm_tn(read, faded)
    gh_ref[0:1, :] = dbias
    gh_ref[1:2, :] = ddecay
    gh_ref[2:, :] = jnp.zeros((gh_ref.shape[0] - 2, 128), f32)

    def conv_back(ext, taps, out_ref, cols, grads_ref, pre_ref, tail_ref):
        def spread_rows(start, count):
            total = taps[0:1, :] * ext[start + KC - 1 : start + KC - 1 + count, :]
            for k in range(1, KC):
                at = start + KC - 1 - k
                total = total + taps[k : k + 1, :] * ext[at : at + count, :]
            return total

        head_ref[:, cols] = spread_rows(0, 8)
        grads = [0.0] * (KC + 1)
        for c in range(chunks):
            at = CBLK * c
            dpre = spread_rows(8 + at, CBLK)
            out_ref[at : at + CBLK, :] = dpre.astype(low)
            if c == chunks - 1:
                edge_ref[:, cols] = dpre[CBLK - 8 :, :]
        for k in range(KC):
            shift = KC - 1 - k
            main = jnp.sum(pre_ref[...] * ext[8 + shift : 8 + shift + tokens, :], 0, keepdims=True)
            edge = jnp.sum(tail_ref[...] * ext[shift : shift + 8, :], 0, keepdims=True)
            grads[k] = main + edge
        grads[KC] = jnp.sum(ext[8 : 8 + tokens, :], 0, keepdims=True)
        for k in range(KC + 1):
            grads_ref[k : k + 1, :] = grads[k]
        grads_ref[KC + 1 :, :] = jnp.zeros((grads_ref.shape[0] - KC - 1, ext.shape[1]), f32)

    conv_back(dve, taps_ref, dx_ref, slice(0, channels), gx_ref, x_ref, xt_ref)
    bc_cols = slice(channels, channels + 2 * NS)
    conv_back(dbce, taps_bc_ref, dbc_ref, bc_cols, gbc_ref, bc_ref, bct_ref)


def block(height, width, col=0):
    return pl.BlockSpec((height, width), lambda s: (s, col))


def whole(shape):
    return pl.BlockSpec(shape, lambda s: (0, 0))


def shaped(rows, cols, dtype):
    return jax.ShapeDtypeStruct((rows, cols), dtype)


def run(body, seqs, inputs, outputs, scratch=(), at=None, flops=0):
    arrays = [a for a, _ in inputs]
    specs = [s for _, s in inputs]
    if at is not None:
        arrays = [at] + arrays
        specs = [pl.BlockSpec(memory_space=pltpu.SMEM)] + specs
    moved = sum(a.size * a.dtype.itemsize for a in arrays)
    return pl.pallas_call(
        body,
        grid=(seqs,),
        in_specs=specs,
        out_specs=[block(r, c) for r, c, _ in outputs],
        out_shape=[shaped(seqs * r, c, d) for r, c, d in outputs],
        scratch_shapes=list(scratch),
        compiler_params=vmem_params(),
        cost_estimate=pl.CostEstimate(flops=flops, bytes_accessed=moved, transcendentals=0),
    )(*arrays)


def prep(pre, cosine, sine, seqs, tokens, q_at, q_cols, kv_at):
    return run(
        prep_body,
        seqs,
        [
            (pre, block(tokens, q_cols, q_at // q_cols)),
            (pre, block(tokens, 128, kv_at // 128)),
            (cosine, block(tokens, 128)),
            (sine, block(tokens, 128)),
        ],
        [(tokens, q_cols, low), (tokens, 128, low)],
    )


def attend(queries, keyvals, at, seqs, tokens):
    hops, cols = len(keyvals), queries.shape[1]
    work = 4 * seqs * tokens * tokens * hops * (cols // HEAD_SIZE) * 256
    return run(
        functools.partial(attend_body, hops=hops),
        seqs,
        [(queries, block(tokens, cols))] + [(kv, block(tokens, 128)) for kv in keyvals],
        [(tokens, cols, low), (tokens, 128, f32)],
        at=at,
        flops=work,
    )


def attend_back(queries, keyvals, grads, grad_at, outs, lse, cosine, sine, at, seqs, tokens):
    hops, cols = len(keyvals), queries.shape[1]
    work = 10 * seqs * tokens * tokens * hops * (cols // HEAD_SIZE) * 256
    return run(
        functools.partial(attend_back_body, hops=hops),
        seqs,
        [
            (queries, block(tokens, cols)),
            (grads, block(tokens, cols, grad_at // cols)),
            (outs, block(tokens, cols)),
            (lse, block(tokens, 128)),
            (cosine, block(tokens, 128)),
            (sine, block(tokens, 128)),
        ]
        + [(kv, block(tokens, 128)) for kv in keyvals],
        [(tokens, cols, low)] + [(tokens, 128, low)] * hops,
        at=at,
        flops=work,
    )


def keyval_sum(parts, cosine, sine, seqs, tokens):
    return run(
        keyval_sum_body,
        seqs,
        [(a, block(tokens, 128)) for a in (cosine, sine, *parts)],
        [(tokens, 128, low)],
    )[0]


SENT = NS + 16


def scan(pre, tails, taps, taps_bc, per_head, seqs, tokens, channels, heads):
    step_at = pre.shape[1] // 128 - 1
    return run(
        functools.partial(scan_body, heads=heads),
        seqs,
        [
            (pre, block(tokens, channels, 1)),
            (pre, block(tokens, 2 * NS, 2 * channels // (2 * NS))),
            (pre, block(tokens, 128, step_at)),
            (tails, block(8, channels)),
            (tails, block(8, 2 * NS, channels // (2 * NS))),
            (taps, whole(taps.shape)),
            (taps_bc, whole(taps_bc.shape)),
            (per_head, whole(per_head.shape)),
        ],
        [
            (tokens, channels, f32),
            (tokens, 2 * NS, f32),
            (tokens, channels, f32),
            (tokens, 128, f32),
            (tokens // CBLK * NS, channels, f32),
            (SENT, channels, low),
        ],
        scratch=[pltpu.VMEM((tokens + 8, channels), f32), pltpu.VMEM((tokens + 8, 2 * NS), f32)],
        flops=8 * seqs * tokens * CBLK * channels,
    )


def gate(pre, y, v, vbc, logs, per_head, earlier, seqs, tokens, channels):
    return run(
        gate_body,
        seqs,
        [
            (pre, block(tokens, channels, 0)),
            (y, block(tokens, channels)),
            (v, block(tokens, channels)),
            (vbc, block(tokens, 2 * NS)),
            (logs, block(tokens, 128)),
            (per_head, whole(per_head.shape)),
        ]
        + [(a, block(SENT, channels)) for a in earlier],
        [(tokens, channels, low), (tokens, channels, f32), (NS, channels, f32)],
        flops=4 * seqs * tokens * CBLK * channels,
    )


def gate_back(grads, pre, y, v, vbc, logs, per_head, sent, seqs, tokens, channels):
    return run(
        gate_back_body,
        seqs,
        [
            (grads, block(tokens, channels, 0)),
            (pre, block(tokens, channels, 0)),
            (y, block(tokens, channels)),
            (v, block(tokens, channels)),
            (vbc, block(tokens, 2 * NS)),
            (logs, block(tokens, 128)),
            (per_head, whole(per_head.shape)),
            (sent, block(SENT, channels)),
        ],
        [
            (tokens, channels, f32),
            (tokens, channels, low),
            (SENT, channels, low),
            (8, channels, f32),
        ],
        flops=4 * seqs * tokens * CBLK * channels,
    )


def scan_back(
    dy, y, v, vbc, pre, tails, taps, taps_bc, per_head, logs, states, carried, later,
    seqs, tokens, channels, heads,
):
    step_at = pre.shape[1] // 128 - 1
    return run(
        functools.partial(scan_back_body, heads=heads),
        seqs,
        [
            (dy, block(tokens, channels)),
            (y, block(tokens, channels)),
            (v, block(tokens, channels)),
            (vbc, block(tokens, 2 * NS)),
            (pre, block(tokens, channels, 1)),
            (pre, block(tokens, 2 * NS, 2 * channels // (2 * NS))),
            (pre, block(tokens, 128, step_at)),
            (tails, block(8, channels)),
            (tails, block(8, 2 * NS, channels // (2 * NS))),
            (taps, whole(taps.shape)),
            (taps_bc, whole(taps_bc.shape)),
            (per_head, whole(per_head.shape)),
            (logs, block(tokens, 128)),
            (states, block(tokens // CBLK * NS, channels)),
            (carried, block(NS, channels)),
        ]
        + [(a, block(SENT, channels)) for a in later],
        [
            (tokens, channels, low),
            (tokens, 2 * NS, low),
            (tokens, 128, low),
            (8, channels + 2 * NS, f32),
            (8, channels + 2 * NS, f32),
            (8, channels, f32),
            (8, 2 * NS, f32),
            (8, 128, f32),
        ],
        scratch=[
            pltpu.VMEM((tokens + 16, channels), f32),
            pltpu.VMEM((tokens + 16, 2 * NS), f32),
        ],
        flops=30 * seqs * tokens * CBLK * channels,
    )


def passed_along(block, axis, distance):
    devices = range(lax.axis_size(axis))
    route = [(i - distance, i) for i in devices if i - distance in devices]
    return lax.ppermute(block, axis, route)


def pair_sum(part):
    if lax.axis_size("tp") != 2:
        return lax.psum(part, "tp")
    mine = part.astype(low)
    other = lax.ppermute(mine, "tp", [(0, 1), (1, 0)])
    return mine.astype(f32) + other.astype(f32)


def rms_norm(values, gain):
    return values * lax.rsqrt(jnp.mean(values * values, -1, keepdims=True) + eps_norm) * gain


def angle_tables(positions):
    half = HEAD_SIZE // 2
    freqs = rope_base ** (-2.0 * jnp.arange(half, dtype=f32) / HEAD_SIZE)
    angles = positions.reshape(-1, 1).astype(f32) * freqs
    cosine, sine = jnp.cos(angles), jnp.sin(angles)
    return jnp.tile(cosine, (1, 4)), jnp.concatenate([-sine, sine, -sine, sine], 1)


def per_device(
    hidden_in,
    positions,
    valid_mask,
    teacher,
    cotangent,
    mixer_gain,
    query_weight,
    keyvalue_projection_weight,
    attnout_weight,
    stream_weight,
    state_weight,
    step_weight,
    conv_stream,
    bias_stream,
    conv_state,
    bias_state,
    step_bias,
    decay_log,
    skip_scale,
    mambaout_weight,
    ffn_gain,
    gateup_weight,
    down_weight,
):
    seqs, tokens, width = hidden_in.shape
    owners = ("dp", "ctx")
    rows = query_weight.shape[0]
    q_cols = query_weight.shape[1]
    kv_cols = keyvalue_projection_weight.shape[2]
    channels = stream_weight.shape[2]
    bc_cols = state_weight.shape[1]
    heads = step_weight.shape[1]
    hidden_units = gateup_weight.shape[2]
    step_cols = 128
    hops = lax.axis_size("ctx")

    tallies = jnp.sum(valid_mask.reshape(seqs * tokens // CBLK, CBLK), -1).astype(low)
    spare = jnp.zeros((rows, step_cols - heads), low)
    spare = spare.at[0, : tallies.shape[0]].set(tallies)
    mixer_shard = jnp.concatenate(
        [
            stream_weight.reshape(rows, 2 * channels),
            state_weight,
            query_weight,
            keyvalue_projection_weight.reshape(rows, 2 * kv_cols),
            step_weight,
            spare,
        ],
        1,
    )
    mixer_full = lax.all_gather(mixer_shard, owners, axis=0, tiled=True)
    ffn_shard = jnp.concatenate(
        [
            gateup_weight.reshape(rows, 2 * hidden_units),
            down_weight.T,
            mambaout_weight.T,
            attnout_weight.T,
        ],
        1,
    )
    ffn_full = lax.all_gather(ffn_shard, owners, axis=0, tiled=True)
    gateup_full = ffn_full[:, : 2 * hidden_units]
    down_full = ffn_full[:, 2 * hidden_units : 3 * hidden_units]
    out_full_w = ffn_full[:, 3 * hidden_units :]

    edges = [0]
    for size in (channels, channels, bc_cols, q_cols, kv_cols, kv_cols, heads):
        edges.append(edges[-1] + size)
    all_cols = mixer_full.shape[1]
    counts = mixer_full.reshape(-1, rows, all_cols)[:, 0, edges[7] : edges[7] + tallies.shape[0]]
    valid_total = jnp.sum(counts.astype(f32))

    at = lax.axis_index("ctx").astype(jnp.int32).reshape(1)
    cosine, sine = angle_tables(positions)

    def taps_of(taps, bias):
        spare_rows = jnp.zeros((8 - KC - 1, taps.shape[1]), f32)
        return jnp.concatenate([taps, bias[None], spare_rows], 0)

    taps, taps_bc = taps_of(conv_stream, bias_stream), taps_of(conv_state, bias_state)
    per_head = jnp.pad(
        jnp.stack([step_bias, jnp.exp(decay_log), skip_scale]), ((0, 5), (0, 128 - heads))
    )

    hidden = hidden_in.astype(f32)
    normed = rms_norm(hidden, mixer_gain).astype(low).reshape(seqs * tokens, width)
    pre = jnp.dot(normed, mixer_full, preferred_element_type=f32)

    def last_rows(array):
        return array.reshape(seqs, tokens, -1)[:, tokens - 8 :].reshape(seqs * 8, -1)

    tails = passed_along(last_rows(pre[:, channels : edges[3]]), "ctx", 1)
    queries, keyval = prep(pre, cosine, sine, seqs, tokens, edges[3], q_cols, edges[4])
    keyvals = [keyval] + [passed_along(keyval, "ctx", d) for d in range(1, hops)]
    v, vbc, y_own, logs, states, sent = scan(
        pre, tails, taps, taps_bc, per_head, seqs, tokens, channels, heads
    )
    earlier = [passed_along(sent, "ctx", d) for d in range(1, hops)]
    attended, lse = attend(queries, keyvals, at, seqs, tokens)
    gated, y, carried = gate(
        pre, y_own, v, vbc, logs, per_head, earlier, seqs, tokens, channels
    )
    mixers = jnp.concatenate([gated, attended], -1)
    by_seq = lambda array: array.reshape(seqs, tokens, -1)

    mask_float = valid_mask.astype(f32)[..., None]
    loss_scale = 1.0 / (valid_total * width)
    squares_local = jnp.zeros((), f32)
    each = range(seqs)
    resid, normed_two, gateup, inner, out_full = [], [], [], [], []
    mixed = [
        pair_sum(
            jnp.einsum("ti,di->td", by_seq(mixers)[s], out_full_w, preferred_element_type=f32)
        )
        for s in each
    ]
    for s in each:
        resid.append(hidden[s] + mixed[s])
        normed_two.append(rms_norm(resid[s], ffn_gain).astype(low))
        gateup.append(jnp.dot(normed_two[s], gateup_full, preferred_element_type=f32))
        inner.append(
            (jax.nn.silu(gateup[s][:, :hidden_units]) * gateup[s][:, hidden_units:]).astype(low)
        )
    down = [
        pair_sum(jnp.einsum("tf,df->td", inner[s], down_full, preferred_element_type=f32))
        for s in each
    ]
    out_grad, down_in, gateup_low = [], [], []

    def swiglu_flat(both):
        return jax.nn.silu(both[:, :hidden_units]) * both[:, hidden_units:]

    for s in each:
        out_full.append(resid[s] + down[s])
        diff = out_full[s] - teacher[s].astype(f32)
        squares_local = squares_local + jnp.sum(mask_float[s] * diff * diff)
        out_grad.append(cotangent[s].astype(f32) + mask_float[s] * 2.0 * diff * loss_scale)
        down_in.append(out_grad[s].astype(low))
        inner_grad = jnp.einsum("td,df->tf", down_in[s], down_full, preferred_element_type=f32)
        gateup_low.append(jax.vjp(swiglu_flat, gateup[s])[1](inner_grad)[0].astype(low))
    normed_two_part = [
        jnp.einsum("tc,dc->td", gateup_low[s], gateup_full, preferred_element_type=f32)
        for s in each
    ]
    normed_two_grad = [pair_sum(normed_two_part[s]) for s in each]
    block_out = jnp.stack(out_full).astype(low)

    def wgrad(left, right):
        return jnp.einsum("td,tc->dc", left, right, preferred_element_type=f32).astype(low)

    join = lambda parts: jnp.concatenate(parts, 0)
    ffn_terms = jnp.concatenate(
        [
            wgrad(join(normed_two), join(gateup_low)),
            wgrad(join(down_in), join(inner)),
        ],
        1,
    )
    ffn_reduced = lax.psum_scatter(ffn_terms, owners, scatter_dimension=0, tiled=True)

    resid_grad, ffn_gain_grad = [], 0.0
    for s in each:
        back = jax.vjp(rms_norm, resid[s], ffn_gain)[1](normed_two_grad[s])
        resid_grad.append(out_grad[s] + back[0])
        ffn_gain_grad = ffn_gain_grad + back[1]
    resid_grad = jnp.concatenate(resid_grad, 0)
    mixed_low = resid_grad.astype(low)
    out_wgrad = wgrad(mixed_low, mixers)
    mixers_grad = jnp.dot(mixed_low, out_full_w, preferred_element_type=f32)

    dy, dz, sent_back, skip_rows = gate_back(
        mixers_grad, pre, y, v, vbc, logs, per_head, sent, seqs, tokens, channels
    )
    later = [passed_along(sent_back, "ctx", -d) for d in range(1, hops)]
    query_back, *keyval_parts = attend_back(
        queries, keyvals, mixers_grad, channels, attended, lse, cosine, sine, at, seqs, tokens
    )
    keyval_parts = [keyval_parts[0]] + [
        passed_along(keyval_parts[d], "ctx", -d) for d in range(1, hops)
    ]
    dx, dbc, dstep, edge, head, conv_rows, conv_bc_rows, head_rows = scan_back(
        dy, y, v, vbc, pre, tails, taps, taps_bc, per_head, logs, states, carried, later,
        seqs, tokens, channels, heads,
    )
    keyval_back = keyval_sum(keyval_parts, cosine, sine, seqs, tokens)
    mended = (edge + passed_along(head, "ctx", -1)).astype(low)
    pre_grad = jnp.concatenate([dz, dx, dbc, query_back, keyval_back, dstep], -1)
    for s in each:
        pre_grad = lax.dynamic_update_slice(
            pre_grad, mended[8 * s : 8 * s + 8], (tokens * (s + 1) - 8, channels)
        )
    mixer_terms = jnp.concatenate([wgrad(normed, pre_grad), out_wgrad], 1)
    mixer_reduced = lax.psum_scatter(mixer_terms, owners, scatter_dimension=0, tiled=True)
    normed_part = jnp.einsum("tc,dc->td", pre_grad, mixer_full, preferred_element_type=f32)
    hidden_rows = hidden.reshape(seqs * tokens, width)
    _, norm_one_back = jax.vjp(rms_norm, hidden_rows, mixer_gain)
    mixer_gain_grad = norm_one_back(normed_part)[1]
    normed_grad = join([pair_sum(by_seq(normed_part)[s]) for s in each])
    input_grad = (resid_grad + norm_one_back(normed_grad)[0]).astype(low)

    tp_index = lax.axis_index("tp")
    tp_count = lax.axis_size("tp")

    def widen(piece, axis_dim):
        shape_full = list(piece.shape)
        shape_full[axis_dim] = piece.shape[axis_dim] * tp_count
        blank = jnp.zeros(tuple(shape_full), f32)
        return lax.dynamic_update_slice_in_dim(
            blank, piece, tp_index * piece.shape[axis_dim], axis_dim
        )

    def narrow(wide, axis_dim, piece_size):
        return lax.dynamic_slice_in_dim(wide, tp_index * piece_size, piece_size, axis_dim)

    over_seqs = lambda array: jnp.sum(array.reshape(seqs, 8, -1), 0)
    conv_sum, conv_bc_sum, head_sum = map(over_seqs, (conv_rows, conv_bc_rows, head_rows))
    skip_grad = jnp.sum(over_seqs(skip_rows)[0].reshape(heads, MP), -1)
    summed = lax.psum(
        (
            mixer_gain_grad,
            ffn_gain_grad / tp_count,
            widen(conv_sum[: KC + 1], 1),
            conv_bc_sum[: KC + 1],
            widen(jnp.stack([head_sum[0, :heads], head_sum[1, :heads], skip_grad]), 1),
            squares_local / tp_count,
        ),
        ("dp", "ctx", "tp"),
    )
    conv_total = narrow(summed[2], 1, channels)
    head_total = narrow(summed[4], 1, heads)
    loss = summed[5] * loss_scale
    reduced = mixer_reduced.astype(f32)
    ffn_reduced = ffn_reduced.astype(f32)
    piece = [reduced[:, edges[i] : edges[i + 1]] for i in range(7)]
    state_reduced = pair_sum(piece[2])
    out_reduced = reduced[:, all_cols:]
    return (
        block_out,
        loss,
        input_grad.reshape(seqs, tokens, width),
        summed[0],
        piece[3],
        jnp.stack([piece[4], piece[5]], 1),
        out_reduced[:, channels:].T,
        reduced[:, : 2 * channels].reshape(rows, 2, channels),
        state_reduced,
        piece[6],
        conv_total[:KC],
        conv_total[KC],
        summed[3][:KC],
        summed[3][KC],
        head_total[0],
        head_total[1],
        head_total[2],
        out_reduced[:, :channels].T,
        summed[1],
        ffn_reduced[:, : 2 * hidden_units].reshape(rows, 2, hidden_units),
        ffn_reduced[:, 2 * hidden_units :].T,
    )


def solution(mesh):
    return jax.shard_map(
        per_device,
        mesh=mesh,
        in_specs=(
            P("dp", "ctx", None),
            P("dp", "ctx"),
            P("dp", "ctx"),
            P("dp", "ctx", None),
            P("dp", "ctx", None),
            P(),
            P(("dp", "ctx"), "tp"),
            P(("dp", "ctx"), None, "tp"),
            P("tp", ("dp", "ctx")),
            P(("dp", "ctx"), None, "tp"),
            P(("dp", "ctx"), None),
            P(("dp", "ctx"), "tp"),
            P(None, "tp"),
            P("tp"),
            P(),
            P(),
            P("tp"),
            P("tp"),
            P("tp"),
            P("tp", ("dp", "ctx")),
            P(),
            P(("dp", "ctx"), None, "tp"),
            P("tp", ("dp", "ctx")),
        ),
        out_specs=(
            P("dp", "ctx", None),
            P(),
            P("dp", "ctx", None),
            P(),
            P(("dp", "ctx"), "tp"),
            P(("dp", "ctx"), None, "tp"),
            P("tp", ("dp", "ctx")),
            P(("dp", "ctx"), None, "tp"),
            P(("dp", "ctx"), None),
            P(("dp", "ctx"), "tp"),
            P(None, "tp"),
            P("tp"),
            P(),
            P(),
            P("tp"),
            P("tp"),
            P("tp"),
            P("tp", ("dp", "ctx")),
            P(),
            P(("dp", "ctx"), None, "tp"),
            P("tp", ("dp", "ctx")),
        ),
        check_vma=False,
    )
```

```python
import functools

import jax
import jax.numpy as jnp
from jax import lax
from jax.experimental import pallas as pl
from jax.experimental.pallas import tpu as pltpu
from jax.sharding import PartitionSpec as P

HEAD_SIZE = 64
MP = 64
NS = 128
KC = 4
CBLK = 128
VMEM_BYTES = 56 * 1024 * 1024

low = jnp.bfloat16
f32 = jnp.float32
highest = lax.Precision.HIGHEST
NEG = -1e30
eps_norm = 1e-05
rope_base = 100000000000.0


def vmem_params():
    return pltpu.CompilerParams(
        dimension_semantics=("arbitrary",), vmem_limit_bytes=VMEM_BYTES
    )


def mm(left, right):
    return jnp.dot(left, right, preferred_element_type=f32)


def mm_nt(left, right):
    return lax.dot_general(left, right, (((1,), (1,)), ((), ())), preferred_element_type=f32)


def mm_tn(left, right):
    return lax.dot_general(left, right, (((0,), (0,)), ((), ())), preferred_element_type=f32)


def iota(shape, axis):
    return lax.broadcasted_iota(jnp.int32, shape, axis)


def sigmoid(v):
    return 1.0 / (1.0 + jnp.exp(-v))


def softplus(v):
    return jnp.maximum(v, 0.0) + jnp.log1p(jnp.exp(-jnp.abs(v)))


def silu_grad(v, sig):
    return sig * (1.0 + v * (1.0 - sig))


def halves(v):
    high = v.astype(low)
    return high, (v - high.astype(f32)).astype(low)


def head_map(channels):
    shape = (128, channels)
    return jnp.where(iota(shape, 1) // MP == iota(shape, 0), 1.0, 0.0).astype(low)


def expand(per_head, spread):
    high, rest = halves(per_head)
    return mm(high, spread) + mm(rest, spread)


def collect(per_channel, spread):
    high, rest = halves(per_channel)
    return mm_nt(high, spread) + mm_nt(rest, spread)


def rotate(u, cosine, sine):
    first = (iota(u.shape, 1) // 32) % 2 == 0
    return u * cosine + jnp.where(first, pltpu.roll(u, 96, 1), pltpu.roll(u, 32, 1)) * sine


def prep_body(q_ref, kv_ref, cos_ref, sin_ref, q_out, kv_out):
    cosine, sine = cos_ref[...], sin_ref[...]
    scale = HEAD_SIZE ** (-0.5)
    for j in range(q_ref.shape[1] // 128):
        cols = slice(128 * j, 128 * j + 128)
        q_out[:, cols] = rotate(q_ref[:, cols], cosine, sine).astype(low) * jnp.asarray(scale, low)
    kv = kv_ref[...]
    keep = iota(kv.shape, 1) < HEAD_SIZE
    kv_out[...] = jnp.where(keep, rotate(kv, cosine, sine), kv).astype(low)


def attend_body(at_ref, q_ref, *refs, hops):
    kv_refs, (o_ref, lse_ref) = refs[:hops], refs[hops:]
    at = at_ref[0]
    tokens = q_ref.shape[0]
    lane = iota((tokens, 128), 1)
    lo = lane < HEAD_SIZE
    causal = iota((tokens, tokens), 0) >= iota((tokens, tokens), 1)
    lse_all = jnp.zeros((tokens, 128), f32)
    for j in range(q_ref.shape[1] // 128):
        pair = q_ref[:, 128 * j : 128 * j + 128].astype(f32)
        sides = []
        for side in range(2):
            query = pair if side == 0 else pltpu.roll(pair, HEAD_SIZE, 1)
            query = jnp.where(lo, query, 0.0).astype(low)
            scores = []
            for d in range(hops):
                score = mm_nt(query, kv_refs[d][...])
                scores.append(
                    jnp.where(causal if d == 0 else at >= d, score, NEG)
                )
            top = functools.reduce(
                jnp.maximum, [jnp.max(s, -1, keepdims=True) for s in scores]
            )
            total, mixed = 0.0, 0.0
            for d in range(hops):
                expo = jnp.exp(scores[d] - top)
                total = total + jnp.sum(expo, -1, keepdims=True)
                mixed = mixed + mm(expo.astype(low), kv_refs[d][...])
            sides.append(mixed * (1.0 / total))
            lse_all = jnp.where(lane == 2 * j + side, top + jnp.log(total), lse_all)
        o_ref[:, 128 * j : 128 * j + 128] = jnp.where(
            lo, pltpu.roll(sides[0], HEAD_SIZE, 1), sides[1]
        ).astype(low)
    lse_ref[...] = lse_all


def attend_back_body(at_ref, q_ref, go_ref, o_ref, lse_ref, cos_ref, sin_ref, *refs, hops):
    kv_refs, (gq_ref,), gkv_refs = refs[:hops], refs[hops : hops + 1], refs[hops + 1 :]
    at = at_ref[0]
    tokens = q_ref.shape[0]
    lane = iota((tokens, 128), 1)
    lo = lane < HEAD_SIZE
    causal = iota((tokens, tokens), 0) >= iota((tokens, tokens), 1)
    cosine, sine = cos_ref[...], sin_ref[...]
    lse_all = lse_ref[...]
    scale = HEAD_SIZE ** (-0.5)
    gkv = [jnp.zeros((tokens, 128), f32) for _ in range(hops)]
    for j in range(q_ref.shape[1] // 128):
        cols = slice(128 * j, 128 * j + 128)
        pair = q_ref[:, cols].astype(f32)
        go_pair = go_ref[:, cols].astype(low).astype(f32)
        weighed = go_pair * o_ref[:, cols].astype(f32)
        sides = []
        for side in range(2):
            query = pair if side == 0 else pltpu.roll(pair, HEAD_SIZE, 1)
            query = jnp.where(lo, query, 0.0).astype(low)
            grad = pltpu.roll(go_pair, HEAD_SIZE, 1) if side == 0 else go_pair
            grad = jnp.where(lo, 0.0, grad).astype(low)
            centre = jnp.sum(jnp.where(lo == (side == 0), weighed, 0.0), -1, keepdims=True)
            lse = jnp.sum(jnp.where(lane == 2 * j + side, lse_all, 0.0), -1, keepdims=True)
            gq = 0.0
            for d in range(hops):
                kv = kv_refs[d][...]
                score = mm_nt(query, kv)
                prob = jnp.exp(jnp.where(causal if d == 0 else at >= d, score, NEG) - lse)
                gprob = mm_nt(grad, kv)
                gscore = (prob * (gprob - centre)).astype(low)
                gq = gq + mm(gscore, kv)
                gkv[d] = gkv[d] + mm_tn(gscore, query) + mm_tn(prob.astype(low), grad)
            sides.append(gq * scale)
        joined = jnp.where(lo, sides[0], pltpu.roll(sides[1], HEAD_SIZE, 1))
        gq_ref[:, cols] = rotate(joined, cosine, -sine).astype(low)
    for d in range(hops):
        gkv_refs[d][...] = gkv[d].astype(low)


def keyval_sum_body(cos_ref, sin_ref, *refs):
    parts, (out_ref,) = refs[:-1], refs[-1:]
    total = parts[0][...].astype(f32)
    for part in parts[1:]:
        total = total + part[...].astype(f32)
    keep = iota(total.shape, 1) < HEAD_SIZE
    rotated = rotate(total, cos_ref[...], -sin_ref[...])
    out_ref[...] = jnp.where(keep, rotated, total).astype(low)


def decay_pair(logs, logs_t, first, keep):
    both = []
    for head in (first, first + 1):
        gap = logs[:, head : head + 1] - logs_t[head : head + 1, :]
        both.append(jnp.exp(jnp.where(keep, gap, NEG)))
    return both


def step_terms(step_ref, rows, heads_ref, heads):
    raw = step_ref[rows, :] + heads_ref[0:1, :]
    live = iota(raw.shape, 1) < heads
    steps = jnp.where(live, softplus(raw), 0.0)
    return jnp.where(live, raw, 0.0), steps


def lower_triangle(size):
    return iota((size, size), 0) >= iota((size, size), 1)


def scan_body(
    x_ref, bc_ref, step_ref, xt_ref, bct_ref, taps_ref, taps_bc_ref, heads_ref,
    v_ref, vbc_ref, y_ref, logs_ref, states_ref, send_ref,
    xe, bce, *, heads,
):
    tokens, channels = x_ref.shape
    xe[0:8, :] = xt_ref[...]
    xe[8:, :] = x_ref[...]
    bce[0:8, :] = bct_ref[...]
    bce[8:, :] = bc_ref[...]
    spread = head_map(channels)
    keep = lower_triangle(CBLK)
    triangle = jnp.where(keep, 1.0, 0.0)
    lo = iota((CBLK, 128), 1) < MP
    rate = heads_ref[1:2, :]
    state = None
    carry = jnp.zeros((1, 128), f32)
    total_decay = None
    for c in range(tokens // CBLK):
        rows = slice(CBLK * c, CBLK * c + CBLK)

        def conv(ext, taps):
            start = CBLK * c + 8 - (KC - 1)
            total = taps[KC : KC + 1, :] + taps[0:1, :] * ext[start : start + CBLK, :]
            for k in range(1, KC):
                total = total + taps[k : k + 1, :] * ext[start + k : start + k + CBLK, :]
            return total

        v = conv(xe, taps_ref)
        v_ref[rows, :] = v
        xs = v * sigmoid(v)
        vbc = conv(bce, taps_bc_ref)
        vbc_ref[rows, :] = vbc
        bc = (vbc * sigmoid(vbc)).astype(low)
        entry, read = bc[:, :NS], bc[:, NS:]
        _, steps = step_terms(step_ref, rows, heads_ref, heads)
        logs = jnp.dot(triangle, -steps * rate, precision=highest, preferred_element_type=f32)
        logs_t = logs.T
        total = logs[CBLK - 1 : CBLK, :]
        logs_ref[rows, :] = logs + carry
        carry = carry + total
        decays = expand(jnp.exp(logs), spread)
        steps_wide = expand(steps, spread)
        tails_wide = expand(jnp.exp(total - logs) * steps, spread)
        weighted = (xs * steps_wide).astype(low)
        inner = mm_nt(read, entry)
        if state is not None:
            incoming = decays * mm(read, state.astype(low))
        for j in range(channels // 128):
            cols = slice(128 * j, 128 * j + 128)
            left, right = decay_pair(logs, logs_t, 2 * j, keep)
            stacked = jnp.concatenate([(inner * left).astype(low), (inner * right).astype(low)], 0)
            result = mm(stacked, weighted[:, cols])
            out = jnp.where(lo, result[:CBLK], result[CBLK:])
            if state is not None:
                out = out + incoming[:, cols]
            y_ref[rows, cols] = out
        added = mm_tn(entry, (xs * tails_wide).astype(low))
        last = decays[CBLK - 1 : CBLK, :]
        state = added if state is None else last * state + added
        total_decay = last if total_decay is None else total_decay * last
        states_ref[NS * c : NS * c + NS, :] = state
    send_ref[0:NS, :] = state.astype(low)
    send_ref[NS:, :] = jnp.broadcast_to(total_decay, (send_ref.shape[0] - NS, channels)).astype(low)


def chained(refs):
    state = None
    for ref in reversed(refs):
        own = ref[0:NS, :].astype(f32)
        if state is None:
            state = own
        else:
            state = own + ref[NS : NS + 1, :].astype(f32) * state
    return state


def gate_body(z_ref, y_ref, v_ref, vbc_ref, logs_ref, heads_ref, *refs):
    earlier, (gated_ref, y_out, carried_ref) = refs[:-3], refs[-3:]
    tokens, channels = y_ref.shape
    spread = head_map(channels)
    skip = expand(heads_ref[...], spread)[2:3, :]
    carried = chained(earlier) if earlier else jnp.zeros((NS, channels), f32)
    carried_ref[...] = carried
    carried_low = carried.astype(low)
    for c in range(tokens // CBLK):
        rows = slice(CBLK * c, CBLK * c + CBLK)
        vc = vbc_ref[rows, NS:]
        read = (vc * sigmoid(vc)).astype(low)
        y = y_ref[rows, :] + expand(jnp.exp(logs_ref[rows, :]), spread) * mm(read, carried_low)
        y_out[rows, :] = y
        v = v_ref[rows, :]
        z = z_ref[rows, :]
        gated_ref[rows, :] = ((y + skip * (v * sigmoid(v))) * (z * sigmoid(z))).astype(low)


def gate_back_body(
    g_ref, z_ref, y_ref, v_ref, vbc_ref, logs_ref, heads_ref, sent_ref,
    dy_ref, dz_ref, dskip_ref, send_ref,
):
    tokens, channels = y_ref.shape
    spread = head_map(channels)
    skip = expand(heads_ref[...], spread)[2:3, :]
    state, dskip = 0.0, 0.0
    for c in range(tokens // CBLK):
        rows = slice(CBLK * c, CBLK * c + CBLK)
        vc = vbc_ref[rows, NS:]
        read = (vc * sigmoid(vc)).astype(low)
        v = v_ref[rows, :]
        xs = v * sigmoid(v)
        z = z_ref[rows, :]
        sig = sigmoid(z)
        grad = g_ref[rows, :].astype(f32)
        dy = grad * (z * sig)
        dz_ref[rows, :] = (grad * (y_ref[rows, :] + skip * xs) * silu_grad(z, sig)).astype(low)
        dy_ref[rows, :] = dy
        dskip = dskip + jnp.sum(dy * xs, 0, keepdims=True)
        faded = (dy * expand(jnp.exp(logs_ref[rows, :]), spread)).astype(low)
        state = state + mm_tn(read, faded)
    send_ref[0:NS, :] = state.astype(low)
    send_ref[NS:, :] = sent_ref[NS:, :]
    dskip_ref[...] = jnp.broadcast_to(dskip, dskip_ref.shape)


def scan_back_body(
    dy_ref, y_ref, v_ref, vbc_ref, x_ref, bc_ref, step_ref, xt_ref, bct_ref,
    taps_ref, taps_bc_ref, heads_ref, logs_ref, states_ref, carried_ref, *refs, heads,
):
    later, refs = refs[:-10], refs[-10:]
    dx_ref, dbc_ref, dstep_ref, edge_ref, head_ref, gx_ref, gbc_ref, gh_ref, dve, dbce = refs
    tokens, channels = y_ref.shape
    chunks = tokens // CBLK
    spread = head_map(channels)
    keep = lower_triangle(CBLK)
    triangle = jnp.where(keep, 1.0, 0.0)
    lo = iota((CBLK, 128), 1) < MP
    rate = heads_ref[1:2, :]
    skip = expand(heads_ref[...], spread)[2:3, :]
    dstate = chained(later) if later else jnp.zeros((NS, channels), f32)
    dve[0:8, :] = jnp.zeros((8, channels), f32)
    dve[8 + tokens :, :] = jnp.zeros((8, channels), f32)
    dbce[0:8, :] = jnp.zeros((8, 2 * NS), f32)
    dbce[8 + tokens :, :] = jnp.zeros((8, 2 * NS), f32)
    dbias, ddecay = 0.0, 0.0
    for c in reversed(range(chunks)):
        rows = slice(CBLK * c, CBLK * c + CBLK)
        v = v_ref[rows, :]
        sig = sigmoid(v)
        xs = v * sig
        vbc = vbc_ref[rows, :]
        sig_bc = sigmoid(vbc)
        bc = (vbc * sig_bc).astype(low)
        entry, read = bc[:, :NS], bc[:, NS:]
        raw, steps = step_terms(step_ref, rows, heads_ref, heads)
        logs = jnp.dot(triangle, -steps * rate, precision=highest, preferred_element_type=f32)
        logs_t = logs.T
        total = logs[CBLK - 1 : CBLK, :]
        decays = expand(jnp.exp(logs), spread)
        steps_wide = expand(steps, spread)
        tails_wide = expand(jnp.exp(total - logs), spread)
        last = decays[CBLK - 1 : CBLK, :]
        if c == 0:
            state = carried_ref[...]
        else:
            before = expand(jnp.exp(logs_ref[CBLK * c - 8 : CBLK * c, :]), spread)[7:8, :]
            state = states_ref[NS * (c - 1) : NS * c, :] + before * carried_ref[...]
        dy = dy_ref[rows, :]
        dy_low = dy.astype(low)
        w = xs * steps_wide
        w_low = w.astype(low)
        inner = mm_nt(read, entry)
        state_low = state.astype(low)
        dstate_low = dstate.astype(low)
        dw_later = tails_wide * mm(entry, dstate_low)
        faded = (dy * decays).astype(low)
        dread = mm_nt(faded, state_low)
        dentry = mm_nt((w * tails_wide).astype(low), dstate_low)
        dinner = 0.0
        pieces = []
        for j in range(channels // 128):
            cols = slice(128 * j, 128 * j + 128)
            left, right = decay_pair(logs, logs_t, 2 * j, keep)
            dy_pair, w_pair = dy_low[:, cols], w_low[:, cols]
            weights = jnp.concatenate([(inner * left).astype(low), (inner * right).astype(low)], 1)
            result = mm_tn(weights, dy_pair)
            pieces.append(jnp.where(lo, result[:CBLK], result[CBLK:]) + dw_later[:, cols])
            zero = jnp.zeros_like(dy_pair)
            parted = jnp.concatenate([jnp.where(lo, dy_pair, zero), jnp.where(lo, zero, dy_pair)], 0)
            dweights = mm_nt(parted, w_pair)
            dinner = dinner + dweights[:CBLK] * left + dweights[CBLK:] * right
        dw = jnp.concatenate(pieces, 1)
        dinner_low = dinner.astype(low)
        dread = dread + mm(dinner_low, entry)
        dentry = dentry + mm_tn(dinner_low, read)
        dlogs = collect(dy * y_ref[rows, :] - w * dw, spread)
        dtotal = jnp.sum(w * dw_later, 0, keepdims=True) + last * jnp.sum(
            dstate * state, 0, keepdims=True
        )
        dtotal = collect(jnp.broadcast_to(dtotal, (8, channels)), spread)[0:1, :]
        dfall = (
            lax.dot_general(
                triangle, dlogs, (((0,), (0,)), ((), ())),
                precision=highest, preferred_element_type=f32,
            )
            + dtotal
        )
        dsteps = collect(xs * dw, spread) - rate * dfall
        ddecay = ddecay - rate * jnp.sum(steps * dfall, 0, keepdims=True)
        live = iota(raw.shape, 1) < heads
        draw = jnp.where(live, dsteps * sigmoid(raw), 0.0)
        dbias = dbias + jnp.sum(draw, 0, keepdims=True)
        dstep_ref[rows, :] = draw.astype(low)
        dve[8 + CBLK * c : 8 + CBLK * c + CBLK, :] = (steps_wide * dw + skip * dy) * silu_grad(v, sig)
        dbce[8 + CBLK * c : 8 + CBLK * c + CBLK, :] = jnp.concatenate(
            [dentry, dread], 1
        ) * silu_grad(vbc, sig_bc)
        dstate = last * dstate + mm_tn(read, faded)
    gh_ref[0:1, :] = dbias
    gh_ref[1:2, :] = ddecay
    gh_ref[2:, :] = jnp.zeros((gh_ref.shape[0] - 2, 128), f32)

    def conv_back(ext, taps, out_ref, cols, grads_ref, pre_ref, tail_ref):
        def spread_rows(start, count):
            total = taps[0:1, :] * ext[start + KC - 1 : start + KC - 1 + count, :]
            for k in range(1, KC):
                at = start + KC - 1 - k
                total = total + taps[k : k + 1, :] * ext[at : at + count, :]
            return total

        head_ref[0:8, cols] = jnp.zeros((8, ext.shape[1]), f32)
        head_ref[8:16, cols] = spread_rows(0, 8)
        grads = [0.0] * (KC + 1)
        for c in range(chunks):
            at = CBLK * c
            dpre = spread_rows(8 + at, CBLK)
            out_ref[at : at + CBLK, :] = dpre.astype(low)
            if c == chunks - 1:
                edge_ref[:, cols] = dpre[CBLK - 16 :, :]
        for k in range(KC):
            shift = KC - 1 - k
            main = jnp.sum(pre_ref[...] * ext[8 + shift : 8 + shift + tokens, :], 0, keepdims=True)
            edge = jnp.sum(tail_ref[...] * ext[shift : shift + 8, :], 0, keepdims=True)
            grads[k] = main + edge
        grads[KC] = jnp.sum(ext[8 : 8 + tokens, :], 0, keepdims=True)
        for k in range(KC + 1):
            grads_ref[k : k + 1, :] = grads[k]
        grads_ref[KC + 1 :, :] = jnp.zeros((grads_ref.shape[0] - KC - 1, ext.shape[1]), f32)

    conv_back(dve, taps_ref, dx_ref, slice(0, channels), gx_ref, x_ref, xt_ref)
    bc_cols = slice(channels, channels + 2 * NS)
    conv_back(dbce, taps_bc_ref, dbc_ref, bc_cols, gbc_ref, bc_ref, bct_ref)


def block(height, width, col=0, first=0):
    return pl.BlockSpec((height, width), lambda s: (first + s, col))


def whole(shape):
    return pl.BlockSpec(shape, lambda s: (0, 0))


def shaped(rows, cols, dtype):
    return jax.ShapeDtypeStruct((rows, cols), dtype)


def run(body, seqs, inputs, outputs, scratch=(), at=None, flops=0, shared=()):
    arrays = [a for a, _ in inputs]
    specs = [s for _, s in inputs]
    if at is not None:
        arrays = [at] + arrays
        specs = [pl.BlockSpec(memory_space=pltpu.SMEM)] + specs
    moved = sum(a.size * a.dtype.itemsize for a in arrays)
    out_specs = [block(r, c) for r, c, _ in outputs]
    out_shape = [shaped(seqs * r, c, d) for r, c, d in outputs]
    aliases, count = {}, len(arrays)
    for r, c, d, total, first, previous in shared:
        if previous is not None:
            aliases[len(arrays)] = len(out_shape)
            arrays.append(previous)
            specs.append(pl.BlockSpec(memory_space=pl.ANY))
        out_specs.append(block(r, c, 0, first))
        out_shape.append(shaped(total * r, c, d))
    kept = len(aliases)

    def inner(*refs):
        body(*refs[:count], *refs[count + kept :])

    return pl.pallas_call(
        inner,
        grid=(seqs,),
        in_specs=specs,
        out_specs=out_specs,
        out_shape=out_shape,
        scratch_shapes=list(scratch),
        input_output_aliases=aliases,
        compiler_params=vmem_params(),
        cost_estimate=pl.CostEstimate(flops=flops, bytes_accessed=moved, transcendentals=0),
    )(*arrays)


def prep(pre, cosine, sine, seqs, tokens, q_at, q_cols, kv_at):
    return run(
        prep_body,
        seqs,
        [
            (pre, block(tokens, q_cols, q_at // q_cols)),
            (pre, block(tokens, 128, kv_at // 128)),
            (cosine, block(tokens, 128)),
            (sine, block(tokens, 128)),
        ],
        [(tokens, q_cols, low), (tokens, 128, low)],
    )


def attend(queries, keyvals, at, seqs, tokens):
    hops, cols = len(keyvals), queries.shape[1]
    work = 4 * seqs * tokens * tokens * hops * (cols // HEAD_SIZE) * 256
    return run(
        functools.partial(attend_body, hops=hops),
        seqs,
        [(queries, block(tokens, cols))] + [(kv, block(tokens, 128)) for kv in keyvals],
        [(tokens, cols, low), (tokens, 128, f32)],
        at=at,
        flops=work,
    )


def attend_back(
    queries, keyvals, grads, grad_at, outs, lse, cosine, sine, at, first, seqs, tokens, previous
):
    hops, cols = len(keyvals), queries.shape[1]
    work = 10 * tokens * tokens * hops * (cols // HEAD_SIZE) * 256
    return run(
        functools.partial(attend_back_body, hops=hops),
        1,
        [
            (queries, block(tokens, cols, 0, first)),
            (grads, block(tokens, cols, grad_at // cols)),
            (outs, block(tokens, cols, 0, first)),
            (lse, block(tokens, 128, 0, first)),
            (cosine, block(tokens, 128, 0, first)),
            (sine, block(tokens, 128, 0, first)),
        ]
        + [(kv, block(tokens, 128, 0, first)) for kv in keyvals],
        [(tokens, cols, low)],
        at=at,
        flops=work,
        shared=[(tokens, 128, low, seqs, first, p) for p in previous],
    )


def keyval_sum(parts, cosine, sine, seqs, tokens):
    return run(
        keyval_sum_body,
        seqs,
        [(a, block(tokens, 128)) for a in (cosine, sine, *parts)],
        [(tokens, 128, low)],
    )[0]


SENT = NS + 16


class Columns:
    def __init__(self, channels, q_cols):
        self.channels = channels
        self.x, self.z, self.q = 0, channels, 2 * channels
        self.bc = self.q + q_cols
        self.kv = self.bc + 2 * NS
        self.step = self.kv + 128
        self.total = self.step + 128

    def x_block(self, tokens, first=0):
        return block(tokens, self.channels, 0, first)

    def z_block(self, tokens, first=0):
        return block(tokens, self.channels, 1, first)

    def bc_block(self, tokens, first=0):
        return block(tokens, 2 * NS, self.bc // (2 * NS), first)

    def step_block(self, tokens, first=0):
        return block(tokens, 128, self.step // 128, first)


def scan(pre, cols, tails, taps, taps_bc, per_head, seqs, tokens, heads):
    channels = cols.channels
    return run(
        functools.partial(scan_body, heads=heads),
        seqs,
        [
            (pre, cols.x_block(tokens)),
            (pre, cols.bc_block(tokens)),
            (pre, cols.step_block(tokens)),
            (tails, block(8, channels)),
            (tails, block(8, 2 * NS, channels // (2 * NS))),
            (taps, whole(taps.shape)),
            (taps_bc, whole(taps_bc.shape)),
            (per_head, whole(per_head.shape)),
        ],
        [
            (tokens, channels, f32),
            (tokens, 2 * NS, f32),
            (tokens, channels, f32),
            (tokens, 128, f32),
            (tokens // CBLK * NS, channels, f32),
            (SENT, channels, low),
        ],
        scratch=[pltpu.VMEM((tokens + 8, channels), f32), pltpu.VMEM((tokens + 8, 2 * NS), f32)],
        flops=8 * seqs * tokens * CBLK * channels,
    )


def gate(pre, cols, y, v, vbc, logs, per_head, earlier, first, tokens):
    channels = cols.channels
    return run(
        gate_body,
        1,
        [
            (pre, cols.z_block(tokens, first)),
            (y, block(tokens, channels, 0, first)),
            (v, block(tokens, channels, 0, first)),
            (vbc, block(tokens, 2 * NS, 0, first)),
            (logs, block(tokens, 128, 0, first)),
            (per_head, whole(per_head.shape)),
        ]
        + [(a, block(SENT, channels, 0, first)) for a in earlier],
        [(tokens, channels, low), (tokens, channels, f32), (NS, channels, f32)],
        flops=4 * tokens * CBLK * channels,
    )


def gate_back(grads, pre, cols, y, v, vbc, logs, per_head, sent, first, seqs, tokens, previous):
    channels = cols.channels
    return run(
        gate_back_body,
        1,
        [
            (grads, block(tokens, channels)),
            (pre, cols.z_block(tokens, first)),
            (y, block(tokens, channels)),
            (v, block(tokens, channels, 0, first)),
            (vbc, block(tokens, 2 * NS, 0, first)),
            (logs, block(tokens, 128, 0, first)),
            (per_head, whole(per_head.shape)),
            (sent, block(SENT, channels, 0, first)),
        ],
        [
            (tokens, channels, f32),
            (tokens, channels, low),
            (8, channels, f32),
        ],
        flops=4 * tokens * CBLK * channels,
        shared=[(SENT, channels, low, seqs, first, previous)],
    )


def scan_back(
    dy, y, v, vbc, pre, cols, tails, taps, taps_bc, per_head, logs, states, carried, later,
    first, tokens, heads,
):
    channels = cols.channels
    return run(
        functools.partial(scan_back_body, heads=heads),
        1,
        [
            (dy, block(tokens, channels)),
            (y, block(tokens, channels)),
            (v, block(tokens, channels, 0, first)),
            (vbc, block(tokens, 2 * NS, 0, first)),
            (pre, cols.x_block(tokens, first)),
            (pre, cols.bc_block(tokens, first)),
            (pre, cols.step_block(tokens, first)),
            (tails, block(8, channels, 0, first)),
            (tails, block(8, 2 * NS, channels // (2 * NS), first)),
            (taps, whole(taps.shape)),
            (taps_bc, whole(taps_bc.shape)),
            (per_head, whole(per_head.shape)),
            (logs, block(tokens, 128, 0, first)),
            (states, block(tokens // CBLK * NS, channels, 0, first)),
            (carried, block(NS, channels)),
        ]
        + [(a, block(SENT, channels, 0, first)) for a in later],
        [
            (tokens, channels, low),
            (tokens, 2 * NS, low),
            (tokens, 128, low),
            (16, channels + 2 * NS, f32),
            (16, channels + 2 * NS, f32),
            (8, channels, f32),
            (8, 2 * NS, f32),
            (8, 128, f32),
        ],
        scratch=[
            pltpu.VMEM((tokens + 16, channels), f32),
            pltpu.VMEM((tokens + 16, 2 * NS), f32),
        ],
        flops=30 * tokens * CBLK * channels,
    )


TILE = 256


def hold(held, first_tile, rows, parts):
    col = first_tile * TILE
    for part in parts:
        width = min(part.shape[1], TILE)
        for at in range(0, part.shape[1], width):
            inside = col % TILE
            held[col // TILE, rows, inside : inside + width] = part[:, at : at + width]
            col += width


def early_grads_body(left_ref, weight_ref, *refs, seqs):
    pieces, (wgrad_ref, part_ref, held) = refs[:-3], refs[-3:]
    tile = pl.program_id(0)
    tokens = held.shape[1] // seqs

    @pl.when(tile == 0)
    def _():
        for s in range(seqs):
            hold(held, 0, slice(tokens * s, tokens * (s + 1)), pieces[2 * s : 2 * s + 2])
        part_ref[...] = jnp.zeros_like(part_ref)

    grads = held[tile]
    wgrad_ref[...] = mm(left_ref[...], grads).astype(low)
    part_ref[...] += mm_nt(grads, weight_ref[...])


def late_grads_body(left_ref, weight_ref, start_ref, keyval_ref, *refs, seqs):
    pieces, (wgrad_ref, part_ref, held, total) = refs[:-4], refs[-4:]
    tile = pl.program_id(0)
    tokens = held.shape[1] // seqs

    @pl.when(tile == 0)
    def _():
        for s in range(seqs):
            dx, dbc, dstep, edge, head = pieces[5 * s : 5 * s + 5]
            rows = slice(tokens * s, tokens * (s + 1))
            hold(held, 0, rows, (dx, dbc, keyval_ref.at[rows, :], dstep))
            mended = (edge[...] + head[16 * s : 16 * s + 16, :]).astype(low)
            for at in range(0, mended.shape[1], TILE):
                held[at // TILE, tokens * (s + 1) - 16 : tokens * (s + 1), :] = mended[
                    :, at : at + TILE
                ]
        total[...] = start_ref[...]

    grads = held[tile]
    wgrad_ref[...] = mm(left_ref[...], grads).astype(low)
    total[...] += mm_nt(grads, weight_ref[...])

    @pl.when(tile == pl.num_programs(0) - 1)
    def _():
        part_ref[...] = total[...].astype(low)


def tiled_grads(body, left, weight, tile_of, tiles, arrays, part_dtype, scratch):
    width, rows = left.shape
    return pl.pallas_call(
        body,
        grid=(tiles,),
        in_specs=[whole(left.shape), pl.BlockSpec((width, TILE), lambda t: (0, tile_of(t)))]
        + [whole(a.shape) for a in arrays],
        out_specs=[pl.BlockSpec((width, TILE), lambda t: (0, t)), whole((rows, width))],
        out_shape=[shaped(width, tiles * TILE, low), shaped(rows, width, part_dtype)],
        scratch_shapes=[pltpu.VMEM((tiles, rows, TILE), low), *scratch],
        compiler_params=vmem_params(),
        cost_estimate=pl.CostEstimate(
            flops=4 * rows * tiles * TILE * width,
            bytes_accessed=4 * width * tiles * TILE,
            transcendentals=0,
        ),
    )(left, weight, *arrays)


def early_grads(left, weight, cols, pieces, seqs):
    first = cols.z // TILE
    tiles = (cols.bc - cols.z) // TILE
    return tiled_grads(
        functools.partial(early_grads_body, seqs=seqs),
        left, weight, lambda t: t + first, tiles, [a for p in pieces for a in p], f32, [],
    )


def late_grads(left, weight, cols, start, keyval, pieces, seqs):
    before = cols.z // TILE
    skipped = (cols.bc - cols.z) // TILE
    return tiled_grads(
        functools.partial(late_grads_body, seqs=seqs),
        left,
        weight,
        lambda t: jnp.where(t < before, t, t + skipped),
        cols.total // TILE - skipped,
        [start, keyval] + [a for p in pieces for a in p],
        low,
        [pltpu.VMEM(start.shape, f32)],
    )


def passed_along(array, axis, distance):
    devices = range(lax.axis_size(axis))
    route = [(i - distance, i) for i in devices if i - distance in devices]
    return lax.ppermute(array, axis, route)


def after(array, *others):
    return lax.optimization_barrier((array, *others))[0]


def swapped(array, axis, distance):
    devices = range(lax.axis_size(axis))
    return lax.ppermute(array, axis, [(i, i ^ distance) for i in devices])


def offer(part):
    mine = part.astype(low)
    return mine, swapped(mine, "tp", 1)


def summed_pair(mine, other):
    return mine.astype(f32) + other.astype(f32)


def sum_over(array, axes):
    for axis in axes:
        distance = 1
        while distance < lax.axis_size(axis):
            array = array + swapped(array, axis, distance)
            distance *= 2
    return array


def place(axis, distance=0):
    return lax.axis_index(axis).astype(jnp.uint32) ^ jnp.uint32(distance)


def place(axis, distance=0):
    return lax.axis_index(axis).astype(jnp.uint32) ^ jnp.uint32(distance)


def picked(array, at, dim):
    return lax.dynamic_index_in_dim(array, at, dim, False)


def core_sum(terms):
    dp, ctx = lax.axis_size("dp"), lax.axis_size("ctx")
    rows, cols = terms.shape[0] // (dp * ctx), terms.shape[1]
    one = jnp.uint32(1)
    pieces = terms.reshape(dp, ctx // 2, 2, rows, cols)
    got = swapped(picked(pieces, place("ctx", 1) & one, 2), "ctx", 1)
    return (picked(pieces, place("ctx") & one, 2).astype(f32) + got.astype(f32)).astype(low)


def spread(held, axis, dim, shift):
    own = picked(held, place(axis) >> jnp.uint32(shift), dim)
    sends = [
        picked(held, place(axis, d << shift) >> jnp.uint32(shift), dim)
        for d in range(1, held.shape[dim])
    ]
    return own, sends, [swapped(a, axis, (d + 1) << shift) for d, a in enumerate(sends)]


def added(own, got):
    total = own.astype(f32)
    for block_in in got:
        total = total + block_in.astype(f32)
    return total


def rms_norm(values, gain):
    return values * lax.rsqrt(jnp.mean(values * values, -1, keepdims=True) + eps_norm) * gain


def angle_tables(positions):
    half = HEAD_SIZE // 2
    freqs = rope_base ** (-2.0 * jnp.arange(half, dtype=f32) / HEAD_SIZE)
    angles = positions.reshape(-1, 1).astype(f32) * freqs
    cosine, sine = jnp.cos(angles), jnp.sin(angles)
    return jnp.tile(cosine, (1, 4)), jnp.concatenate([-sine, sine, -sine, sine], 1)


def per_device(
    hidden_in,
    positions,
    valid_mask,
    teacher,
    cotangent,
    mixer_gain,
    query_weight,
    keyvalue_projection_weight,
    attnout_weight,
    stream_weight,
    state_weight,
    step_weight,
    conv_stream,
    bias_stream,
    conv_state,
    bias_state,
    step_bias,
    decay_log,
    skip_scale,
    mambaout_weight,
    ffn_gain,
    gateup_weight,
    down_weight,
):
    seqs, tokens, width = hidden_in.shape
    owners = ("dp", "ctx")
    rows = query_weight.shape[0]
    q_cols = query_weight.shape[1]
    kv_cols = keyvalue_projection_weight.shape[2]
    channels = stream_weight.shape[2]
    bc_cols = state_weight.shape[1]
    heads = step_weight.shape[1]
    hidden_units = gateup_weight.shape[2]
    step_cols = 128
    hops = lax.axis_size("ctx")
    each = range(seqs)

    tallies = jnp.sum(valid_mask.reshape(seqs * tokens // CBLK, CBLK), -1).astype(low)
    spare = jnp.zeros((rows, step_cols - heads), low)
    spare = spare.at[0, : tallies.shape[0]].set(tallies)
    mixer_shard = jnp.concatenate(
        [
            stream_weight[:, 1],
            stream_weight[:, 0],
            query_weight,
            state_weight,
            keyvalue_projection_weight.reshape(rows, 2 * kv_cols),
            step_weight,
            spare,
            mambaout_weight.T,
            attnout_weight.T,
        ],
        1,
    )
    cols = Columns(channels, q_cols)
    all_cols = cols.total
    mixer_both = lax.all_gather(mixer_shard, owners, axis=0, tiled=True)
    mixer_full, out_full_w = mixer_both[:, :all_cols], mixer_both[:, all_cols:]
    ffn_shard = jnp.concatenate(
        [gateup_weight.reshape(rows, 2 * hidden_units), down_weight.T], 1
    )
    ffn_full = lax.all_gather(ffn_shard, owners, axis=0, tiled=True)
    gateup_full = ffn_full[:, : 2 * hidden_units]
    down_full = ffn_full[:, 2 * hidden_units :]

    counts = mixer_both.reshape(-1, rows, mixer_both.shape[1])
    counts = counts[:, 0, cols.step + heads : cols.step + heads + tallies.shape[0]]
    valid_total = jnp.sum(counts.astype(f32))

    at = lax.axis_index("ctx").astype(jnp.int32).reshape(1)
    cosine, sine = angle_tables(positions)

    def taps_of(taps, bias):
        spare_rows = jnp.zeros((8 - KC - 1, taps.shape[1]), f32)
        return jnp.concatenate([taps, bias[None], spare_rows], 0)

    taps, taps_bc = taps_of(conv_stream, bias_stream), taps_of(conv_state, bias_state)
    per_head = jnp.pad(
        jnp.stack([step_bias, jnp.exp(decay_log), skip_scale]), ((0, 5), (0, 128 - heads))
    )

    hidden = hidden_in.astype(f32)
    normed = rms_norm(hidden, mixer_gain).astype(low).reshape(seqs * tokens, width)
    normed, normed_t = lax.optimization_barrier((normed, normed.T))
    pre = jnp.dot(normed, mixer_full, preferred_element_type=f32)

    def last_rows(array):
        return array.reshape(seqs, tokens, -1)[:, tokens - 8 :].reshape(seqs * 8, -1)

    ends = last_rows(pre)
    ends = jnp.concatenate([ends[:, : cols.z], ends[:, cols.bc : cols.kv]], 1)
    tails = passed_along(ends, "ctx", 1)
    queries, keyval = prep(pre, cosine, sine, seqs, tokens, cols.q, q_cols, cols.kv)
    keyvals = [keyval] + [passed_along(keyval, "ctx", d) for d in range(1, hops)]
    v, vbc, y_own, logs, states, sent = scan(
        pre, cols, tails, taps, taps_bc, per_head, seqs, tokens, heads
    )
    earlier = [passed_along(sent, "ctx", d) for d in range(1, hops)]
    attended, lse = attend(after(queries, sent), keyvals, at, seqs, tokens)
    y, carried, mixers, offers = [], [], [], []
    for s in each:
        here = gate(pre, cols, y_own, v, vbc, logs, per_head, earlier, s, tokens)
        y.append(here[1])
        carried.append(here[2])
        mixers.append(
            jnp.concatenate([here[0], attended[tokens * s : tokens * (s + 1)]], -1)
        )
        offers.append(
            offer(jnp.einsum("ti,di->td", mixers[s], out_full_w, preferred_element_type=f32))
        )

    mask_float = valid_mask.astype(f32)[..., None]
    loss_scale = 1.0 / (valid_total * width)
    squares_local = jnp.zeros((), f32)
    resid, normed_two, gateup, inner = [], [], [], []
    down_offers = []
    for s in each:
        mine, other = offers[s]
        other = after(other, offers[-1][0], *(d[0] for d in down_offers))
        resid.append(hidden[s] + summed_pair(mine, other))
        normed_two.append(rms_norm(resid[s], ffn_gain).astype(low))
        gateup.append(jnp.dot(normed_two[s], gateup_full, preferred_element_type=f32))
        inner.append(
            (jax.nn.silu(gateup[s][:, :hidden_units]) * gateup[s][:, hidden_units:]).astype(low)
        )
        down_offers.append(
            offer(jnp.einsum("tf,df->td", inner[s], down_full, preferred_element_type=f32))
        )
    out_full, out_grad, down_in, gateup_low, back_offers = [], [], [], [], []

    def swiglu_flat(both):
        return jax.nn.silu(both[:, :hidden_units]) * both[:, hidden_units:]

    for s in each:
        mine, other = down_offers[s]
        other = after(other, down_offers[-1][0], *(d[0] for d in back_offers))
        out_full.append(resid[s] + summed_pair(mine, other))
        diff = out_full[s] - teacher[s].astype(f32)
        squares_local = squares_local + jnp.sum(mask_float[s] * diff * diff)
        out_grad.append(cotangent[s].astype(f32) + mask_float[s] * 2.0 * diff * loss_scale)
        down_in.append(out_grad[s].astype(low))
        inner_grad = jnp.einsum("td,df->tf", down_in[s], down_full, preferred_element_type=f32)
        gateup_low.append(jax.vjp(swiglu_flat, gateup[s])[1](inner_grad)[0].astype(low))
        back_offers.append(
            offer(jnp.einsum("tc,dc->td", gateup_low[s], gateup_full, preferred_element_type=f32))
        )
    block_out = jnp.stack(out_full).astype(low)

    def wgrad(left, right):
        return jnp.einsum("td,tc->dc", left, right, preferred_element_type=f32).astype(low)

    join = lambda parts: jnp.concatenate(parts, 0)
    ffn_wgrads = [
        wgrad(join(normed_two), join(gateup_low)),
        wgrad(join(down_in), join(inner)),
    ]

    ffn_terms = jnp.concatenate(ffn_wgrads, 1)
    ffn_reduced = lax.psum_scatter(ffn_terms, owners, scatter_dimension=0, tiled=True)

    resid_grad, mixed_low, ffn_gain_grad = [], [], 0.0
    dy, dz, skip_rows, mixers_grads = [], [], [], []
    sent_back = None
    for s in each:
        mine, other = back_offers[s]
        other = after(other, ffn_terms, *([sent_back] if s else []))
        back = jax.vjp(rms_norm, resid[s], ffn_gain)[1](summed_pair(mine, other))
        resid_grad.append(out_grad[s] + back[0])
        ffn_gain_grad = ffn_gain_grad + back[1]
        mixed_low.append(resid_grad[s].astype(low))
        mixers_grads.append(jnp.dot(mixed_low[s], out_full_w, preferred_element_type=f32))
        *here, sent_back = gate_back(
            mixers_grads[s], pre, cols, y[s], v, vbc, logs, per_head, sent, s, seqs, tokens,
            sent_back,
        )
        dy.append(here[0])
        dz.append(here[1])
        skip_rows.append(here[2])
    later = [passed_along(sent_back, "ctx", -d) for d in range(1, hops)]
    query_back, keyval_parts = [], [None] * hops
    for s in each:
        gq, *keyval_parts = attend_back(
            queries, keyvals, after(mixers_grads[s], sent_back), channels, attended, lse,
            cosine, sine, at, s, seqs, tokens, keyval_parts,
        )
        query_back.append(gq)
    keyval_parts = [keyval_parts[0]] + [
        passed_along(keyval_parts[d], "ctx", -d) for d in range(1, hops)
    ]
    out_wgrad = wgrad(join(mixed_low), join(mixers))
    early_terms, part = early_grads(
        after(normed_t, *later), mixer_both, cols, [[dz[s], query_back[s]] for s in each], seqs
    )
    early_terms = jnp.concatenate([early_terms, out_wgrad], 1)
    early_reduced = lax.psum_scatter(early_terms, owners, scatter_dimension=0, tiled=True)
    scan_backs = []
    for s in each:
        scan_backs.append(
            scan_back(
                after(dy[s], early_terms), y[s], v, vbc, pre, cols, tails, taps, taps_bc, per_head,
                logs, states, carried[s], later, s, tokens, heads,
            )
        )
    keyval_back = keyval_sum(keyval_parts, cosine, sine, seqs, tokens)
    head = passed_along(join([scan_backs[s][4] for s in each]), "ctx", -1)
    late_terms, part = late_grads(
        normed_t, mixer_both, cols, after(part, ffn_reduced), keyval_back,
        [[*scan_backs[s][:4], head] for s in each], seqs,
    )
    part = [part[tokens * s : tokens * (s + 1)] for s in each]
    part_other = [swapped(p, "tp", 1) for p in part]
    own, sends, got = spread(core_sum(late_terms), "ctx", 1, 1)

    hidden_rows = [hidden[s] for s in each]
    norm_one_back = [jax.vjp(rms_norm, hidden_rows[s], mixer_gain)[1] for s in each]
    mixer_gain_grad = sum(norm_one_back[s](part[s].astype(f32))[1] for s in each)

    tp_index = lax.axis_index("tp")
    tp_count = lax.axis_size("tp")

    def widen(piece, axis_dim):
        shape_full = list(piece.shape)
        shape_full[axis_dim] = piece.shape[axis_dim] * tp_count
        blank = jnp.zeros(tuple(shape_full), f32)
        return lax.dynamic_update_slice_in_dim(
            blank, piece, tp_index * piece.shape[axis_dim], axis_dim
        )

    def narrow(wide, axis_dim, piece_size):
        return lax.dynamic_slice_in_dim(wide, tp_index * piece_size, piece_size, axis_dim)

    conv_sum, conv_bc_sum, head_sum = (
        sum(scan_backs[s][i] for s in each) for i in (5, 6, 7)
    )
    skip_grad = jnp.sum(sum(skip_rows[s][0] for s in each).reshape(heads, MP), -1)
    small = [
        mixer_gain_grad,
        ffn_gain_grad / tp_count,
        widen(conv_sum[: KC + 1], 1),
        conv_bc_sum[: KC + 1],
        widen(jnp.stack([head_sum[0, :heads], head_sum[1, :heads], skip_grad]), 1),
        (squares_local / tp_count).reshape(1),
    ]
    flat = jnp.concatenate([a.reshape(-1) for a in small])
    fill = -flat.shape[0] % 1024
    flat = after(jnp.pad(flat, (0, fill)).reshape(-1, 128), *sends)
    flat = sum_over(flat, ("ctx",))
    held = after(added(own, got).astype(low), part_other[0], flat)
    own, sends, got = spread(held, "dp", 0, 0)
    flat = sum_over(after(flat, *sends), ("tp", "dp"))
    late_reduced = added(own, [after(got[0], flat), *got[1:]])
    flat = flat.reshape(-1)
    input_grad = []
    for s in each:
        other = part_other[s] if s == 0 else after(part_other[s], *sends)
        back = norm_one_back[s](summed_pair(part[s], other))[0]
        input_grad.append((resid_grad[s] + back).astype(low))
    summed, start = [], 0
    for a in small:
        summed.append(flat[start : start + a.size].reshape(a.shape))
        start += a.size
    conv_total = narrow(summed[2], 1, channels)
    head_total = narrow(summed[4], 1, heads)
    loss = summed[5][0] * loss_scale
    ffn_reduced = ffn_reduced.astype(f32)
    early_reduced = after(early_reduced, late_reduced).astype(f32)
    out_reduced = early_reduced[:, channels + q_cols :]
    state_reduced = summed_pair(*offer(late_reduced[:, channels : channels + bc_cols]))
    rest = late_reduced[:, channels + bc_cols :]
    return (
        block_out,
        loss,
        jnp.stack(input_grad),
        summed[0],
        early_reduced[:, channels : channels + q_cols],
        jnp.stack([rest[:, :kv_cols], rest[:, kv_cols : 2 * kv_cols]], 1),
        out_reduced[:, channels:].T,
        jnp.stack([early_reduced[:, :channels], late_reduced[:, :channels]], 1),
        state_reduced,
        rest[:, 2 * kv_cols : 2 * kv_cols + heads],
        conv_total[:KC],
        conv_total[KC],
        summed[3][:KC],
        summed[3][KC],
        head_total[0],
        head_total[1],
        head_total[2],
        out_reduced[:, :channels].T,
        summed[1],
        ffn_reduced[:, : 2 * hidden_units].reshape(rows, 2, hidden_units),
        ffn_reduced[:, 2 * hidden_units :].T,
    )


def solution(mesh):
    return jax.shard_map(
        per_device,
        mesh=mesh,
        in_specs=(
            P("dp", "ctx", None),
            P("dp", "ctx"),
            P("dp", "ctx"),
            P("dp", "ctx", None),
            P("dp", "ctx", None),
            P(),
            P(("dp", "ctx"), "tp"),
            P(("dp", "ctx"), None, "tp"),
            P("tp", ("dp", "ctx")),
            P(("dp", "ctx"), None, "tp"),
            P(("dp", "ctx"), None),
            P(("dp", "ctx"), "tp"),
            P(None, "tp"),
            P("tp"),
            P(),
            P(),
            P("tp"),
            P("tp"),
            P("tp"),
            P("tp", ("dp", "ctx")),
            P(),
            P(("dp", "ctx"), None, "tp"),
            P("tp", ("dp", "ctx")),
        ),
        out_specs=(
            P("dp", "ctx", None),
            P(),
            P("dp", "ctx", None),
            P(),
            P(("dp", "ctx"), "tp"),
            P(("dp", "ctx"), None, "tp"),
            P("tp", ("dp", "ctx")),
            P(("dp", "ctx"), None, "tp"),
            P(("dp", "ctx"), None),
            P(("dp", "ctx"), "tp"),
            P(None, "tp"),
            P("tp"),
            P(),
            P(),
            P("tp"),
            P("tp"),
            P("tp"),
            P("tp", ("dp", "ctx")),
            P(),
            P(("dp", "ctx"), None, "tp"),
            P("tp", ("dp", "ctx")),
        ),
        check_vma=False,
    )
```

```python
import functools

import jax
import jax.numpy as jnp
from jax import lax
from jax.experimental import pallas as pl
from jax.experimental.pallas import tpu as pltpu
from jax.sharding import PartitionSpec as P

HEAD_SIZE = 64
MP = 64
NS = 128
KC = 4
CBLK = 128
VMEM_BYTES = 56 * 1024 * 1024

low = jnp.bfloat16
f32 = jnp.float32
highest = lax.Precision.HIGHEST
NEG = -1e30
eps_norm = 1e-05
rope_base = 100000000000.0


def vmem_params():
    return pltpu.CompilerParams(
        dimension_semantics=("arbitrary",), vmem_limit_bytes=VMEM_BYTES
    )


def mm(left, right):
    return jnp.dot(left, right, preferred_element_type=f32)


def mm_nt(left, right):
    return lax.dot_general(left, right, (((1,), (1,)), ((), ())), preferred_element_type=f32)


def mm_tn(left, right):
    return lax.dot_general(left, right, (((0,), (0,)), ((), ())), preferred_element_type=f32)


def iota(shape, axis):
    return lax.broadcasted_iota(jnp.int32, shape, axis)


def sigmoid(v):
    return 1.0 / (1.0 + jnp.exp(-v))


def softplus(v):
    return jnp.maximum(v, 0.0) + jnp.log1p(jnp.exp(-jnp.abs(v)))


def silu_grad(v, sig):
    return sig * (1.0 + v * (1.0 - sig))


def halves(v):
    high = v.astype(low)
    return high, (v - high.astype(f32)).astype(low)


def head_map(channels):
    shape = (128, channels)
    return jnp.where(iota(shape, 1) // MP == iota(shape, 0), 1.0, 0.0).astype(low)


def expand(per_head, spread):
    high, rest = halves(per_head)
    return mm(high, spread) + mm(rest, spread)


def collect(per_channel, spread):
    high, rest = halves(per_channel)
    return mm_nt(high, spread) + mm_nt(rest, spread)


def rotate(u, cosine, sine):
    first = (iota(u.shape, 1) // 32) % 2 == 0
    return u * cosine + jnp.where(first, pltpu.roll(u, 96, 1), pltpu.roll(u, 32, 1)) * sine


def prep_body(q_ref, kv_ref, cos_ref, sin_ref, q_out, kv_out):
    cosine, sine = cos_ref[...], sin_ref[...]
    scale = HEAD_SIZE ** (-0.5)
    for j in range(q_ref.shape[1] // 128):
        cols = slice(128 * j, 128 * j + 128)
        q_out[:, cols] = rotate(q_ref[:, cols], cosine, sine).astype(low) * jnp.asarray(scale, low)
    kv = kv_ref[...]
    keep = iota(kv.shape, 1) < HEAD_SIZE
    kv_out[...] = jnp.where(keep, rotate(kv, cosine, sine), kv).astype(low)


def attend_body(at_ref, q_ref, *refs, hops):
    kv_refs, (o_ref, lse_ref) = refs[:hops], refs[hops:]
    at = at_ref[0]
    tokens = q_ref.shape[0]
    lane = iota((tokens, 128), 1)
    lo = lane < HEAD_SIZE
    causal = iota((tokens, tokens), 0) >= iota((tokens, tokens), 1)
    lse_all = jnp.zeros((tokens, 128), f32)
    for j in range(q_ref.shape[1] // 128):
        pair = q_ref[:, 128 * j : 128 * j + 128].astype(f32)
        sides = []
        for side in range(2):
            query = pair if side == 0 else pltpu.roll(pair, HEAD_SIZE, 1)
            query = jnp.where(lo, query, 0.0).astype(low)
            scores = []
            for d in range(hops):
                score = mm_nt(query, kv_refs[d][...])
                scores.append(
                    jnp.where(causal if d == 0 else at >= d, score, NEG)
                )
            top = functools.reduce(
                jnp.maximum, [jnp.max(s, -1, keepdims=True) for s in scores]
            )
            total, mixed = 0.0, 0.0
            for d in range(hops):
                expo = jnp.exp(scores[d] - top)
                total = total + jnp.sum(expo, -1, keepdims=True)
                mixed = mixed + mm(expo.astype(low), kv_refs[d][...])
            sides.append(mixed * (1.0 / total))
            lse_all = jnp.where(lane == 2 * j + side, top + jnp.log(total), lse_all)
        o_ref[:, 128 * j : 128 * j + 128] = jnp.where(
            lo, pltpu.roll(sides[0], HEAD_SIZE, 1), sides[1]
        ).astype(low)
    lse_ref[...] = lse_all


def attend_back_body(at_ref, q_ref, go_ref, o_ref, lse_ref, cos_ref, sin_ref, *refs, hops):
    kv_refs, (gq_ref,), gkv_refs = refs[:hops], refs[hops : hops + 1], refs[hops + 1 :]
    at = at_ref[0]
    tokens = q_ref.shape[0]
    lane = iota((tokens, 128), 1)
    lo = lane < HEAD_SIZE
    causal = iota((tokens, tokens), 0) >= iota((tokens, tokens), 1)
    cosine, sine = cos_ref[...], sin_ref[...]
    lse_all = lse_ref[...]
    scale = HEAD_SIZE ** (-0.5)
    gkv = [jnp.zeros((tokens, 128), f32) for _ in range(hops)]
    for j in range(q_ref.shape[1] // 128):
        cols = slice(128 * j, 128 * j + 128)
        pair = q_ref[:, cols].astype(f32)
        go_pair = go_ref[:, cols].astype(low).astype(f32)
        weighed = go_pair * o_ref[:, cols].astype(f32)
        sides = []
        for side in range(2):
            query = pair if side == 0 else pltpu.roll(pair, HEAD_SIZE, 1)
            query = jnp.where(lo, query, 0.0).astype(low)
            grad = pltpu.roll(go_pair, HEAD_SIZE, 1) if side == 0 else go_pair
            grad = jnp.where(lo, 0.0, grad).astype(low)
            centre = jnp.sum(jnp.where(lo == (side == 0), weighed, 0.0), -1, keepdims=True)
            lse = jnp.sum(jnp.where(lane == 2 * j + side, lse_all, 0.0), -1, keepdims=True)
            gq = 0.0
            for d in range(hops):
                kv = kv_refs[d][...]
                score = mm_nt(query, kv)
                prob = jnp.exp(jnp.where(causal if d == 0 else at >= d, score, NEG) - lse)
                gprob = mm_nt(grad, kv)
                gscore = (prob * (gprob - centre)).astype(low)
                gq = gq + mm(gscore, kv)
                gkv[d] = gkv[d] + mm_tn(gscore, query) + mm_tn(prob.astype(low), grad)
            sides.append(gq * scale)
        joined = jnp.where(lo, sides[0], pltpu.roll(sides[1], HEAD_SIZE, 1))
        gq_ref[:, cols] = rotate(joined, cosine, -sine).astype(low)
    for d in range(hops):
        gkv_refs[d][...] = gkv[d].astype(low)


def keyval_sum_body(cos_ref, sin_ref, *refs):
    parts, (out_ref,) = refs[:-1], refs[-1:]
    total = parts[0][...].astype(f32)
    for part in parts[1:]:
        total = total + part[...].astype(f32)
    keep = iota(total.shape, 1) < HEAD_SIZE
    rotated = rotate(total, cos_ref[...], -sin_ref[...])
    out_ref[...] = jnp.where(keep, rotated, total).astype(low)


def decay_pair(logs, logs_t, first, keep):
    both = []
    for head in (first, first + 1):
        gap = logs[:, head : head + 1] - logs_t[head : head + 1, :]
        both.append(jnp.exp(jnp.where(keep, gap, NEG)))
    return both


def step_terms(step_ref, rows, heads_ref, heads):
    raw = step_ref[rows, :] + heads_ref[0:1, :]
    live = iota(raw.shape, 1) < heads
    steps = jnp.where(live, softplus(raw), 0.0)
    return jnp.where(live, raw, 0.0), steps


def lower_triangle(size):
    return iota((size, size), 0) >= iota((size, size), 1)


def scan_body(
    x_ref, bc_ref, step_ref, xt_ref, bct_ref, taps_ref, taps_bc_ref, heads_ref,
    v_ref, vbc_ref, y_ref, logs_ref, states_ref, send_ref,
    xe, bce, *, heads,
):
    tokens, channels = x_ref.shape
    xe[0:8, :] = xt_ref[...]
    xe[8:, :] = x_ref[...]
    bce[0:8, :] = bct_ref[...]
    bce[8:, :] = bc_ref[...]
    spread = head_map(channels)
    keep = lower_triangle(CBLK)
    triangle = jnp.where(keep, 1.0, 0.0)
    lo = iota((CBLK, 128), 1) < MP
    rate = heads_ref[1:2, :]
    state = None
    carry = jnp.zeros((1, 128), f32)
    total_decay = None
    for c in range(tokens // CBLK):
        rows = slice(CBLK * c, CBLK * c + CBLK)

        def conv(ext, taps):
            start = CBLK * c + 8 - (KC - 1)
            total = taps[KC : KC + 1, :] + taps[0:1, :] * ext[start : start + CBLK, :]
            for k in range(1, KC):
                total = total + taps[k : k + 1, :] * ext[start + k : start + k + CBLK, :]
            return total

        v = conv(xe, taps_ref)
        v_ref[rows, :] = v
        xs = v * sigmoid(v)
        vbc = conv(bce, taps_bc_ref)
        vbc_ref[rows, :] = vbc
        bc = (vbc * sigmoid(vbc)).astype(low)
        entry, read = bc[:, :NS], bc[:, NS:]
        _, steps = step_terms(step_ref, rows, heads_ref, heads)
        logs = jnp.dot(triangle, -steps * rate, precision=highest, preferred_element_type=f32)
        logs_t = logs.T
        total = logs[CBLK - 1 : CBLK, :]
        logs_ref[rows, :] = logs + carry
        carry = carry + total
        decays = expand(jnp.exp(logs), spread)
        steps_wide = expand(steps, spread)
        tails_wide = expand(jnp.exp(total - logs) * steps, spread)
        weighted = (xs * steps_wide).astype(low)
        inner = mm_nt(read, entry)
        if state is not None:
            incoming = decays * mm(read, state.astype(low))
        for j in range(channels // 128):
            cols = slice(128 * j, 128 * j + 128)
            left, right = decay_pair(logs, logs_t, 2 * j, keep)
            stacked = jnp.concatenate([(inner * left).astype(low), (inner * right).astype(low)], 0)
            result = mm(stacked, weighted[:, cols])
            out = jnp.where(lo, result[:CBLK], result[CBLK:])
            if state is not None:
                out = out + incoming[:, cols]
            y_ref[rows, cols] = out
        added = mm_tn(entry, (xs * tails_wide).astype(low))
        last = decays[CBLK - 1 : CBLK, :]
        state = added if state is None else last * state + added
        total_decay = last if total_decay is None else total_decay * last
        states_ref[NS * c : NS * c + NS, :] = state
    send_ref[0:NS, :] = state.astype(low)
    send_ref[NS:, :] = jnp.broadcast_to(total_decay, (send_ref.shape[0] - NS, channels)).astype(low)


def by_chip(refs):
    return [refs[:1], *(refs[i : i + 2] for i in range(1, len(refs), 2))]


def chained(groups):
    state = None
    for group in reversed(groups):
        own = sum(ref[0:NS, :].astype(f32) for ref in group)
        if state is None:
            state = own
        else:
            state = own + sum(ref[NS : NS + 1, :].astype(f32) for ref in group) * state
    return state


def gate_body(z_ref, y_ref, v_ref, vbc_ref, logs_ref, heads_ref, *refs):
    earlier, (gated_ref, y_out, carried_ref) = refs[:-3], refs[-3:]
    tokens, channels = y_ref.shape
    spread = head_map(channels)
    skip = expand(heads_ref[...], spread)[2:3, :]
    carried = chained(by_chip(earlier))
    carried_ref[...] = carried
    carried_low = carried.astype(low)
    for c in range(tokens // CBLK):
        rows = slice(CBLK * c, CBLK * c + CBLK)
        vc = vbc_ref[rows, NS:]
        read = (vc * sigmoid(vc)).astype(low)
        y = y_ref[rows, :] + expand(jnp.exp(logs_ref[rows, :]), spread) * mm(read, carried_low)
        y_out[rows, :] = y
        v = v_ref[rows, :]
        z = z_ref[rows, :]
        gated_ref[rows, :] = ((y + skip * (v * sigmoid(v))) * (z * sigmoid(z))).astype(low)


def gate_back_body(
    g_ref, z_ref, y_ref, v_ref, vbc_ref, logs_ref, heads_ref, sent_ref,
    dy_ref, dz_ref, dskip_ref, send_ref,
):
    tokens, channels = y_ref.shape
    spread = head_map(channels)
    skip = expand(heads_ref[...], spread)[2:3, :]
    state, dskip = 0.0, 0.0
    for c in range(tokens // CBLK):
        rows = slice(CBLK * c, CBLK * c + CBLK)
        vc = vbc_ref[rows, NS:]
        read = (vc * sigmoid(vc)).astype(low)
        v = v_ref[rows, :]
        xs = v * sigmoid(v)
        z = z_ref[rows, :]
        sig = sigmoid(z)
        grad = g_ref[rows, :].astype(f32)
        dy = grad * (z * sig)
        dz_ref[rows, :] = (grad * (y_ref[rows, :] + skip * xs) * silu_grad(z, sig)).astype(low)
        dy_ref[rows, :] = dy
        dskip = dskip + jnp.sum(dy * xs, 0, keepdims=True)
        faded = (dy * expand(jnp.exp(logs_ref[rows, :]), spread)).astype(low)
        state = state + mm_tn(read, faded)
    send_ref[0:NS, :] = state.astype(low)
    send_ref[NS:, :] = sent_ref[NS:, :]
    dskip_ref[...] = jnp.broadcast_to(dskip, dskip_ref.shape)


def scan_back_body(
    dy_ref, y_ref, v_ref, vbc_ref, x_ref, bc_ref, step_ref, xt_ref, bct_ref,
    taps_ref, taps_bc_ref, heads_ref, logs_ref, states_ref, carried_ref, *refs, heads,
):
    later, refs = refs[:-10], refs[-10:]
    dx_ref, dbc_ref, dstep_ref, edge_ref, head_ref, gx_ref, gbc_ref, gh_ref, dve, dbce = refs
    tokens, channels = y_ref.shape
    chunks = tokens // CBLK
    spread = head_map(channels)
    keep = lower_triangle(CBLK)
    triangle = jnp.where(keep, 1.0, 0.0)
    lo = iota((CBLK, 128), 1) < MP
    rate = heads_ref[1:2, :]
    skip = expand(heads_ref[...], spread)[2:3, :]
    dstate = chained(by_chip(later))
    dve[0:8, :] = jnp.zeros((8, channels), f32)
    dve[8 + tokens :, :] = jnp.zeros((8, channels), f32)
    dbce[0:8, :] = jnp.zeros((8, 2 * NS), f32)
    dbce[8 + tokens :, :] = jnp.zeros((8, 2 * NS), f32)
    dbias, ddecay = 0.0, 0.0
    for c in reversed(range(chunks)):
        rows = slice(CBLK * c, CBLK * c + CBLK)
        v = v_ref[rows, :]
        sig = sigmoid(v)
        xs = v * sig
        vbc = vbc_ref[rows, :]
        sig_bc = sigmoid(vbc)
        bc = (vbc * sig_bc).astype(low)
        entry, read = bc[:, :NS], bc[:, NS:]
        raw, steps = step_terms(step_ref, rows, heads_ref, heads)
        logs = jnp.dot(triangle, -steps * rate, precision=highest, preferred_element_type=f32)
        logs_t = logs.T
        total = logs[CBLK - 1 : CBLK, :]
        decays = expand(jnp.exp(logs), spread)
        steps_wide = expand(steps, spread)
        tails_wide = expand(jnp.exp(total - logs), spread)
        last = decays[CBLK - 1 : CBLK, :]
        if c == 0:
            state = carried_ref[...]
        else:
            before = expand(jnp.exp(logs_ref[CBLK * c - 8 : CBLK * c, :]), spread)[7:8, :]
            state = states_ref[NS * (c - 1) : NS * c, :] + before * carried_ref[...]
        dy = dy_ref[rows, :]
        dy_low = dy.astype(low)
        w = xs * steps_wide
        w_low = w.astype(low)
        inner = mm_nt(read, entry)
        state_low = state.astype(low)
        dstate_low = dstate.astype(low)
        dw_later = tails_wide * mm(entry, dstate_low)
        faded = (dy * decays).astype(low)
        dread = mm_nt(faded, state_low)
        dentry = mm_nt((w * tails_wide).astype(low), dstate_low)
        dinner = 0.0
        pieces = []
        for j in range(channels // 128):
            cols = slice(128 * j, 128 * j + 128)
            left, right = decay_pair(logs, logs_t, 2 * j, keep)
            dy_pair, w_pair = dy_low[:, cols], w_low[:, cols]
            weights = jnp.concatenate([(inner * left).astype(low), (inner * right).astype(low)], 1)
            result = mm_tn(weights, dy_pair)
            pieces.append(jnp.where(lo, result[:CBLK], result[CBLK:]) + dw_later[:, cols])
            zero = jnp.zeros_like(dy_pair)
            parted = jnp.concatenate([jnp.where(lo, dy_pair, zero), jnp.where(lo, zero, dy_pair)], 0)
            dweights = mm_nt(parted, w_pair)
            dinner = dinner + dweights[:CBLK] * left + dweights[CBLK:] * right
        dw = jnp.concatenate(pieces, 1)
        dinner_low = dinner.astype(low)
        dread = dread + mm(dinner_low, entry)
        dentry = dentry + mm_tn(dinner_low, read)
        dlogs = collect(dy * y_ref[rows, :] - w * dw, spread)
        dtotal = jnp.sum(w * dw_later, 0, keepdims=True) + last * jnp.sum(
            dstate * state, 0, keepdims=True
        )
        dtotal = collect(jnp.broadcast_to(dtotal, (8, channels)), spread)[0:1, :]
        dfall = (
            lax.dot_general(
                triangle, dlogs, (((0,), (0,)), ((), ())),
                precision=highest, preferred_element_type=f32,
            )
            + dtotal
        )
        dsteps = collect(xs * dw, spread) - rate * dfall
        ddecay = ddecay - rate * jnp.sum(steps * dfall, 0, keepdims=True)
        live = iota(raw.shape, 1) < heads
        draw = jnp.where(live, dsteps * sigmoid(raw), 0.0)
        dbias = dbias + jnp.sum(draw, 0, keepdims=True)
        dstep_ref[rows, :] = draw.astype(low)
        dve[8 + CBLK * c : 8 + CBLK * c + CBLK, :] = (steps_wide * dw + skip * dy) * silu_grad(v, sig)
        dbce[8 + CBLK * c : 8 + CBLK * c + CBLK, :] = jnp.concatenate(
            [dentry, dread], 1
        ) * silu_grad(vbc, sig_bc)
        dstate = last * dstate + mm_tn(read, faded)
    gh_ref[0:1, :] = dbias
    gh_ref[1:2, :] = ddecay
    gh_ref[2:, :] = jnp.zeros((gh_ref.shape[0] - 2, 128), f32)

    def conv_back(ext, taps, out_ref, cols, grads_ref, pre_ref, tail_ref):
        def spread_rows(start, count):
            total = taps[0:1, :] * ext[start + KC - 1 : start + KC - 1 + count, :]
            for k in range(1, KC):
                at = start + KC - 1 - k
                total = total + taps[k : k + 1, :] * ext[at : at + count, :]
            return total

        head_ref[0:8, cols] = jnp.zeros((8, ext.shape[1]), f32)
        head_ref[8:16, cols] = spread_rows(0, 8)
        grads = [0.0] * (KC + 1)
        for c in range(chunks):
            at = CBLK * c
            dpre = spread_rows(8 + at, CBLK)
            out_ref[at : at + CBLK, :] = dpre.astype(low)
            if c == chunks - 1:
                edge_ref[:, cols] = dpre[CBLK - 16 :, :]
        for k in range(KC):
            shift = KC - 1 - k
            main = jnp.sum(pre_ref[...] * ext[8 + shift : 8 + shift + tokens, :], 0, keepdims=True)
            edge = jnp.sum(tail_ref[...] * ext[shift : shift + 8, :], 0, keepdims=True)
            grads[k] = main + edge
        grads[KC] = jnp.sum(ext[8 : 8 + tokens, :], 0, keepdims=True)
        for k in range(KC + 1):
            grads_ref[k : k + 1, :] = grads[k]
        grads_ref[KC + 1 :, :] = jnp.zeros((grads_ref.shape[0] - KC - 1, ext.shape[1]), f32)

    conv_back(dve, taps_ref, dx_ref, slice(0, channels), gx_ref, x_ref, xt_ref)
    bc_cols = slice(channels, channels + 2 * NS)
    conv_back(dbce, taps_bc_ref, dbc_ref, bc_cols, gbc_ref, bc_ref, bct_ref)


def block(height, width, col=0, first=0):
    return pl.BlockSpec((height, width), lambda s: (first + s, col))


def whole(shape):
    return pl.BlockSpec(shape, lambda s: (0, 0))


def shaped(rows, cols, dtype):
    return jax.ShapeDtypeStruct((rows, cols), dtype)


def run(body, seqs, inputs, outputs, scratch=(), at=None, flops=0, shared=()):
    arrays = [a for a, _ in inputs]
    specs = [s for _, s in inputs]
    if at is not None:
        arrays = [at] + arrays
        specs = [pl.BlockSpec(memory_space=pltpu.SMEM)] + specs
    moved = sum(a.size * a.dtype.itemsize for a in arrays)
    out_specs = [block(r, c) for r, c, _ in outputs]
    out_shape = [shaped(seqs * r, c, d) for r, c, d in outputs]
    aliases, count = {}, len(arrays)
    for r, c, d, total, first, previous in shared:
        if previous is not None:
            aliases[len(arrays)] = len(out_shape)
            arrays.append(previous)
            specs.append(pl.BlockSpec(memory_space=pl.ANY))
        out_specs.append(block(r, c, 0, first))
        out_shape.append(shaped(total * r, c, d))
    kept = len(aliases)

    def inner(*refs):
        body(*refs[:count], *refs[count + kept :])

    return pl.pallas_call(
        inner,
        grid=(seqs,),
        in_specs=specs,
        out_specs=out_specs,
        out_shape=out_shape,
        scratch_shapes=list(scratch),
        input_output_aliases=aliases,
        compiler_params=vmem_params(),
        cost_estimate=pl.CostEstimate(flops=flops, bytes_accessed=moved, transcendentals=0),
    )(*arrays)


def prep(pre, cosine, sine, seqs, tokens, q_at, q_cols, kv_at):
    return run(
        prep_body,
        seqs,
        [
            (pre, block(tokens, q_cols, q_at // q_cols)),
            (pre, block(tokens, 128, kv_at // 128)),
            (cosine, block(tokens, 128)),
            (sine, block(tokens, 128)),
        ],
        [(tokens, q_cols, low), (tokens, 128, low)],
    )


def attend(queries, keyvals, at, seqs, tokens):
    hops, cols = len(keyvals), queries.shape[1]
    work = 4 * seqs * tokens * tokens * hops * (cols // HEAD_SIZE) * 256
    return run(
        functools.partial(attend_body, hops=hops),
        seqs,
        [(queries, block(tokens, cols))] + [(kv, block(tokens, 128)) for kv in keyvals],
        [(tokens, cols, low), (tokens, 128, f32)],
        at=at,
        flops=work,
    )


def attend_back(
    queries, keyvals, grads, grad_at, outs, lse, cosine, sine, at, first, seqs, tokens, previous
):
    hops, cols = len(keyvals), queries.shape[1]
    work = 10 * tokens * tokens * hops * (cols // HEAD_SIZE) * 256
    return run(
        functools.partial(attend_back_body, hops=hops),
        1,
        [
            (queries, block(tokens, cols, 0, first)),
            (grads, block(tokens, cols, grad_at // cols)),
            (outs, block(tokens, cols, 0, first)),
            (lse, block(tokens, 128, 0, first)),
            (cosine, block(tokens, 128, 0, first)),
            (sine, block(tokens, 128, 0, first)),
        ]
        + [(kv, block(tokens, 128, 0, first)) for kv in keyvals],
        [(tokens, cols, low)],
        at=at,
        flops=work,
        shared=[(tokens, 128, low, seqs, first, p) for p in previous],
    )


def keyval_sum(parts, cosine, sine, seqs, tokens):
    return run(
        keyval_sum_body,
        seqs,
        [(a, block(tokens, 128)) for a in (cosine, sine, *parts)],
        [(tokens, 128, low)],
    )[0]


SENT = NS + 16


class Columns:
    def __init__(self, channels, q_cols):
        self.channels = channels
        self.x, self.z, self.q = 0, channels, 2 * channels
        self.bc = self.q + q_cols
        self.kv = self.bc + 2 * NS
        self.step = self.kv + 128
        self.total = self.step + 128

    def x_block(self, tokens, first=0):
        return block(tokens, self.channels, 0, first)

    def z_block(self, tokens, first=0):
        return block(tokens, self.channels, 1, first)

    def bc_block(self, tokens, first=0):
        return block(tokens, 2 * NS, self.bc // (2 * NS), first)

    def step_block(self, tokens, first=0):
        return block(tokens, 128, self.step // 128, first)


def scan(pre, cols, tails, taps, taps_bc, per_head, seqs, tokens, heads):
    channels = cols.channels
    return run(
        functools.partial(scan_body, heads=heads),
        seqs,
        [
            (pre, cols.x_block(tokens)),
            (pre, cols.bc_block(tokens)),
            (pre, cols.step_block(tokens)),
            (tails, block(8, channels)),
            (tails, block(8, 2 * NS, channels // (2 * NS))),
            (taps, whole(taps.shape)),
            (taps_bc, whole(taps_bc.shape)),
            (per_head, whole(per_head.shape)),
        ],
        [
            (tokens, channels, f32),
            (tokens, 2 * NS, f32),
            (tokens, channels, f32),
            (tokens, 128, f32),
            (tokens // CBLK * NS, channels, f32),
            (SENT, channels, low),
        ],
        scratch=[pltpu.VMEM((tokens + 8, channels), f32), pltpu.VMEM((tokens + 8, 2 * NS), f32)],
        flops=8 * seqs * tokens * CBLK * channels,
    )


def gate(pre, cols, y, v, vbc, logs, per_head, earlier, first, tokens):
    channels = cols.channels
    return run(
        gate_body,
        1,
        [
            (pre, cols.z_block(tokens, first)),
            (y, block(tokens, channels, 0, first)),
            (v, block(tokens, channels, 0, first)),
            (vbc, block(tokens, 2 * NS, 0, first)),
            (logs, block(tokens, 128, 0, first)),
            (per_head, whole(per_head.shape)),
        ]
        + [(a, block(SENT, channels, 0, first)) for a in earlier],
        [(tokens, channels, low), (tokens, channels, f32), (NS, channels, f32)],
        flops=4 * tokens * CBLK * channels,
    )


def gate_back(grads, pre, cols, y, v, vbc, logs, per_head, sent, first, seqs, tokens, previous):
    channels = cols.channels
    return run(
        gate_back_body,
        1,
        [
            (grads, block(tokens, channels)),
            (pre, cols.z_block(tokens, first)),
            (y, block(tokens, channels)),
            (v, block(tokens, channels, 0, first)),
            (vbc, block(tokens, 2 * NS, 0, first)),
            (logs, block(tokens, 128, 0, first)),
            (per_head, whole(per_head.shape)),
            (sent, block(SENT, channels, 0, first)),
        ],
        [
            (tokens, channels, f32),
            (tokens, channels, low),
            (8, channels, f32),
        ],
        flops=4 * tokens * CBLK * channels,
        shared=[(SENT, channels, low, seqs, first, previous)],
    )


def scan_back(
    dy, y, v, vbc, pre, cols, tails, taps, taps_bc, per_head, logs, states, carried, later,
    first, tokens, heads,
):
    channels = cols.channels
    return run(
        functools.partial(scan_back_body, heads=heads),
        1,
        [
            (dy, block(tokens, channels)),
            (y, block(tokens, channels)),
            (v, block(tokens, channels, 0, first)),
            (vbc, block(tokens, 2 * NS, 0, first)),
            (pre, cols.x_block(tokens, first)),
            (pre, cols.bc_block(tokens, first)),
            (pre, cols.step_block(tokens, first)),
            (tails, block(8, channels, 0, first)),
            (tails, block(8, 2 * NS, channels // (2 * NS), first)),
            (taps, whole(taps.shape)),
            (taps_bc, whole(taps_bc.shape)),
            (per_head, whole(per_head.shape)),
            (logs, block(tokens, 128, 0, first)),
            (states, block(tokens // CBLK * NS, channels, 0, first)),
            (carried, block(NS, channels)),
        ]
        + [(a, block(SENT, channels, 0, first)) for a in later],
        [
            (tokens, channels, low),
            (tokens, 2 * NS, low),
            (tokens, 128, low),
            (16, channels + 2 * NS, f32),
            (16, channels + 2 * NS, f32),
            (8, channels, f32),
            (8, 2 * NS, f32),
            (8, 128, f32),
        ],
        scratch=[
            pltpu.VMEM((tokens + 16, channels), f32),
            pltpu.VMEM((tokens + 16, 2 * NS), f32),
        ],
        flops=30 * tokens * CBLK * channels,
    )


TILE = 256


def wide(rows, col=0, width=None):
    return pl.BlockSpec((TILE, rows if width is None else width), lambda t: (t, col))


def tall(array):
    return pl.BlockSpec((array.shape[0], TILE), lambda t: (0, t))


def tiled(body, width, arrays, specs, outputs, scratch, flops):
    return pl.pallas_call(
        body,
        grid=(width // TILE,),
        in_specs=specs,
        out_specs=[spec for _, _, spec in outputs],
        out_shape=[jax.ShapeDtypeStruct(shape, dtype) for shape, dtype, _ in outputs],
        scratch_shapes=scratch,
        compiler_params=vmem_params(),
        cost_estimate=pl.CostEstimate(
            flops=flops,
            bytes_accessed=sum(a.size * a.dtype.itemsize for a in arrays),
            transcendentals=0,
        ),
    )(*arrays)


def early_grads_body(left_ref, wz_ref, wq_ref, *refs, seqs):
    dz, dq, grads, gated = (refs[seqs * i : seqs * i + seqs] for i in range(4))
    attended, out_ref, part_ref, held = refs[-4:]
    tokens = held.shape[0] // seqs
    z_cols = dz[0].shape[1]

    @pl.when(pl.program_id(0) == 0)
    def _():
        for s in range(seqs):
            held[tokens * s : tokens * (s + 1), :z_cols] = dz[s][...]
            held[tokens * s : tokens * (s + 1), z_cols:] = dq[s][...]

    split = held.shape[1]
    out_ref[:, :split] = mm(left_ref[...], held[...]).astype(low)
    middle = split + z_cols
    from_gated, from_attended = 0.0, 0.0
    for s in range(seqs):
        grad = grads[s][...]
        from_gated = from_gated + mm_tn(grad, gated[s][...])
        from_attended = from_attended + mm_tn(grad, attended[tokens * s : tokens * (s + 1), :])
    out_ref[:, split:middle] = from_gated.astype(low)
    out_ref[:, middle:] = from_attended.astype(low)
    part_ref[...] = mm_nt(held[:, :z_cols], wz_ref[...]) + mm_nt(held[:, z_cols:], wq_ref[...])


def early_grads(left, weight, cols, dz, dq, grads, gated, attended):
    width, rows = left.shape
    own = cols.bc - cols.z
    out_cols = own + gated[0].shape[1] + attended.shape[1]
    q_cols = cols.bc - cols.q
    return tiled(
        functools.partial(early_grads_body, seqs=len(dz)),
        width,
        [left, weight, weight, *dz, *dq, *grads, *gated, attended],
        [
            wide(rows),
            wide(cols.channels, cols.z // cols.channels),
            wide(q_cols, cols.q // q_cols),
        ]
        + [whole(a.shape) for a in (*dz, *dq)]
        + [tall(a) for a in grads]
        + [whole(a.shape) for a in (*gated, attended)],
        [
            ((width, out_cols), low, wide(out_cols)),
            ((rows, width), f32, pl.BlockSpec((rows, TILE), lambda t: (0, t))),
        ],
        [pltpu.VMEM((rows, own), low)],
        2 * rows * width * (own + out_cols),
    )


def late_grads_body(left_ref, wx_ref, wbc_ref, wrest_ref, start_ref, keyval_ref, head_ref, *refs, seqs):
    dx, dbc, dstep, edge = (refs[seqs * i : seqs * i + seqs] for i in range(4))
    out_ref, part_ref, held = refs[-3:]
    tokens = held.shape[0] // seqs
    channels = dx[0].shape[1]
    conv_cols = channels + dbc[0].shape[1]

    @pl.when(pl.program_id(0) == 0)
    def _():
        for s in range(seqs):
            rows = slice(tokens * s, tokens * (s + 1))
            held[rows, :channels] = dx[s][...]
            held[rows, channels:conv_cols] = dbc[s][...]
            held[rows, conv_cols : conv_cols + 128] = keyval_ref[rows, :]
            held[rows, conv_cols + 128 :] = dstep[s][...]
            held[tokens * (s + 1) - 16 : tokens * (s + 1), :conv_cols] = (
                edge[s][...] + head_ref[16 * s : 16 * s + 16, :]
            ).astype(low)

    out_ref[...] = mm(left_ref[...], held[...]).astype(low)
    part_ref[...] = (
        start_ref[...]
        + mm_nt(held[:, :channels], wx_ref[...])
        + mm_nt(held[:, channels:conv_cols], wbc_ref[...])
        + mm_nt(held[:, conv_cols:], wrest_ref[...])
    ).astype(low)


def late_grads(left, weight, cols, start, keyval, head, dx, dbc, dstep, edge):
    width, rows = left.shape
    own = cols.total - (cols.bc - cols.z)
    bc_cols, rest = cols.kv - cols.bc, cols.total - cols.kv
    return tiled(
        functools.partial(late_grads_body, seqs=len(dx)),
        width,
        [left, weight, weight, weight, start, keyval, head, *dx, *dbc, *dstep, *edge],
        [
            wide(rows),
            wide(cols.channels, 0),
            wide(bc_cols, cols.bc // bc_cols),
            wide(rest, cols.kv // rest),
            tall(start),
            whole(keyval.shape),
            whole(head.shape),
        ]
        + [whole(a.shape) for a in (*dx, *dbc, *dstep, *edge)],
        [
            ((width, own), low, wide(own)),
            ((rows, width), low, pl.BlockSpec((rows, TILE), lambda t: (0, t))),
        ],
        [pltpu.VMEM((rows, own), low)],
        4 * rows * width * own,
    )


def passed_along(array, axis, distance):
    devices = range(lax.axis_size(axis))
    route = [(i - distance, i) for i in devices if i - distance in devices]
    return lax.ppermute(array, axis, route)


def after(array, *others):
    return lax.optimization_barrier((array, *others))[0]


def swapped(array, axis, distance):
    devices = range(lax.axis_size(axis))
    return lax.ppermute(array, axis, [(i, i ^ distance) for i in devices])


def offer(part):
    mine = part.astype(low)
    return mine, swapped(mine, "tp", 1)


def summed_pair(mine, other):
    return mine.astype(f32) + other.astype(f32)


def sum_over(array, axes):
    for axis in axes:
        distance = 1
        while distance < lax.axis_size(axis):
            array = array + swapped(array, axis, distance)
            distance *= 2
    return array


def place(axis, distance=0):
    return lax.axis_index(axis).astype(jnp.uint32) ^ jnp.uint32(distance)


def place(axis, distance=0):
    return lax.axis_index(axis).astype(jnp.uint32) ^ jnp.uint32(distance)


def picked(array, at, dim):
    return lax.dynamic_index_in_dim(array, at, dim, False)


def states_beside(sent, seqs, side):
    chips = range(lax.axis_size("ctx") // 2)
    near, far = (1, 0) if side < 0 else (0, 1)
    got = lax.ppermute(sent, "ctx", [(2 * k + far, 2 * k + near) for k in chips])
    own, got = (a.reshape(seqs, SENT, -1).astype(f32) for a in (sent, got))
    is_decay = lax.broadcasted_iota(jnp.int32, (1, SENT, 1), 1) >= NS
    got = jnp.where((lax.axis_index("ctx") & 1) == near, got, jnp.where(is_decay, 1.0, 0.0))
    both = jnp.where(is_decay, own * got, own + own[:, NS : NS + 1] * got)
    first, both = (a.astype(low).reshape(sent.shape) for a in (got, both))
    beside = [first]
    for d in chips[1:]:
        for core in range(2):
            route = [(2 * k + near, 2 * (k - side * d) + core) for k in chips if k - side * d in chips]
            beside.append(lax.ppermute(both, "ctx", route))
    return beside


def core_sum(terms):
    dp, ctx = lax.axis_size("dp"), lax.axis_size("ctx")
    rows, cols = terms.shape[0] // (dp * ctx), terms.shape[1]
    one = jnp.uint32(1)
    pieces = terms.reshape(dp, ctx // 2, 2, rows, cols)
    got = swapped(picked(pieces, place("ctx", 1) & one, 2), "ctx", 1)
    return (picked(pieces, place("ctx") & one, 2).astype(f32) + got.astype(f32)).astype(low)


def spread(held, axis, dim, shift):
    own = picked(held, place(axis) >> jnp.uint32(shift), dim)
    sends = [
        picked(held, place(axis, d << shift) >> jnp.uint32(shift), dim)
        for d in range(1, held.shape[dim])
    ]
    return own, sends, [swapped(a, axis, (d + 1) << shift) for d, a in enumerate(sends)]


def added(own, got):
    total = own.astype(f32)
    for block_in in got:
        total = total + block_in.astype(f32)
    return total


def rms_norm(values, gain):
    return values * lax.rsqrt(jnp.mean(values * values, -1, keepdims=True) + eps_norm) * gain


def angle_tables(positions):
    half = HEAD_SIZE // 2
    freqs = rope_base ** (-2.0 * jnp.arange(half, dtype=f32) / HEAD_SIZE)
    angles = positions.reshape(-1, 1).astype(f32) * freqs
    cosine, sine = jnp.cos(angles), jnp.sin(angles)
    return jnp.tile(cosine, (1, 4)), jnp.concatenate([-sine, sine, -sine, sine], 1)


def per_device(
    hidden_in,
    positions,
    valid_mask,
    teacher,
    cotangent,
    mixer_gain,
    query_weight,
    keyvalue_projection_weight,
    attnout_weight,
    stream_weight,
    state_weight,
    step_weight,
    conv_stream,
    bias_stream,
    conv_state,
    bias_state,
    step_bias,
    decay_log,
    skip_scale,
    mambaout_weight,
    ffn_gain,
    gateup_weight,
    down_weight,
):
    seqs, tokens, width = hidden_in.shape
    owners = ("dp", "ctx")
    rows = query_weight.shape[0]
    q_cols = query_weight.shape[1]
    kv_cols = keyvalue_projection_weight.shape[2]
    channels = stream_weight.shape[2]
    bc_cols = state_weight.shape[1]
    heads = step_weight.shape[1]
    hidden_units = gateup_weight.shape[2]
    step_cols = 128
    hops = lax.axis_size("ctx")
    each = range(seqs)

    tallies = jnp.sum(valid_mask.reshape(seqs * tokens // CBLK, CBLK), -1).astype(low)
    spare = jnp.zeros((rows, step_cols - heads), low)
    spare = spare.at[0, : tallies.shape[0]].set(tallies)
    mixer_shard = jnp.concatenate(
        [
            stream_weight[:, 1],
            stream_weight[:, 0],
            query_weight,
            state_weight,
            keyvalue_projection_weight.reshape(rows, 2 * kv_cols),
            step_weight,
            spare,
            mambaout_weight.T,
            attnout_weight.T,
        ],
        1,
    )
    cols = Columns(channels, q_cols)
    all_cols = cols.total
    mixer_both = lax.all_gather(mixer_shard, owners, axis=0, tiled=True)
    mixer_full, out_full_w = mixer_both[:, :all_cols], mixer_both[:, all_cols:]
    ffn_shard = jnp.concatenate(
        [gateup_weight.reshape(rows, 2 * hidden_units), down_weight.T], 1
    )
    ffn_full = lax.all_gather(ffn_shard, owners, axis=0, tiled=True)
    gateup_full = ffn_full[:, : 2 * hidden_units]
    down_full = ffn_full[:, 2 * hidden_units :]

    counts = mixer_both.reshape(-1, rows, mixer_both.shape[1])
    counts = counts[:, 0, cols.step + heads : cols.step + heads + tallies.shape[0]]
    valid_total = jnp.sum(counts.astype(f32))

    at = lax.axis_index("ctx").astype(jnp.int32).reshape(1)
    cosine, sine = angle_tables(positions)

    def taps_of(taps, bias):
        spare_rows = jnp.zeros((8 - KC - 1, taps.shape[1]), f32)
        return jnp.concatenate([taps, bias[None], spare_rows], 0)

    taps, taps_bc = taps_of(conv_stream, bias_stream), taps_of(conv_state, bias_state)
    per_head = jnp.pad(
        jnp.stack([step_bias, jnp.exp(decay_log), skip_scale]), ((0, 5), (0, 128 - heads))
    )

    hidden = hidden_in.astype(f32)
    normed = rms_norm(hidden, mixer_gain).astype(low).reshape(seqs * tokens, width)
    normed, normed_t = lax.optimization_barrier((normed, normed.T))
    pre = jnp.dot(normed, mixer_full, preferred_element_type=f32)

    def last_rows(array):
        return array.reshape(seqs, tokens, -1)[:, tokens - 8 :].reshape(seqs * 8, -1)

    ends = last_rows(pre)
    ends = jnp.concatenate([ends[:, : cols.z], ends[:, cols.bc : cols.kv]], 1)
    tails = passed_along(ends, "ctx", 1)
    queries, keyval = prep(pre, cosine, sine, seqs, tokens, cols.q, q_cols, cols.kv)
    keyvals = [keyval] + [passed_along(keyval, "ctx", d) for d in range(1, hops)]
    v, vbc, y_own, logs, states, sent = scan(
        after(pre, keyval), cols, tails, taps, taps_bc, per_head, seqs, tokens, heads
    )
    earlier = states_beside(after(sent, *keyvals[1:]), seqs, -1)
    attended, lse = attend(after(queries, earlier[0]), keyvals, at, seqs, tokens)
    gated, y, carried, offers = [], [], [], []
    for s in each:
        here = gate(pre, cols, y_own, v, vbc, logs, per_head, earlier, s, tokens)
        y.append(here[1])
        carried.append(here[2])
        gated.append(here[0])
        mixers = jnp.concatenate([here[0], attended[tokens * s : tokens * (s + 1)]], -1)
        offers.append(
            offer(jnp.einsum("ti,di->td", mixers, out_full_w, preferred_element_type=f32))
        )

    mask_float = valid_mask.astype(f32)[..., None]
    loss_scale = 1.0 / (valid_total * width)
    squares_local = jnp.zeros((), f32)
    resid, normed_two, gateup, inner = [], [], [], []
    down_offers = []
    for s in each:
        mine, other = offers[s]
        other = after(other, offers[-1][0], *(d[0] for d in down_offers))
        resid.append(hidden[s] + summed_pair(mine, other))
        normed_two.append(rms_norm(resid[s], ffn_gain).astype(low))
        gateup.append(jnp.dot(normed_two[s], gateup_full, preferred_element_type=f32))
        inner.append(
            (jax.nn.silu(gateup[s][:, :hidden_units]) * gateup[s][:, hidden_units:]).astype(low)
        )
        down_offers.append(
            offer(jnp.einsum("tf,df->td", inner[s], down_full, preferred_element_type=f32))
        )
    out_full, out_grad, down_in, gateup_low, back_offers = [], [], [], [], []

    def swiglu_flat(both):
        return jax.nn.silu(both[:, :hidden_units]) * both[:, hidden_units:]

    for s in each:
        mine, other = down_offers[s]
        other = after(other, down_offers[-1][0], *(d[0] for d in back_offers))
        out_full.append(resid[s] + summed_pair(mine, other))
        diff = out_full[s] - teacher[s].astype(f32)
        squares_local = squares_local + jnp.sum(mask_float[s] * diff * diff)
        out_grad.append(cotangent[s].astype(f32) + mask_float[s] * 2.0 * diff * loss_scale)
        down_in.append(out_grad[s].astype(low))
        inner_grad = jnp.einsum("td,df->tf", down_in[s], down_full, preferred_element_type=f32)
        gateup_low.append(jax.vjp(swiglu_flat, gateup[s])[1](inner_grad)[0].astype(low))
        back_offers.append(
            offer(jnp.einsum("tc,dc->td", gateup_low[s], gateup_full, preferred_element_type=f32))
        )
    block_out = jnp.stack(out_full).astype(low)

    join = lambda parts: jnp.concatenate(parts, 0)
    def wgrad(left, right):
        left, right = join(left), join(right)
        return jnp.einsum("td,tc->dc", left, right, preferred_element_type=f32).astype(low)

    ffn_terms = jnp.concatenate([wgrad(normed_two, gateup_low), wgrad(down_in, inner)], 1)
    ffn_reduced = lax.psum_scatter(ffn_terms, owners, scatter_dimension=0, tiled=True)

    resid_grad, mixed_low, ffn_gain_grad = [], [], 0.0
    dy, dz, skip_rows, mixers_grads = [], [], [], []
    sent_back = None
    for s in each:
        mine, other = back_offers[s]
        other = after(other, ffn_terms, *([sent_back] if s else []))
        back = jax.vjp(rms_norm, resid[s], ffn_gain)[1](summed_pair(mine, other))
        resid_grad.append(out_grad[s] + back[0])
        ffn_gain_grad = ffn_gain_grad + back[1]
        mixed_low.append(resid_grad[s].astype(low))
        mixers_grads.append(jnp.dot(mixed_low[s], out_full_w, preferred_element_type=f32))
        *here, sent_back = gate_back(
            mixers_grads[s], pre, cols, y[s], v, vbc, logs, per_head, sent, s, seqs, tokens,
            sent_back,
        )
        dy.append(here[0])
        dz.append(here[1])
        skip_rows.append(here[2])
    later = states_beside(sent_back, seqs, 1)
    query_back, keyval_parts = [], [None] * hops
    for s in each:
        gq, *keyval_parts = attend_back(
            queries, keyvals, after(mixers_grads[s], later[0]), channels, attended, lse,
            cosine, sine, at, s, seqs, tokens, keyval_parts,
        )
        query_back.append(gq)
    keyval_parts = [keyval_parts[0]] + [
        passed_along(keyval_parts[d], "ctx", -d) for d in range(1, hops)
    ]
    early_terms, part = early_grads(
        after(normed_t, *later), mixer_both, cols, dz, query_back, mixed_low, gated, attended
    )
    early_reduced = lax.psum_scatter(early_terms, owners, scatter_dimension=0, tiled=True)
    scan_backs = []
    for s in each:
        scan_backs.append(
            scan_back(
                after(dy[s], early_terms), y[s], v, vbc, pre, cols, tails, taps, taps_bc, per_head,
                logs, states, carried[s], later, s, tokens, heads,
            )
        )
    keyval_back = keyval_sum(keyval_parts, cosine, sine, seqs, tokens)
    head = passed_along(join([scan_backs[s][4] for s in each]), "ctx", -1)
    dx, dbc, dstep, edge = (list(a) for a in list(zip(*scan_backs))[:4])
    late_terms, part = late_grads(
        normed_t, mixer_both, cols, after(part, ffn_reduced), keyval_back, head, dx, dbc, dstep, edge
    )
    part = [part[tokens * s : tokens * (s + 1)] for s in each]
    part_other = [swapped(p, "tp", 1) for p in part]
    own, sends, got = spread(core_sum(late_terms), "ctx", 1, 1)

    hidden_rows = [hidden[s] for s in each]
    norm_one_back = [jax.vjp(rms_norm, hidden_rows[s], mixer_gain)[1] for s in each]
    mixer_gain_grad = sum(norm_one_back[s](part[s].astype(f32))[1] for s in each)

    tp_index = lax.axis_index("tp")
    tp_count = lax.axis_size("tp")

    def widen(piece, axis_dim):
        shape_full = list(piece.shape)
        shape_full[axis_dim] = piece.shape[axis_dim] * tp_count
        blank = jnp.zeros(tuple(shape_full), f32)
        return lax.dynamic_update_slice_in_dim(
            blank, piece, tp_index * piece.shape[axis_dim], axis_dim
        )

    def narrow(wide, axis_dim, piece_size):
        return lax.dynamic_slice_in_dim(wide, tp_index * piece_size, piece_size, axis_dim)

    conv_sum, conv_bc_sum, head_sum = (
        sum(scan_backs[s][i] for s in each) for i in (5, 6, 7)
    )
    skip_grad = jnp.sum(sum(skip_rows[s][0] for s in each).reshape(heads, MP), -1)
    small = [
        mixer_gain_grad,
        ffn_gain_grad / tp_count,
        widen(conv_sum[: KC + 1], 1),
        conv_bc_sum[: KC + 1],
        widen(jnp.stack([head_sum[0, :heads], head_sum[1, :heads], skip_grad]), 1),
        (squares_local / tp_count).reshape(1),
    ]
    flat = jnp.concatenate([a.reshape(-1) for a in small])
    fill = -flat.shape[0] % 1024
    flat = after(jnp.pad(flat, (0, fill)).reshape(-1, 128), *sends)
    flat = sum_over(flat, ("ctx",))
    held, early_reduced, *_ = lax.optimization_barrier(
        (added(own, got).astype(low), early_reduced, part_other[0], flat)
    )
    own, sends, got = spread(held, "dp", 0, 0)
    flat = sum_over(after(flat, *sends), ("tp", "dp"))
    late_reduced = added(own, [after(got[0], flat), *got[1:]])
    flat = flat.reshape(-1)
    input_grad = []
    for s in each:
        other = part_other[s] if s == 0 else after(part_other[s], *sends)
        back = norm_one_back[s](summed_pair(part[s], other))[0]
        input_grad.append((resid_grad[s] + back).astype(low))
    summed, start = [], 0
    for a in small:
        summed.append(flat[start : start + a.size].reshape(a.shape))
        start += a.size
    conv_total = narrow(summed[2], 1, channels)
    head_total = narrow(summed[4], 1, heads)
    loss = summed[5][0] * loss_scale
    ffn_reduced = ffn_reduced.astype(f32)
    early_reduced = early_reduced.astype(f32)
    out_reduced = early_reduced[:, channels + q_cols :]
    state_reduced = summed_pair(*offer(late_reduced[:, channels : channels + bc_cols]))
    rest = late_reduced[:, channels + bc_cols :]
    return (
        block_out,
        loss,
        jnp.stack(input_grad),
        summed[0],
        early_reduced[:, channels : channels + q_cols],
        jnp.stack([rest[:, :kv_cols], rest[:, kv_cols : 2 * kv_cols]], 1),
        out_reduced[:, channels:].T,
        jnp.stack([early_reduced[:, :channels], late_reduced[:, :channels]], 1),
        state_reduced,
        rest[:, 2 * kv_cols : 2 * kv_cols + heads],
        conv_total[:KC],
        conv_total[KC],
        summed[3][:KC],
        summed[3][KC],
        head_total[0],
        head_total[1],
        head_total[2],
        out_reduced[:, :channels].T,
        summed[1],
        ffn_reduced[:, : 2 * hidden_units].reshape(rows, 2, hidden_units),
        ffn_reduced[:, 2 * hidden_units :].T,
    )


def solution(mesh):
    return jax.shard_map(
        per_device,
        mesh=mesh,
        in_specs=(
            P("dp", "ctx", None),
            P("dp", "ctx"),
            P("dp", "ctx"),
            P("dp", "ctx", None),
            P("dp", "ctx", None),
            P(),
            P(("dp", "ctx"), "tp"),
            P(("dp", "ctx"), None, "tp"),
            P("tp", ("dp", "ctx")),
            P(("dp", "ctx"), None, "tp"),
            P(("dp", "ctx"), None),
            P(("dp", "ctx"), "tp"),
            P(None, "tp"),
            P("tp"),
            P(),
            P(),
            P("tp"),
            P("tp"),
            P("tp"),
            P("tp", ("dp", "ctx")),
            P(),
            P(("dp", "ctx"), None, "tp"),
            P("tp", ("dp", "ctx")),
        ),
        out_specs=(
            P("dp", "ctx", None),
            P(),
            P("dp", "ctx", None),
            P(),
            P(("dp", "ctx"), "tp"),
            P(("dp", "ctx"), None, "tp"),
            P("tp", ("dp", "ctx")),
            P(("dp", "ctx"), None, "tp"),
            P(("dp", "ctx"), None),
            P(("dp", "ctx"), "tp"),
            P(None, "tp"),
            P("tp"),
            P(),
            P(),
            P("tp"),
            P("tp"),
            P("tp"),
            P("tp", ("dp", "ctx")),
            P(),
            P(("dp", "ctx"), None, "tp"),
            P("tp", ("dp", "ctx")),
        ),
        check_vma=False,
    )
```

```python
import functools

import jax
import jax.numpy as jnp
from jax import lax
from jax.experimental import pallas as pl
from jax.experimental.pallas import tpu as pltpu
from jax.sharding import PartitionSpec as P

HEAD_SIZE = 64
MP = 64
NS = 128
KC = 4
CBLK = 128
VMEM_BYTES = 56 * 1024 * 1024

low = jnp.bfloat16
f32 = jnp.float32
highest = lax.Precision.HIGHEST
NEG = -1e30
eps_norm = 1e-05
rope_base = 100000000000.0


def vmem_params():
    return pltpu.CompilerParams(
        dimension_semantics=("arbitrary",), vmem_limit_bytes=VMEM_BYTES
    )


def mm(left, right):
    return jnp.dot(left, right, preferred_element_type=f32)


def mm_nt(left, right):
    return lax.dot_general(left, right, (((1,), (1,)), ((), ())), preferred_element_type=f32)


def mm_tn(left, right):
    return lax.dot_general(left, right, (((0,), (0,)), ((), ())), preferred_element_type=f32)


def iota(shape, axis):
    return lax.broadcasted_iota(jnp.int32, shape, axis)


def sigmoid(v):
    return 1.0 / (1.0 + jnp.exp(-v))


def softplus(v):
    return jnp.maximum(v, 0.0) + jnp.log1p(jnp.exp(-jnp.abs(v)))


def silu_grad(v, sig):
    return sig * (1.0 + v * (1.0 - sig))


def halves(v):
    high = v.astype(low)
    return high, (v - high.astype(f32)).astype(low)


def head_map(channels):
    shape = (128, channels)
    return jnp.where(iota(shape, 1) // MP == iota(shape, 0), 1.0, 0.0).astype(low)


def expand(per_head, spread):
    high, rest = halves(per_head)
    return mm(high, spread) + mm(rest, spread)


def collect(per_channel, spread):
    high, rest = halves(per_channel)
    return mm_nt(high, spread) + mm_nt(rest, spread)


def rotate(u, cosine, sine):
    first = (iota(u.shape, 1) // 32) % 2 == 0
    return u * cosine + jnp.where(first, pltpu.roll(u, 96, 1), pltpu.roll(u, 32, 1)) * sine


def prep_body(q_ref, kv_ref, cos_ref, sin_ref, q_out, kv_out):
    cosine, sine = cos_ref[...], sin_ref[...]
    scale = HEAD_SIZE ** (-0.5)
    for j in range(q_ref.shape[1] // 128):
        cols = slice(128 * j, 128 * j + 128)
        q_out[:, cols] = rotate(q_ref[:, cols], cosine, sine).astype(low) * jnp.asarray(scale, low)
    kv = kv_ref[...]
    keep = iota(kv.shape, 1) < HEAD_SIZE
    kv_out[...] = jnp.where(keep, rotate(kv, cosine, sine), kv).astype(low)


def attend_body(at_ref, q_ref, *refs, hops):
    kv_refs, (o_ref, lse_ref) = refs[:hops], refs[hops:]
    at = at_ref[0]
    tokens = q_ref.shape[0]
    lane = iota((tokens, 128), 1)
    lo = lane < HEAD_SIZE
    causal = iota((tokens, tokens), 0) >= iota((tokens, tokens), 1)
    lse_all = jnp.zeros((tokens, 128), f32)
    for j in range(q_ref.shape[1] // 128):
        pair = q_ref[:, 128 * j : 128 * j + 128].astype(f32)
        sides = []
        for side in range(2):
            query = pair if side == 0 else pltpu.roll(pair, HEAD_SIZE, 1)
            query = jnp.where(lo, query, 0.0).astype(low)
            scores = []
            for d in range(hops):
                score = mm_nt(query, kv_refs[d][...])
                scores.append(
                    jnp.where(causal if d == 0 else at >= d, score, NEG)
                )
            top = functools.reduce(
                jnp.maximum, [jnp.max(s, -1, keepdims=True) for s in scores]
            )
            total, mixed = 0.0, 0.0
            for d in range(hops):
                expo = jnp.exp(scores[d] - top)
                total = total + jnp.sum(expo, -1, keepdims=True)
                mixed = mixed + mm(expo.astype(low), kv_refs[d][...])
            sides.append(mixed * (1.0 / total))
            lse_all = jnp.where(lane == 2 * j + side, top + jnp.log(total), lse_all)
        o_ref[:, 128 * j : 128 * j + 128] = jnp.where(
            lo, pltpu.roll(sides[0], HEAD_SIZE, 1), sides[1]
        ).astype(low)
    lse_ref[...] = lse_all


def attend_back_body(at_ref, q_ref, go_ref, o_ref, lse_ref, cos_ref, sin_ref, *refs, hops):
    kv_refs, (gq_ref,), gkv_refs = refs[:hops], refs[hops : hops + 1], refs[hops + 1 :]
    at = at_ref[0]
    tokens = q_ref.shape[0]
    lane = iota((tokens, 128), 1)
    lo = lane < HEAD_SIZE
    causal = iota((tokens, tokens), 0) >= iota((tokens, tokens), 1)
    cosine, sine = cos_ref[...], sin_ref[...]
    lse_all = lse_ref[...]
    scale = HEAD_SIZE ** (-0.5)
    gkv = [jnp.zeros((tokens, 128), f32) for _ in range(hops)]
    for j in range(q_ref.shape[1] // 128):
        cols = slice(128 * j, 128 * j + 128)
        pair = q_ref[:, cols].astype(f32)
        go_pair = go_ref[:, cols].astype(low).astype(f32)
        weighed = go_pair * o_ref[:, cols].astype(f32)
        sides = []
        for side in range(2):
            query = pair if side == 0 else pltpu.roll(pair, HEAD_SIZE, 1)
            query = jnp.where(lo, query, 0.0).astype(low)
            grad = pltpu.roll(go_pair, HEAD_SIZE, 1) if side == 0 else go_pair
            grad = jnp.where(lo, 0.0, grad).astype(low)
            centre = jnp.sum(jnp.where(lo == (side == 0), weighed, 0.0), -1, keepdims=True)
            lse = jnp.sum(jnp.where(lane == 2 * j + side, lse_all, 0.0), -1, keepdims=True)
            gq = 0.0
            for d in range(hops):
                kv = kv_refs[d][...]
                score = mm_nt(query, kv)
                prob = jnp.exp(jnp.where(causal if d == 0 else at >= d, score, NEG) - lse)
                gprob = mm_nt(grad, kv)
                gscore = (prob * (gprob - centre)).astype(low)
                gq = gq + mm(gscore, kv)
                gkv[d] = gkv[d] + mm_tn(gscore, query) + mm_tn(prob.astype(low), grad)
            sides.append(gq * scale)
        joined = jnp.where(lo, sides[0], pltpu.roll(sides[1], HEAD_SIZE, 1))
        gq_ref[:, cols] = rotate(joined, cosine, -sine).astype(low)
    for d in range(hops):
        gkv_refs[d][...] = gkv[d].astype(low)


def keyval_total(cosine, sine, parts):
    total = parts[0].astype(f32)
    for part in parts[1:]:
        total = total + part.astype(f32)
    keep = iota(total.shape, 1) < HEAD_SIZE
    return jnp.where(keep, rotate(total, cosine, -sine), total).astype(low)


def decay_pair(logs, logs_t, first, keep):
    both = []
    for head in (first, first + 1):
        gap = logs[:, head : head + 1] - logs_t[head : head + 1, :]
        both.append(jnp.exp(jnp.where(keep, gap, NEG)))
    return both


def step_terms(step_ref, rows, heads_ref, heads):
    raw = step_ref[rows, :] + heads_ref[0:1, :]
    live = iota(raw.shape, 1) < heads
    steps = jnp.where(live, softplus(raw), 0.0)
    return jnp.where(live, raw, 0.0), steps


def lower_triangle(size):
    return iota((size, size), 0) >= iota((size, size), 1)


def scan_body(
    x_ref, bc_ref, step_ref, xt_ref, bct_ref, taps_ref, taps_bc_ref, heads_ref,
    v_ref, vbc_ref, y_ref, logs_ref, states_ref, send_ref,
    xe, bce, *, heads,
):
    tokens, channels = x_ref.shape
    xe[0:8, :] = xt_ref[...]
    xe[8:, :] = x_ref[...]
    bce[0:8, :] = bct_ref[...]
    bce[8:, :] = bc_ref[...]
    spread = head_map(channels)
    keep = lower_triangle(CBLK)
    triangle = jnp.where(keep, 1.0, 0.0)
    lo = iota((CBLK, 128), 1) < MP
    rate = heads_ref[1:2, :]
    state = None
    carry = jnp.zeros((1, 128), f32)
    total_decay = None
    for c in range(tokens // CBLK):
        rows = slice(CBLK * c, CBLK * c + CBLK)

        def conv(ext, taps):
            start = CBLK * c + 8 - (KC - 1)
            total = taps[KC : KC + 1, :] + taps[0:1, :] * ext[start : start + CBLK, :]
            for k in range(1, KC):
                total = total + taps[k : k + 1, :] * ext[start + k : start + k + CBLK, :]
            return total

        v = conv(xe, taps_ref)
        v_ref[rows, :] = v
        xs = v * sigmoid(v)
        vbc = conv(bce, taps_bc_ref)
        vbc_ref[rows, :] = vbc
        bc = (vbc * sigmoid(vbc)).astype(low)
        entry, read = bc[:, :NS], bc[:, NS:]
        _, steps = step_terms(step_ref, rows, heads_ref, heads)
        logs = jnp.dot(triangle, -steps * rate, precision=highest, preferred_element_type=f32)
        logs_t = logs.T
        total = logs[CBLK - 1 : CBLK, :]
        logs_ref[rows, :] = logs + carry
        carry = carry + total
        decays = expand(jnp.exp(logs), spread)
        steps_wide = expand(steps, spread)
        tails_wide = expand(jnp.exp(total - logs) * steps, spread)
        weighted = (xs * steps_wide).astype(low)
        inner = mm_nt(read, entry)
        if state is not None:
            incoming = decays * mm(read, state.astype(low))
        for j in range(channels // 128):
            cols = slice(128 * j, 128 * j + 128)
            left, right = decay_pair(logs, logs_t, 2 * j, keep)
            stacked = jnp.concatenate([(inner * left).astype(low), (inner * right).astype(low)], 0)
            result = mm(stacked, weighted[:, cols])
            out = jnp.where(lo, result[:CBLK], result[CBLK:])
            if state is not None:
                out = out + incoming[:, cols]
            y_ref[rows, cols] = out
        added = mm_tn(entry, (xs * tails_wide).astype(low))
        last = decays[CBLK - 1 : CBLK, :]
        state = added if state is None else last * state + added
        total_decay = last if total_decay is None else total_decay * last
        states_ref[NS * c : NS * c + NS, :] = state
    send_ref[0:NS, :] = state.astype(low)
    send_ref[NS:, :] = jnp.broadcast_to(total_decay, (send_ref.shape[0] - NS, channels)).astype(low)


def by_chip(refs):
    return [refs[:1], *(refs[i : i + 2] for i in range(1, len(refs), 2))]


def chained(groups):
    state = None
    for group in reversed(groups):
        own = sum(ref[0:NS, :].astype(f32) for ref in group)
        if state is None:
            state = own
        else:
            state = own + sum(ref[NS : NS + 1, :].astype(f32) for ref in group) * state
    return state


def gate_body(z_ref, y_ref, v_ref, vbc_ref, logs_ref, heads_ref, *refs):
    earlier, (gated_ref, y_out, carried_ref) = refs[:-3], refs[-3:]
    tokens, channels = y_ref.shape
    spread = head_map(channels)
    skip = expand(heads_ref[...], spread)[2:3, :]
    carried = chained(by_chip(earlier))
    carried_ref[...] = carried
    carried_low = carried.astype(low)
    for c in range(tokens // CBLK):
        rows = slice(CBLK * c, CBLK * c + CBLK)
        vc = vbc_ref[rows, NS:]
        read = (vc * sigmoid(vc)).astype(low)
        y = y_ref[rows, :] + expand(jnp.exp(logs_ref[rows, :]), spread) * mm(read, carried_low)
        y_out[rows, :] = y
        v = v_ref[rows, :]
        z = z_ref[rows, :]
        gated_ref[rows, :] = ((y + skip * (v * sigmoid(v))) * (z * sigmoid(z))).astype(low)


def gate_back_body(
    g_ref, z_ref, y_ref, v_ref, vbc_ref, logs_ref, heads_ref, sent_ref,
    dy_ref, dz_ref, dskip_ref, send_ref,
):
    tokens, channels = y_ref.shape
    spread = head_map(channels)
    skip = expand(heads_ref[...], spread)[2:3, :]
    state, dskip = 0.0, 0.0
    for c in range(tokens // CBLK):
        rows = slice(CBLK * c, CBLK * c + CBLK)
        vc = vbc_ref[rows, NS:]
        read = (vc * sigmoid(vc)).astype(low)
        v = v_ref[rows, :]
        xs = v * sigmoid(v)
        z = z_ref[rows, :]
        sig = sigmoid(z)
        grad = g_ref[rows, :].astype(f32)
        dy = grad * (z * sig)
        dz_ref[rows, :] = (grad * (y_ref[rows, :] + skip * xs) * silu_grad(z, sig)).astype(low)
        dy_ref[rows, :] = dy
        dskip = dskip + jnp.sum(dy * xs, 0, keepdims=True)
        faded = (dy * expand(jnp.exp(logs_ref[rows, :]), spread)).astype(low)
        state = state + mm_tn(read, faded)
    send_ref[0:NS, :] = state.astype(low)
    send_ref[NS:, :] = sent_ref[NS:, :]
    dskip_ref[...] = jnp.broadcast_to(dskip, dskip_ref.shape)


def scan_back_body(
    dy_ref, y_ref, v_ref, vbc_ref, x_ref, bc_ref, step_ref, xt_ref, bct_ref,
    taps_ref, taps_bc_ref, heads_ref, logs_ref, states_ref, carried_ref, *refs, heads,
):
    later, refs = refs[:-10], refs[-10:]
    dx_ref, dbc_ref, dstep_ref, edge_ref, head_ref, gx_ref, gbc_ref, gh_ref, dve, dbce = refs
    tokens, channels = y_ref.shape
    chunks = tokens // CBLK
    spread = head_map(channels)
    keep = lower_triangle(CBLK)
    triangle = jnp.where(keep, 1.0, 0.0)
    lo = iota((CBLK, 128), 1) < MP
    rate = heads_ref[1:2, :]
    skip = expand(heads_ref[...], spread)[2:3, :]
    dstate = chained(by_chip(later))
    dve[0:8, :] = jnp.zeros((8, channels), f32)
    dve[8 + tokens :, :] = jnp.zeros((8, channels), f32)
    dbce[0:8, :] = jnp.zeros((8, 2 * NS), f32)
    dbce[8 + tokens :, :] = jnp.zeros((8, 2 * NS), f32)
    dbias, ddecay = 0.0, 0.0
    for c in reversed(range(chunks)):
        rows = slice(CBLK * c, CBLK * c + CBLK)
        v = v_ref[rows, :]
        sig = sigmoid(v)
        xs = v * sig
        vbc = vbc_ref[rows, :]
        sig_bc = sigmoid(vbc)
        bc = (vbc * sig_bc).astype(low)
        entry, read = bc[:, :NS], bc[:, NS:]
        raw, steps = step_terms(step_ref, rows, heads_ref, heads)
        logs = jnp.dot(triangle, -steps * rate, precision=highest, preferred_element_type=f32)
        logs_t = logs.T
        total = logs[CBLK - 1 : CBLK, :]
        decays = expand(jnp.exp(logs), spread)
        steps_wide = expand(steps, spread)
        tails_wide = expand(jnp.exp(total - logs), spread)
        last = decays[CBLK - 1 : CBLK, :]
        if c == 0:
            state = carried_ref[...]
        else:
            before = expand(jnp.exp(logs_ref[CBLK * c - 8 : CBLK * c, :]), spread)[7:8, :]
            state = states_ref[NS * (c - 1) : NS * c, :] + before * carried_ref[...]
        dy = dy_ref[rows, :]
        dy_low = dy.astype(low)
        w = xs * steps_wide
        w_low = w.astype(low)
        inner = mm_nt(read, entry)
        state_low = state.astype(low)
        dstate_low = dstate.astype(low)
        dw_later = tails_wide * mm(entry, dstate_low)
        faded = (dy * decays).astype(low)
        dread = mm_nt(faded, state_low)
        dentry = mm_nt((w * tails_wide).astype(low), dstate_low)
        dinner = 0.0
        pieces = []
        for j in range(channels // 128):
            cols = slice(128 * j, 128 * j + 128)
            left, right = decay_pair(logs, logs_t, 2 * j, keep)
            dy_pair, w_pair = dy_low[:, cols], w_low[:, cols]
            weights = jnp.concatenate([(inner * left).astype(low), (inner * right).astype(low)], 1)
            result = mm_tn(weights, dy_pair)
            pieces.append(jnp.where(lo, result[:CBLK], result[CBLK:]) + dw_later[:, cols])
            zero = jnp.zeros_like(dy_pair)
            parted = jnp.concatenate([jnp.where(lo, dy_pair, zero), jnp.where(lo, zero, dy_pair)], 0)
            dweights = mm_nt(parted, w_pair)
            dinner = dinner + dweights[:CBLK] * left + dweights[CBLK:] * right
        dw = jnp.concatenate(pieces, 1)
        dinner_low = dinner.astype(low)
        dread = dread + mm(dinner_low, entry)
        dentry = dentry + mm_tn(dinner_low, read)
        dlogs = collect(dy * y_ref[rows, :] - w * dw, spread)
        dtotal = jnp.sum(w * dw_later, 0, keepdims=True) + last * jnp.sum(
            dstate * state, 0, keepdims=True
        )
        dtotal = collect(jnp.broadcast_to(dtotal, (8, channels)), spread)[0:1, :]
        dfall = (
            lax.dot_general(
                triangle, dlogs, (((0,), (0,)), ((), ())),
                precision=highest, preferred_element_type=f32,
            )
            + dtotal
        )
        dsteps = collect(xs * dw, spread) - rate * dfall
        ddecay = ddecay - rate * jnp.sum(steps * dfall, 0, keepdims=True)
        live = iota(raw.shape, 1) < heads
        draw = jnp.where(live, dsteps * sigmoid(raw), 0.0)
        dbias = dbias + jnp.sum(draw, 0, keepdims=True)
        dstep_ref[rows, :] = draw.astype(low)
        dve[8 + CBLK * c : 8 + CBLK * c + CBLK, :] = (steps_wide * dw + skip * dy) * silu_grad(v, sig)
        dbce[8 + CBLK * c : 8 + CBLK * c + CBLK, :] = jnp.concatenate(
            [dentry, dread], 1
        ) * silu_grad(vbc, sig_bc)
        dstate = last * dstate + mm_tn(read, faded)
    gh_ref[0:1, :] = dbias
    gh_ref[1:2, :] = ddecay
    gh_ref[2:, :] = jnp.zeros((gh_ref.shape[0] - 2, 128), f32)

    def conv_back(ext, taps, out_ref, cols, grads_ref, pre_ref, tail_ref):
        def spread_rows(start, count):
            total = taps[0:1, :] * ext[start + KC - 1 : start + KC - 1 + count, :]
            for k in range(1, KC):
                at = start + KC - 1 - k
                total = total + taps[k : k + 1, :] * ext[at : at + count, :]
            return total

        head_ref[0:8, cols] = jnp.zeros((8, ext.shape[1]), f32)
        head_ref[8:16, cols] = spread_rows(0, 8)
        grads = [0.0] * (KC + 1)
        for c in range(chunks):
            at = CBLK * c
            dpre = spread_rows(8 + at, CBLK)
            out_ref[at : at + CBLK, :] = dpre.astype(low)
            if c == chunks - 1:
                edge_ref[:, cols] = dpre[CBLK - 16 :, :]
        for k in range(KC):
            shift = KC - 1 - k
            main = jnp.sum(pre_ref[...] * ext[8 + shift : 8 + shift + tokens, :], 0, keepdims=True)
            edge = jnp.sum(tail_ref[...] * ext[shift : shift + 8, :], 0, keepdims=True)
            grads[k] = main + edge
        grads[KC] = jnp.sum(ext[8 : 8 + tokens, :], 0, keepdims=True)
        for k in range(KC + 1):
            grads_ref[k : k + 1, :] = grads[k]
        grads_ref[KC + 1 :, :] = jnp.zeros((grads_ref.shape[0] - KC - 1, ext.shape[1]), f32)

    conv_back(dve, taps_ref, dx_ref, slice(0, channels), gx_ref, x_ref, xt_ref)
    bc_cols = slice(channels, channels + 2 * NS)
    conv_back(dbce, taps_bc_ref, dbc_ref, bc_cols, gbc_ref, bc_ref, bct_ref)


def block(height, width, col=0, first=0):
    return pl.BlockSpec((height, width), lambda s: (first + s, col))


def whole(shape):
    return pl.BlockSpec(shape, lambda s: (0, 0))


def shaped(rows, cols, dtype):
    return jax.ShapeDtypeStruct((rows, cols), dtype)


def run(body, seqs, inputs, outputs, scratch=(), at=None, flops=0, shared=()):
    arrays = [a for a, _ in inputs]
    specs = [s for _, s in inputs]
    if at is not None:
        arrays = [at] + arrays
        specs = [pl.BlockSpec(memory_space=pltpu.SMEM)] + specs
    moved = sum(a.size * a.dtype.itemsize for a in arrays)
    out_specs = [block(r, c) for r, c, _ in outputs]
    out_shape = [shaped(seqs * r, c, d) for r, c, d in outputs]
    aliases, count = {}, len(arrays)
    for r, c, d, total, first, previous in shared:
        if previous is not None:
            aliases[len(arrays)] = len(out_shape)
            arrays.append(previous)
            specs.append(pl.BlockSpec(memory_space=pl.ANY))
        out_specs.append(block(r, c, 0, first))
        out_shape.append(shaped(total * r, c, d))
    kept = len(aliases)

    def inner(*refs):
        body(*refs[:count], *refs[count + kept :])

    return pl.pallas_call(
        inner,
        grid=(seqs,),
        in_specs=specs,
        out_specs=out_specs,
        out_shape=out_shape,
        scratch_shapes=list(scratch),
        input_output_aliases=aliases,
        compiler_params=vmem_params(),
        cost_estimate=pl.CostEstimate(flops=flops, bytes_accessed=moved, transcendentals=0),
    )(*arrays)


def prep(pre, cosine, sine, seqs, tokens, q_at, q_cols, kv_at):
    return run(
        prep_body,
        seqs,
        [
            (pre, block(tokens, q_cols, q_at // q_cols)),
            (pre, block(tokens, 128, kv_at // 128)),
            (cosine, block(tokens, 128)),
            (sine, block(tokens, 128)),
        ],
        [(tokens, q_cols, low), (tokens, 128, low)],
    )


def attend(queries, keyvals, at, seqs, tokens):
    hops, cols = len(keyvals), queries.shape[1]
    work = 4 * seqs * tokens * tokens * hops * (cols // HEAD_SIZE) * 256
    return run(
        functools.partial(attend_body, hops=hops),
        seqs,
        [(queries, block(tokens, cols))] + [(kv, block(tokens, 128)) for kv in keyvals],
        [(tokens, cols, low), (tokens, 128, f32)],
        at=at,
        flops=work,
    )


def attend_back(
    queries, keyvals, grads, grad_at, outs, lse, cosine, sine, at, first, seqs, tokens, previous
):
    hops, cols = len(keyvals), queries.shape[1]
    work = 10 * tokens * tokens * hops * (cols // HEAD_SIZE) * 256
    return run(
        functools.partial(attend_back_body, hops=hops),
        1,
        [
            (queries, block(tokens, cols, 0, first)),
            (grads, block(tokens, cols, grad_at // cols)),
            (outs, block(tokens, cols, 0, first)),
            (lse, block(tokens, 128, 0, first)),
            (cosine, block(tokens, 128, 0, first)),
            (sine, block(tokens, 128, 0, first)),
        ]
        + [(kv, block(tokens, 128, 0, first)) for kv in keyvals],
        [(tokens, cols, low)],
        at=at,
        flops=work,
        shared=[(tokens, 128, low, seqs, first, p) for p in previous],
    )


SENT = NS + 16


class Columns:
    def __init__(self, channels, q_cols):
        self.channels = channels
        self.x, self.z, self.q = 0, channels, 2 * channels
        self.bc = self.q + q_cols
        self.kv = self.bc + 2 * NS
        self.step = self.kv + 128
        self.total = self.step + 128

    def x_block(self, tokens, first=0):
        return block(tokens, self.channels, 0, first)

    def z_block(self, tokens, first=0):
        return block(tokens, self.channels, 1, first)

    def bc_block(self, tokens, first=0):
        return block(tokens, 2 * NS, self.bc // (2 * NS), first)

    def step_block(self, tokens, first=0):
        return block(tokens, 128, self.step // 128, first)


def scan(pre, cols, tails, taps, taps_bc, per_head, seqs, tokens, heads):
    channels = cols.channels
    return run(
        functools.partial(scan_body, heads=heads),
        seqs,
        [
            (pre, cols.x_block(tokens)),
            (pre, cols.bc_block(tokens)),
            (pre, cols.step_block(tokens)),
            (tails, block(8, channels)),
            (tails, block(8, 2 * NS, channels // (2 * NS))),
            (taps, whole(taps.shape)),
            (taps_bc, whole(taps_bc.shape)),
            (per_head, whole(per_head.shape)),
        ],
        [
            (tokens, channels, f32),
            (tokens, 2 * NS, f32),
            (tokens, channels, f32),
            (tokens, 128, f32),
            (tokens // CBLK * NS, channels, f32),
            (SENT, channels, low),
        ],
        scratch=[pltpu.VMEM((tokens + 8, channels), f32), pltpu.VMEM((tokens + 8, 2 * NS), f32)],
        flops=8 * seqs * tokens * CBLK * channels,
    )


def gate(pre, cols, y, v, vbc, logs, per_head, earlier, first, tokens):
    channels = cols.channels
    return run(
        gate_body,
        1,
        [
            (pre, cols.z_block(tokens, first)),
            (y, block(tokens, channels, 0, first)),
            (v, block(tokens, channels, 0, first)),
            (vbc, block(tokens, 2 * NS, 0, first)),
            (logs, block(tokens, 128, 0, first)),
            (per_head, whole(per_head.shape)),
        ]
        + [(a, block(SENT, channels, 0, first)) for a in earlier],
        [(tokens, channels, low), (tokens, channels, f32), (NS, channels, f32)],
        flops=4 * tokens * CBLK * channels,
    )


def gate_back(grads, pre, cols, y, v, vbc, logs, per_head, sent, first, seqs, tokens, previous):
    channels = cols.channels
    return run(
        gate_back_body,
        1,
        [
            (grads, block(tokens, channels)),
            (pre, cols.z_block(tokens, first)),
            (y, block(tokens, channels)),
            (v, block(tokens, channels, 0, first)),
            (vbc, block(tokens, 2 * NS, 0, first)),
            (logs, block(tokens, 128, 0, first)),
            (per_head, whole(per_head.shape)),
            (sent, block(SENT, channels, 0, first)),
        ],
        [
            (tokens, channels, f32),
            (tokens, channels, low),
            (8, channels, f32),
        ],
        flops=4 * tokens * CBLK * channels,
        shared=[(SENT, channels, low, seqs, first, previous)],
    )


def scan_back(
    dy, y, v, vbc, pre, cols, tails, taps, taps_bc, per_head, logs, states, carried, later,
    first, tokens, heads,
):
    channels = cols.channels
    return run(
        functools.partial(scan_back_body, heads=heads),
        1,
        [
            (dy, block(tokens, channels)),
            (y, block(tokens, channels)),
            (v, block(tokens, channels, 0, first)),
            (vbc, block(tokens, 2 * NS, 0, first)),
            (pre, cols.x_block(tokens, first)),
            (pre, cols.bc_block(tokens, first)),
            (pre, cols.step_block(tokens, first)),
            (tails, block(8, channels, 0, first)),
            (tails, block(8, 2 * NS, channels // (2 * NS), first)),
            (taps, whole(taps.shape)),
            (taps_bc, whole(taps_bc.shape)),
            (per_head, whole(per_head.shape)),
            (logs, block(tokens, 128, 0, first)),
            (states, block(tokens // CBLK * NS, channels, 0, first)),
            (carried, block(NS, channels)),
        ]
        + [(a, block(SENT, channels, 0, first)) for a in later],
        [
            (tokens, channels, low),
            (tokens, 2 * NS, low),
            (tokens, 128, low),
            (16, channels + 2 * NS, f32),
            (16, channels + 2 * NS, f32),
            (8, channels, f32),
            (8, 2 * NS, f32),
            (8, 128, f32),
        ],
        scratch=[
            pltpu.VMEM((tokens + 16, channels), f32),
            pltpu.VMEM((tokens + 16, 2 * NS), f32),
        ],
        flops=30 * tokens * CBLK * channels,
    )


TILE = 256


def wide(rows, col=0, width=None):
    return pl.BlockSpec((TILE, rows if width is None else width), lambda t: (t, col))


def tall(array):
    return pl.BlockSpec((array.shape[0], TILE), lambda t: (0, t))


def tiled(body, width, arrays, specs, outputs, scratch, flops):
    return pl.pallas_call(
        body,
        grid=(width // TILE,),
        in_specs=specs,
        out_specs=[spec for _, _, spec in outputs],
        out_shape=[jax.ShapeDtypeStruct(shape, dtype) for shape, dtype, _ in outputs],
        scratch_shapes=scratch,
        compiler_params=vmem_params(),
        cost_estimate=pl.CostEstimate(
            flops=flops,
            bytes_accessed=sum(a.size * a.dtype.itemsize for a in arrays),
            transcendentals=0,
        ),
    )(*arrays)


def early_grads_body(left_ref, wz_ref, wq_ref, *refs, seqs):
    dz, dq, grads, gated = (refs[seqs * i : seqs * i + seqs] for i in range(4))
    attended, ready, out_ref, part_ref, held = refs[-5:]
    tokens = held.shape[0] // seqs
    z_cols = dz[0].shape[1]

    @pl.when(pl.program_id(0) == 0)
    def _():
        for s in range(seqs):
            held[tokens * s : tokens * (s + 1), :z_cols] = dz[s][...]
            held[tokens * s : tokens * (s + 1), z_cols:] = dq[s][...]

    split = held.shape[1]
    out_ref[:, :split] = mm(left_ref[...], held[...]).astype(low)
    first = split + ready.shape[1]
    middle = first + z_cols
    out_ref[:, split:first] = ready[...]
    from_gated, from_attended = 0.0, 0.0
    for s in range(seqs):
        grad = grads[s][...]
        from_gated = from_gated + mm_tn(grad, gated[s][...])
        from_attended = from_attended + mm_tn(grad, attended[tokens * s : tokens * (s + 1), :])
    out_ref[:, first:middle] = from_gated.astype(low)
    out_ref[:, middle:] = from_attended.astype(low)
    part_ref[...] = mm_nt(held[:, :z_cols], wz_ref[...]) + mm_nt(held[:, z_cols:], wq_ref[...])


def early_grads(left, weight, cols, dz, dq, grads, gated, attended, ready):
    width, rows = left.shape
    own = cols.bc - cols.z
    out_cols = own + ready.shape[1] + gated[0].shape[1] + attended.shape[1]
    q_cols = cols.bc - cols.q
    return tiled(
        functools.partial(early_grads_body, seqs=len(dz)),
        width,
        [left, weight, weight, *dz, *dq, *grads, *gated, attended, ready],
        [
            wide(rows),
            wide(cols.channels, cols.z // cols.channels),
            wide(q_cols, cols.q // q_cols),
        ]
        + [whole(a.shape) for a in (*dz, *dq)]
        + [tall(a) for a in grads]
        + [whole(a.shape) for a in (*gated, attended)]
        + [wide(ready.shape[1])],
        [
            ((width, out_cols), low, wide(out_cols)),
            ((rows, width), f32, pl.BlockSpec((rows, TILE), lambda t: (0, t))),
        ],
        [pltpu.VMEM((rows, own), low)],
        2 * rows * width * (own + out_cols),
    )


def late_grads_body(
    left_ref, wx_ref, wbc_ref, wrest_ref, start_ref, head_ref, cos_ref, sin_ref, *refs, seqs, owned
):
    dx, dbc, dstep, edge = (refs[seqs * i : seqs * i + seqs] for i in range(4))
    keyvals, (out_ref, part_ref, held) = refs[4 * seqs : -3], refs[-3:]
    tokens = held.shape[0] // seqs
    channels = dx[0].shape[1]
    conv_cols = channels + dbc[0].shape[1]

    @pl.when(pl.program_id(0) == 0)
    def _():
        for s in range(seqs):
            rows = slice(tokens * s, tokens * (s + 1))
            held[rows, :channels] = dx[s][...]
            held[rows, channels:conv_cols] = dbc[s][...]
            held[rows, conv_cols : conv_cols + 128] = keyval_total(
                cos_ref[rows, :], sin_ref[rows, :], [ref[rows, :] for ref in keyvals]
            )
            held[rows, conv_cols + 128 :] = dstep[s][...]
            held[tokens * (s + 1) - 16 : tokens * (s + 1), :conv_cols] = (
                edge[s][...] + head_ref[16 * s : 16 * s + 16, :]
            ).astype(low)

    terms = mm(left_ref[...], held[...])
    for core in range(2):
        blocks = [terms[at : at + owned] for at in range(core * owned, TILE, 2 * owned)]
        out_ref[core] = jnp.concatenate(blocks, 0).astype(low)
    part_ref[...] = (
        start_ref[...]
        + mm_nt(held[:, :channels], wx_ref[...])
        + mm_nt(held[:, channels:conv_cols], wbc_ref[...])
        + mm_nt(held[:, conv_cols:], wrest_ref[...])
    ).astype(low)


def late_grads(
    left, weight, cols, start, head, cosine, sine, owned, dx, dbc, dstep, edge, keyvals
):
    width, rows = left.shape
    own = cols.total - (cols.bc - cols.z)
    bc_cols, rest = cols.kv - cols.bc, cols.total - cols.kv
    return tiled(
        functools.partial(late_grads_body, seqs=len(dx), owned=owned),
        width,
        [left, weight, weight, weight, start, head, cosine, sine, *dx, *dbc, *dstep, *edge, *keyvals],
        [
            wide(rows),
            wide(cols.channels, 0),
            wide(bc_cols, cols.bc // bc_cols),
            wide(rest, cols.kv // rest),
            tall(start),
        ]
        + [whole(a.shape) for a in (head, cosine, sine, *dx, *dbc, *dstep, *edge, *keyvals)],
        [
            (
                (2, width // 2, own),
                low,
                pl.BlockSpec((2, TILE // 2, own), lambda t: (0, t, 0)),
            ),
            ((rows, width), low, pl.BlockSpec((rows, TILE), lambda t: (0, t))),
        ],
        [pltpu.VMEM((rows, own), low)],
        4 * rows * width * own,
    )


def passed_along(array, axis, distance):
    devices = range(lax.axis_size(axis))
    route = [(i - distance, i) for i in devices if i - distance in devices]
    return lax.ppermute(array, axis, route)


def after(array, *others):
    return lax.optimization_barrier((array, *others))[0]


def swapped(array, axis, distance):
    devices = range(lax.axis_size(axis))
    return lax.ppermute(array, axis, [(i, i ^ distance) for i in devices])


def offer(part):
    mine = part.astype(low)
    return mine, swapped(mine, "tp", 1)


def summed_pair(mine, other):
    return mine.astype(f32) + other.astype(f32)


def sum_over(array, axes):
    for axis in axes:
        distance = 1
        while distance < lax.axis_size(axis):
            array = array + swapped(array, axis, distance)
            distance *= 2
    return array


def place(axis, distance=0):
    return lax.axis_index(axis).astype(jnp.uint32) ^ jnp.uint32(distance)


def place(axis, distance=0):
    return lax.axis_index(axis).astype(jnp.uint32) ^ jnp.uint32(distance)


def picked(array, at, dim):
    return lax.dynamic_index_in_dim(array, at, dim, False)


def states_beside(sent, seqs, side):
    chips = range(lax.axis_size("ctx") // 2)
    near, far = (1, 0) if side < 0 else (0, 1)
    got = lax.ppermute(sent, "ctx", [(2 * k + far, 2 * k + near) for k in chips])
    own, got = (a.reshape(seqs, SENT, -1).astype(f32) for a in (sent, got))
    is_decay = lax.broadcasted_iota(jnp.int32, (1, SENT, 1), 1) >= NS
    got = jnp.where((lax.axis_index("ctx") & 1) == near, got, jnp.where(is_decay, 1.0, 0.0))
    both = jnp.where(is_decay, own * got, own + own[:, NS : NS + 1] * got)
    first, both = (a.astype(low).reshape(sent.shape) for a in (got, both))
    beside = [first]
    for d in chips[1:]:
        for core in range(2):
            route = [(2 * k + near, 2 * (k - side * d) + core) for k in chips if k - side * d in chips]
            beside.append(lax.ppermute(both, "ctx", route))
    return beside


def core_sum(terms):
    dp, ctx = lax.axis_size("dp"), lax.axis_size("ctx")
    one = jnp.uint32(1)
    got = swapped(picked(terms, place("ctx", 1) & one, 0), "ctx", 1)
    total = picked(terms, place("ctx") & one, 0).astype(f32) + got.astype(f32)
    return total.astype(low).reshape(dp, ctx // 2, -1, terms.shape[2])


def spread(held, axis, dim, shift):
    own = picked(held, place(axis) >> jnp.uint32(shift), dim)
    sends = [
        picked(held, place(axis, d << shift) >> jnp.uint32(shift), dim)
        for d in range(1, held.shape[dim])
    ]
    return own, sends, [swapped(a, axis, (d + 1) << shift) for d, a in enumerate(sends)]


def added(own, got):
    total = own.astype(f32)
    for block_in in got:
        total = total + block_in.astype(f32)
    return total


def rms_norm(values, gain):
    return values * lax.rsqrt(jnp.mean(values * values, -1, keepdims=True) + eps_norm) * gain


def angle_tables(positions):
    half = HEAD_SIZE // 2
    freqs = rope_base ** (-2.0 * jnp.arange(half, dtype=f32) / HEAD_SIZE)
    angles = positions.reshape(-1, 1).astype(f32) * freqs
    cosine, sine = jnp.cos(angles), jnp.sin(angles)
    return jnp.tile(cosine, (1, 4)), jnp.concatenate([-sine, sine, -sine, sine], 1)


def per_device(
    hidden_in,
    positions,
    valid_mask,
    teacher,
    cotangent,
    mixer_gain,
    query_weight,
    keyvalue_projection_weight,
    attnout_weight,
    stream_weight,
    state_weight,
    step_weight,
    conv_stream,
    bias_stream,
    conv_state,
    bias_state,
    step_bias,
    decay_log,
    skip_scale,
    mambaout_weight,
    ffn_gain,
    gateup_weight,
    down_weight,
):
    seqs, tokens, width = hidden_in.shape
    owners = ("dp", "ctx")
    rows = query_weight.shape[0]
    q_cols = query_weight.shape[1]
    kv_cols = keyvalue_projection_weight.shape[2]
    channels = stream_weight.shape[2]
    bc_cols = state_weight.shape[1]
    heads = step_weight.shape[1]
    hidden_units = gateup_weight.shape[2]
    step_cols = 128
    hops = lax.axis_size("ctx")
    each = range(seqs)

    tallies = jnp.sum(valid_mask.reshape(seqs * tokens // CBLK, CBLK), -1).astype(low)
    spare = jnp.zeros((rows, step_cols - heads), low)
    spare = spare.at[0, : tallies.shape[0]].set(tallies)
    mixer_shard = jnp.concatenate(
        [
            stream_weight[:, 1],
            stream_weight[:, 0],
            query_weight,
            state_weight,
            keyvalue_projection_weight.reshape(rows, 2 * kv_cols),
            step_weight,
            spare,
            mambaout_weight.T,
            attnout_weight.T,
        ],
        1,
    )
    cols = Columns(channels, q_cols)
    all_cols = cols.total
    mixer_both = lax.all_gather(mixer_shard, owners, axis=0, tiled=True)
    mixer_full, out_full_w = mixer_both[:, :all_cols], mixer_both[:, all_cols:]
    ffn_shard = jnp.concatenate(
        [gateup_weight.reshape(rows, 2 * hidden_units), down_weight.T], 1
    )
    ffn_full = lax.all_gather(ffn_shard, owners, axis=0, tiled=True)
    gateup_full = ffn_full[:, : 2 * hidden_units]
    down_full = ffn_full[:, 2 * hidden_units :]

    counts = mixer_both.reshape(-1, rows, mixer_both.shape[1])
    counts = counts[:, 0, cols.step + heads : cols.step + heads + tallies.shape[0]]
    valid_total = jnp.sum(counts.astype(f32))

    at = lax.axis_index("ctx").astype(jnp.int32).reshape(1)
    cosine, sine = angle_tables(positions)

    def taps_of(taps, bias):
        spare_rows = jnp.zeros((8 - KC - 1, taps.shape[1]), f32)
        return jnp.concatenate([taps, bias[None], spare_rows], 0)

    taps, taps_bc = taps_of(conv_stream, bias_stream), taps_of(conv_state, bias_state)
    per_head = jnp.pad(
        jnp.stack([step_bias, jnp.exp(decay_log), skip_scale]), ((0, 5), (0, 128 - heads))
    )

    hidden = hidden_in.astype(f32)
    normed = rms_norm(hidden, mixer_gain).astype(low).reshape(seqs * tokens, width)
    normed, normed_t = lax.optimization_barrier((normed, normed.T))
    pre = jnp.dot(normed, mixer_full, preferred_element_type=f32)

    def last_rows(array):
        return array.reshape(seqs, tokens, -1)[:, tokens - 8 :].reshape(seqs * 8, -1)

    ends = last_rows(pre)
    ends = jnp.concatenate([ends[:, : cols.z], ends[:, cols.bc : cols.kv]], 1)
    tails = passed_along(ends, "ctx", 1)
    queries, keyval = prep(pre, cosine, sine, seqs, tokens, cols.q, q_cols, cols.kv)
    keyvals = [keyval] + [passed_along(keyval, "ctx", d) for d in range(1, hops)]
    v, vbc, y_own, logs, states, sent = scan(
        after(pre, keyval), cols, tails, taps, taps_bc, per_head, seqs, tokens, heads
    )
    earlier = states_beside(after(sent, *keyvals[1:]), seqs, -1)
    attended, lse = attend(after(queries, earlier[0]), keyvals, at, seqs, tokens)
    gated, y, carried, offers = [], [], [], []
    for s in each:
        here = gate(pre, cols, y_own, v, vbc, logs, per_head, earlier, s, tokens)
        y.append(here[1])
        carried.append(here[2])
        gated.append(here[0])
        mixers = jnp.concatenate([here[0], attended[tokens * s : tokens * (s + 1)]], -1)
        offers.append(
            offer(jnp.einsum("ti,di->td", mixers, out_full_w, preferred_element_type=f32))
        )

    mask_float = valid_mask.astype(f32)[..., None]
    loss_scale = 1.0 / (valid_total * width)
    squares_local = jnp.zeros((), f32)
    resid, normed_two, gateup, inner = [], [], [], []
    down_offers = []
    for s in each:
        mine, other = offers[s]
        other = after(other, offers[-1][0], *(d[0] for d in down_offers))
        resid.append(hidden[s] + summed_pair(mine, other))
        normed_two.append(rms_norm(resid[s], ffn_gain).astype(low))
        gateup.append(jnp.dot(normed_two[s], gateup_full, preferred_element_type=f32))
        inner.append(
            (jax.nn.silu(gateup[s][:, :hidden_units]) * gateup[s][:, hidden_units:]).astype(low)
        )
        down_offers.append(
            offer(jnp.einsum("tf,df->td", inner[s], down_full, preferred_element_type=f32))
        )
    out_full, out_grad, down_in, gateup_low, back_offers = [], [], [], [], []

    def swiglu_flat(both):
        return jax.nn.silu(both[:, :hidden_units]) * both[:, hidden_units:]

    for s in each:
        mine, other = down_offers[s]
        other = after(other, down_offers[-1][0], *(d[0] for d in back_offers))
        out_full.append(resid[s] + summed_pair(mine, other))
        diff = out_full[s] - teacher[s].astype(f32)
        squares_local = squares_local + jnp.sum(mask_float[s] * diff * diff)
        out_grad.append(cotangent[s].astype(f32) + mask_float[s] * 2.0 * diff * loss_scale)
        down_in.append(out_grad[s].astype(low))
        inner_grad = jnp.einsum("td,df->tf", down_in[s], down_full, preferred_element_type=f32)
        gateup_low.append(jax.vjp(swiglu_flat, gateup[s])[1](inner_grad)[0].astype(low))
        mine = jnp.einsum("tc,dc->td", gateup_low[s], gateup_full, preferred_element_type=f32)
        back_offers.append(offer(mine) if s == 0 else (mine.astype(low),))
    block_out = jnp.stack(out_full).astype(low)

    join = lambda parts: jnp.concatenate(parts, 0)
    def wgrad(left, right):
        left, right = join(left), join(right)
        return jnp.einsum("td,tc->dc", left, right, preferred_element_type=f32).astype(low)

    gateup_terms = wgrad(normed_two, gateup_low)

    resid_grad, mixed_low, ffn_gain_grad = [], [], 0.0
    dy, dz, skip_rows, mixers_grads = [], [], [], []
    sent_back = None
    for s in each:
        mine = back_offers[s][0]
        if s == 0:
            other = after(back_offers[s][1], gateup_terms, back_offers[-1][0])
            gateup_reduced = lax.psum_scatter(
                after(gateup_terms, other), owners, scatter_dimension=0, tiled=True
            )
        else:
            other = after(swapped(after(mine, other), "tp", 1), sent_back)
        back = jax.vjp(rms_norm, resid[s], ffn_gain)[1](summed_pair(mine, other))
        resid_grad.append(out_grad[s] + back[0])
        ffn_gain_grad = ffn_gain_grad + back[1]
        mixed_low.append(resid_grad[s].astype(low))
        mixers_grads.append(jnp.dot(mixed_low[s], out_full_w, preferred_element_type=f32))
        *here, sent_back = gate_back(
            mixers_grads[s], pre, cols, y[s], v, vbc, logs, per_head, sent, s, seqs, tokens,
            sent_back,
        )
        dy.append(here[0])
        dz.append(here[1])
        skip_rows.append(here[2])
    later = states_beside(sent_back, seqs, 1)
    query_back, keyval_parts = [], [None] * hops
    for s in each:
        gq, *keyval_parts = attend_back(
            queries, keyvals, after(mixers_grads[s], later[0]), channels, attended, lse,
            cosine, sine, at, s, seqs, tokens, keyval_parts,
        )
        query_back.append(gq)
    early_terms, part = early_grads(
        after(normed_t, *later), mixer_both, cols, dz, query_back, mixed_low, gated, attended,
        wgrad(down_in, inner),
    )
    early_reduced = lax.psum_scatter(early_terms, owners, scatter_dimension=0, tiled=True)
    keyval_parts = [keyval_parts[0]] + [
        passed_along(keyval_parts[d], "ctx", -d) for d in range(1, hops)
    ]
    scan_backs = []
    for s in each:
        scan_backs.append(
            scan_back(
                after(dy[s], early_terms), y[s], v, vbc, pre, cols, tails, taps, taps_bc, per_head,
                logs, states, carried[s], later, s, tokens, heads,
            )
        )
    head = passed_along(join([scan_backs[s][4] for s in each]), "ctx", -1)
    dx, dbc, dstep, edge = (list(a) for a in list(zip(*scan_backs))[:4])
    late_terms, part = late_grads(
        normed_t, mixer_both, cols, after(part, gateup_reduced), head, cosine, sine, rows,
        dx, dbc, dstep, edge, keyval_parts,
    )
    part = [part[tokens * s : tokens * (s + 1)] for s in each]
    own, sends, got = spread(core_sum(late_terms), "ctx", 1, 1)

    hidden_rows = [hidden[s] for s in each]
    norm_one_back = [jax.vjp(rms_norm, hidden_rows[s], mixer_gain)[1] for s in each]
    mixer_gain_grad = sum(norm_one_back[s](part[s].astype(f32))[1] for s in each)

    tp_index = lax.axis_index("tp")
    tp_count = lax.axis_size("tp")

    def widen(piece, axis_dim):
        shape_full = list(piece.shape)
        shape_full[axis_dim] = piece.shape[axis_dim] * tp_count
        blank = jnp.zeros(tuple(shape_full), f32)
        return lax.dynamic_update_slice_in_dim(
            blank, piece, tp_index * piece.shape[axis_dim], axis_dim
        )

    def narrow(wide, axis_dim, piece_size):
        return lax.dynamic_slice_in_dim(wide, tp_index * piece_size, piece_size, axis_dim)

    conv_sum, conv_bc_sum, head_sum = (
        sum(scan_backs[s][i] for s in each) for i in (5, 6, 7)
    )
    skip_grad = jnp.sum(sum(skip_rows[s][0] for s in each).reshape(heads, MP), -1)
    small = [
        mixer_gain_grad,
        ffn_gain_grad / tp_count,
        widen(conv_sum[: KC + 1], 1),
        conv_bc_sum[: KC + 1],
        widen(jnp.stack([head_sum[0, :heads], head_sum[1, :heads], skip_grad]), 1),
        (squares_local / tp_count).reshape(1),
    ]
    flat = jnp.concatenate([a.reshape(-1) for a in small])
    fill = -flat.shape[0] % 1024
    flat = after(jnp.pad(flat, (0, fill)).reshape(-1, 128), *sends)
    flat = sum_over(flat, ("tp",))
    part_other = [swapped(after(p, flat), "tp", 1) for p in part]
    flat = sum_over(flat, ("dp", "ctx"))
    held = after(added(own, got).astype(low), part_other[0], flat)
    own, sends, got = spread(held, "dp", 0, 0)
    flat = after(flat, *sends).reshape(-1)
    summed, start = [], 0
    for a in small:
        summed.append(flat[start : start + a.size].reshape(a.shape))
        start += a.size
    conv_total = narrow(summed[2], 1, channels)
    head_total = narrow(summed[4], 1, heads)
    loss = summed[5][0] * loss_scale
    small_outs = (summed[0], summed[1], summed[3], conv_total, head_total)
    other = [after(part_other[s], *(small_outs if s else sends)) for s in each]
    normed_grad = join([summed_pair(part[s], other[s]) for s in each])
    norm_back = jax.vjp(rms_norm, hidden.reshape(seqs * tokens, width), mixer_gain)[1]
    input_grad = (join(resid_grad) + norm_back(normed_grad)[0]).astype(low)
    last, early_reduced, _ = lax.optimization_barrier((got[0], early_reduced, input_grad))
    late_reduced = added(own, [last, *got[1:]])
    gateup_reduced = gateup_reduced.astype(f32)
    early_reduced = early_reduced.astype(f32)
    down_reduced = early_reduced[:, channels + q_cols : channels + q_cols + hidden_units]
    out_reduced = early_reduced[:, channels + q_cols + hidden_units :]
    state_reduced = summed_pair(*offer(late_reduced[:, channels : channels + bc_cols]))
    rest = late_reduced[:, channels + bc_cols :]
    return (
        block_out,
        loss,
        input_grad.reshape(seqs, tokens, width),
        summed[0],
        early_reduced[:, channels : channels + q_cols],
        jnp.stack([rest[:, :kv_cols], rest[:, kv_cols : 2 * kv_cols]], 1),
        out_reduced[:, channels:].T,
        jnp.stack([early_reduced[:, :channels], late_reduced[:, :channels]], 1),
        state_reduced,
        rest[:, 2 * kv_cols : 2 * kv_cols + heads],
        conv_total[:KC],
        conv_total[KC],
        summed[3][:KC],
        summed[3][KC],
        head_total[0],
        head_total[1],
        head_total[2],
        out_reduced[:, :channels].T,
        summed[1],
        gateup_reduced.reshape(rows, 2, hidden_units),
        down_reduced.T,
    )


def solution(mesh):
    return jax.shard_map(
        per_device,
        mesh=mesh,
        in_specs=(
            P("dp", "ctx", None),
            P("dp", "ctx"),
            P("dp", "ctx"),
            P("dp", "ctx", None),
            P("dp", "ctx", None),
            P(),
            P(("dp", "ctx"), "tp"),
            P(("dp", "ctx"), None, "tp"),
            P("tp", ("dp", "ctx")),
            P(("dp", "ctx"), None, "tp"),
            P(("dp", "ctx"), None),
            P(("dp", "ctx"), "tp"),
            P(None, "tp"),
            P("tp"),
            P(),
            P(),
            P("tp"),
            P("tp"),
            P("tp"),
            P("tp", ("dp", "ctx")),
            P(),
            P(("dp", "ctx"), None, "tp"),
            P("tp", ("dp", "ctx")),
        ),
        out_specs=(
            P("dp", "ctx", None),
            P(),
            P("dp", "ctx", None),
            P(),
            P(("dp", "ctx"), "tp"),
            P(("dp", "ctx"), None, "tp"),
            P("tp", ("dp", "ctx")),
            P(("dp", "ctx"), None, "tp"),
            P(("dp", "ctx"), None),
            P(("dp", "ctx"), "tp"),
            P(None, "tp"),
            P("tp"),
            P(),
            P(),
            P("tp"),
            P("tp"),
            P("tp"),
            P("tp", ("dp", "ctx")),
            P(),
            P(("dp", "ctx"), None, "tp"),
            P("tp", ("dp", "ctx")),
        ),
        check_vma=False,
    )
```

```python
import functools

import jax
import jax.numpy as jnp
from jax import lax
from jax.experimental import pallas as pl
from jax.experimental.pallas import tpu as pltpu
from jax.sharding import PartitionSpec as P

HEAD_SIZE = 64
MP = 64
NS = 128
KC = 4
CBLK = 128
VMEM_BYTES = 56 * 1024 * 1024

low = jnp.bfloat16
f32 = jnp.float32
highest = lax.Precision.HIGHEST
NEG = -1e30
eps_norm = 1e-05
rope_base = 100000000000.0


def vmem_params():
    return pltpu.CompilerParams(
        dimension_semantics=("arbitrary",), vmem_limit_bytes=VMEM_BYTES
    )


def mm(left, right):
    return jnp.dot(left, right, preferred_element_type=f32)


def mm_nt(left, right):
    return lax.dot_general(left, right, (((1,), (1,)), ((), ())), preferred_element_type=f32)


def mm_tn(left, right):
    return lax.dot_general(left, right, (((0,), (0,)), ((), ())), preferred_element_type=f32)


def iota(shape, axis):
    return lax.broadcasted_iota(jnp.int32, shape, axis)


def sigmoid(v):
    return 1.0 / (1.0 + jnp.exp(-v))


def softplus(v):
    return jnp.maximum(v, 0.0) + jnp.log1p(jnp.exp(-jnp.abs(v)))


def silu_grad(v, sig):
    return sig * (1.0 + v * (1.0 - sig))


def halves(v):
    high = v.astype(low)
    return high, (v - high.astype(f32)).astype(low)


def head_map(channels):
    shape = (128, channels)
    return jnp.where(iota(shape, 1) // MP == iota(shape, 0), 1.0, 0.0).astype(low)


def expand(per_head, spread):
    high, rest = halves(per_head)
    return mm(high, spread) + mm(rest, spread)


def collect(per_channel, spread):
    high, rest = halves(per_channel)
    return mm_nt(high, spread) + mm_nt(rest, spread)


def rotate(u, cosine, sine):
    first = (iota(u.shape, 1) // 32) % 2 == 0
    return u * cosine + jnp.where(first, pltpu.roll(u, 96, 1), pltpu.roll(u, 32, 1)) * sine


def prep_body(q_ref, kv_ref, cos_ref, sin_ref, q_out, kv_out):
    cosine, sine = cos_ref[...], sin_ref[...]
    scale = HEAD_SIZE ** (-0.5)
    for j in range(q_ref.shape[1] // 128):
        cols = slice(128 * j, 128 * j + 128)
        q_out[:, cols] = rotate(q_ref[:, cols], cosine, sine).astype(low) * jnp.asarray(scale, low)
    kv = kv_ref[...]
    keep = iota(kv.shape, 1) < HEAD_SIZE
    kv_out[...] = jnp.where(keep, rotate(kv, cosine, sine), kv).astype(low)


def attend_body(at_ref, q_ref, *refs, hops):
    kv_refs, (o_ref, lse_ref) = refs[:hops], refs[hops:]
    at = at_ref[0]
    tokens = q_ref.shape[0]
    lane = iota((tokens, 128), 1)
    lo = lane < HEAD_SIZE
    causal = iota((tokens, tokens), 0) >= iota((tokens, tokens), 1)
    lse_all = jnp.zeros((tokens, 128), f32)
    for j in range(q_ref.shape[1] // 128):
        pair = q_ref[:, 128 * j : 128 * j + 128].astype(f32)
        sides = []
        for side in range(2):
            query = pair if side == 0 else pltpu.roll(pair, HEAD_SIZE, 1)
            query = jnp.where(lo, query, 0.0).astype(low)
            scores = []
            for d in range(hops):
                score = mm_nt(query, kv_refs[d][...])
                scores.append(
                    jnp.where(causal if d == 0 else at >= d, score, NEG)
                )
            top = functools.reduce(
                jnp.maximum, [jnp.max(s, -1, keepdims=True) for s in scores]
            )
            total, mixed = 0.0, 0.0
            for d in range(hops):
                expo = jnp.exp(scores[d] - top)
                total = total + jnp.sum(expo, -1, keepdims=True)
                mixed = mixed + mm(expo.astype(low), kv_refs[d][...])
            sides.append(mixed * (1.0 / total))
            lse_all = jnp.where(lane == 2 * j + side, top + jnp.log(total), lse_all)
        o_ref[:, 128 * j : 128 * j + 128] = jnp.where(
            lo, pltpu.roll(sides[0], HEAD_SIZE, 1), sides[1]
        ).astype(low)
    lse_ref[...] = lse_all


def attend_back_body(at_ref, q_ref, go_ref, o_ref, lse_ref, cos_ref, sin_ref, *refs, hops):
    kv_refs, (gq_ref,), gkv_refs = refs[:hops], refs[hops : hops + 1], refs[hops + 1 :]
    at = at_ref[0]
    tokens = q_ref.shape[0]
    lane = iota((tokens, 128), 1)
    lo = lane < HEAD_SIZE
    causal = iota((tokens, tokens), 0) >= iota((tokens, tokens), 1)
    cosine, sine = cos_ref[...], sin_ref[...]
    lse_all = lse_ref[...]
    scale = HEAD_SIZE ** (-0.5)
    gkv = [jnp.zeros((tokens, 128), f32) for _ in range(hops)]
    for j in range(q_ref.shape[1] // 128):
        cols = slice(128 * j, 128 * j + 128)
        pair = q_ref[:, cols].astype(f32)
        go_pair = go_ref[:, cols].astype(low).astype(f32)
        weighed = go_pair * o_ref[:, cols].astype(f32)
        sides = []
        for side in range(2):
            query = pair if side == 0 else pltpu.roll(pair, HEAD_SIZE, 1)
            query = jnp.where(lo, query, 0.0).astype(low)
            grad = pltpu.roll(go_pair, HEAD_SIZE, 1) if side == 0 else go_pair
            grad = jnp.where(lo, 0.0, grad).astype(low)
            centre = jnp.sum(jnp.where(lo == (side == 0), weighed, 0.0), -1, keepdims=True)
            lse = jnp.sum(jnp.where(lane == 2 * j + side, lse_all, 0.0), -1, keepdims=True)
            gq = 0.0
            for d in range(hops):
                kv = kv_refs[d][...]
                score = mm_nt(query, kv)
                prob = jnp.exp(jnp.where(causal if d == 0 else at >= d, score, NEG) - lse)
                gprob = mm_nt(grad, kv)
                gscore = (prob * (gprob - centre)).astype(low)
                gq = gq + mm(gscore, kv)
                gkv[d] = gkv[d] + mm_tn(gscore, query) + mm_tn(prob.astype(low), grad)
            sides.append(gq * scale)
        joined = jnp.where(lo, sides[0], pltpu.roll(sides[1], HEAD_SIZE, 1))
        gq_ref[:, cols] = rotate(joined, cosine, -sine).astype(low)
    for d in range(hops):
        gkv_refs[d][...] = gkv[d].astype(low)


def keyval_total(cosine, sine, parts):
    total = parts[0].astype(f32)
    for part in parts[1:]:
        total = total + part.astype(f32)
    keep = iota(total.shape, 1) < HEAD_SIZE
    return jnp.where(keep, rotate(total, cosine, -sine), total).astype(low)


def decay_pair(logs, logs_t, first, keep):
    both = []
    for head in (first, first + 1):
        gap = logs[:, head : head + 1] - logs_t[head : head + 1, :]
        both.append(jnp.exp(jnp.where(keep, gap, NEG)))
    return both


def step_terms(step_ref, rows, heads_ref, heads):
    raw = step_ref[rows, :] + heads_ref[0:1, :]
    live = iota(raw.shape, 1) < heads
    steps = jnp.where(live, softplus(raw), 0.0)
    return jnp.where(live, raw, 0.0), steps


def lower_triangle(size):
    return iota((size, size), 0) >= iota((size, size), 1)


def scan_body(
    x_ref, bc_ref, step_ref, xt_ref, bct_ref, taps_ref, taps_bc_ref, heads_ref,
    v_ref, vbc_ref, y_ref, logs_ref, states_ref, send_ref,
    xe, bce, *, heads,
):
    tokens, channels = x_ref.shape
    xe[0:8, :] = xt_ref[...]
    xe[8:, :] = x_ref[...]
    bce[0:8, :] = bct_ref[...]
    bce[8:, :] = bc_ref[...]
    spread = head_map(channels)
    keep = lower_triangle(CBLK)
    triangle = jnp.where(keep, 1.0, 0.0)
    lo = iota((CBLK, 128), 1) < MP
    rate = heads_ref[1:2, :]
    state = None
    carry = jnp.zeros((1, 128), f32)
    total_decay = None
    for c in range(tokens // CBLK):
        rows = slice(CBLK * c, CBLK * c + CBLK)

        def conv(ext, taps):
            start = CBLK * c + 8 - (KC - 1)
            total = taps[KC : KC + 1, :] + taps[0:1, :] * ext[start : start + CBLK, :]
            for k in range(1, KC):
                total = total + taps[k : k + 1, :] * ext[start + k : start + k + CBLK, :]
            return total

        v = conv(xe, taps_ref)
        v_ref[rows, :] = v
        xs = v * sigmoid(v)
        vbc = conv(bce, taps_bc_ref)
        vbc_ref[rows, :] = vbc
        bc = (vbc * sigmoid(vbc)).astype(low)
        entry, read = bc[:, :NS], bc[:, NS:]
        _, steps = step_terms(step_ref, rows, heads_ref, heads)
        logs = jnp.dot(triangle, -steps * rate, precision=highest, preferred_element_type=f32)
        logs_t = logs.T
        total = logs[CBLK - 1 : CBLK, :]
        logs_ref[rows, :] = logs + carry
        carry = carry + total
        decays = expand(jnp.exp(logs), spread)
        steps_wide = expand(steps, spread)
        tails_wide = expand(jnp.exp(total - logs) * steps, spread)
        weighted = (xs * steps_wide).astype(low)
        inner = mm_nt(read, entry)
        if state is not None:
            incoming = decays * mm(read, state.astype(low))
        for j in range(channels // 128):
            cols = slice(128 * j, 128 * j + 128)
            left, right = decay_pair(logs, logs_t, 2 * j, keep)
            stacked = jnp.concatenate([(inner * left).astype(low), (inner * right).astype(low)], 0)
            result = mm(stacked, weighted[:, cols])
            out = jnp.where(lo, result[:CBLK], result[CBLK:])
            if state is not None:
                out = out + incoming[:, cols]
            y_ref[rows, cols] = out
        added = mm_tn(entry, (xs * tails_wide).astype(low))
        last = decays[CBLK - 1 : CBLK, :]
        state = added if state is None else last * state + added
        total_decay = last if total_decay is None else total_decay * last
        states_ref[NS * c : NS * c + NS, :] = state
    send_ref[0:NS, :] = state.astype(low)
    send_ref[NS:, :] = jnp.broadcast_to(total_decay, (send_ref.shape[0] - NS, channels)).astype(low)


def by_chip(refs):
    return [refs[:1], *(refs[i : i + 2] for i in range(1, len(refs), 2))]


def chained(groups):
    state = None
    for group in reversed(groups):
        own = sum(ref[0:NS, :].astype(f32) for ref in group)
        if state is None:
            state = own
        else:
            state = own + sum(ref[NS : NS + 1, :].astype(f32) for ref in group) * state
    return state


def gate_body(z_ref, y_ref, v_ref, vbc_ref, logs_ref, heads_ref, *refs):
    earlier, (gated_ref, y_out, carried_ref) = refs[:-3], refs[-3:]
    tokens, channels = y_ref.shape
    spread = head_map(channels)
    skip = expand(heads_ref[...], spread)[2:3, :]
    carried = chained(by_chip(earlier))
    carried_ref[...] = carried
    carried_low = carried.astype(low)
    for c in range(tokens // CBLK):
        rows = slice(CBLK * c, CBLK * c + CBLK)
        vc = vbc_ref[rows, NS:]
        read = (vc * sigmoid(vc)).astype(low)
        y = y_ref[rows, :] + expand(jnp.exp(logs_ref[rows, :]), spread) * mm(read, carried_low)
        y_out[rows, :] = y
        v = v_ref[rows, :]
        z = z_ref[rows, :]
        gated_ref[rows, :] = ((y + skip * (v * sigmoid(v))) * (z * sigmoid(z))).astype(low)


def gate_back_body(
    g_ref, z_ref, y_ref, v_ref, vbc_ref, logs_ref, heads_ref, sent_ref,
    dy_ref, dz_ref, dskip_ref, send_ref,
):
    tokens, channels = y_ref.shape
    spread = head_map(channels)
    skip = expand(heads_ref[...], spread)[2:3, :]
    state, dskip = 0.0, 0.0
    for c in range(tokens // CBLK):
        rows = slice(CBLK * c, CBLK * c + CBLK)
        vc = vbc_ref[rows, NS:]
        read = (vc * sigmoid(vc)).astype(low)
        v = v_ref[rows, :]
        xs = v * sigmoid(v)
        z = z_ref[rows, :]
        sig = sigmoid(z)
        grad = g_ref[rows, :].astype(f32)
        dy = grad * (z * sig)
        dz_ref[rows, :] = (grad * (y_ref[rows, :] + skip * xs) * silu_grad(z, sig)).astype(low)
        dy_ref[rows, :] = dy
        dskip = dskip + jnp.sum(dy * xs, 0, keepdims=True)
        faded = (dy * expand(jnp.exp(logs_ref[rows, :]), spread)).astype(low)
        state = state + mm_tn(read, faded)
    send_ref[0:NS, :] = state.astype(low)
    send_ref[NS:, :] = sent_ref[NS:, :]
    dskip_ref[...] = jnp.broadcast_to(dskip, dskip_ref.shape)


def scan_back_body(
    dy_ref, y_ref, v_ref, vbc_ref, x_ref, bc_ref, step_ref, xt_ref, bct_ref,
    taps_ref, taps_bc_ref, heads_ref, logs_ref, states_ref, carried_ref, *refs, heads,
):
    later, refs = refs[:-10], refs[-10:]
    dx_ref, dbc_ref, dstep_ref, edge_ref, head_ref, gx_ref, gbc_ref, gh_ref, dve, dbce = refs
    tokens, channels = y_ref.shape
    chunks = tokens // CBLK
    spread = head_map(channels)
    keep = lower_triangle(CBLK)
    triangle = jnp.where(keep, 1.0, 0.0)
    lo = iota((CBLK, 128), 1) < MP
    rate = heads_ref[1:2, :]
    skip = expand(heads_ref[...], spread)[2:3, :]
    dstate = chained(by_chip(later))
    dve[0:8, :] = jnp.zeros((8, channels), f32)
    dve[8 + tokens :, :] = jnp.zeros((8, channels), f32)
    dbce[0:8, :] = jnp.zeros((8, 2 * NS), f32)
    dbce[8 + tokens :, :] = jnp.zeros((8, 2 * NS), f32)
    dbias, ddecay = 0.0, 0.0
    for c in reversed(range(chunks)):
        rows = slice(CBLK * c, CBLK * c + CBLK)
        v = v_ref[rows, :]
        sig = sigmoid(v)
        xs = v * sig
        vbc = vbc_ref[rows, :]
        sig_bc = sigmoid(vbc)
        bc = (vbc * sig_bc).astype(low)
        entry, read = bc[:, :NS], bc[:, NS:]
        raw, steps = step_terms(step_ref, rows, heads_ref, heads)
        logs = jnp.dot(triangle, -steps * rate, precision=highest, preferred_element_type=f32)
        logs_t = logs.T
        total = logs[CBLK - 1 : CBLK, :]
        decays = expand(jnp.exp(logs), spread)
        steps_wide = expand(steps, spread)
        tails_wide = expand(jnp.exp(total - logs), spread)
        last = decays[CBLK - 1 : CBLK, :]
        if c == 0:
            state = carried_ref[...]
        else:
            before = expand(jnp.exp(logs_ref[CBLK * c - 8 : CBLK * c, :]), spread)[7:8, :]
            state = states_ref[NS * (c - 1) : NS * c, :] + before * carried_ref[...]
        dy = dy_ref[rows, :]
        dy_low = dy.astype(low)
        w = xs * steps_wide
        w_low = w.astype(low)
        inner = mm_nt(read, entry)
        state_low = state.astype(low)
        dstate_low = dstate.astype(low)
        dw_later = tails_wide * mm(entry, dstate_low)
        faded = (dy * decays).astype(low)
        dread = mm_nt(faded, state_low)
        dentry = mm_nt((w * tails_wide).astype(low), dstate_low)
        dinner = 0.0
        pieces = []
        for j in range(channels // 128):
            cols = slice(128 * j, 128 * j + 128)
            left, right = decay_pair(logs, logs_t, 2 * j, keep)
            dy_pair, w_pair = dy_low[:, cols], w_low[:, cols]
            weights = jnp.concatenate([(inner * left).astype(low), (inner * right).astype(low)], 1)
            result = mm_tn(weights, dy_pair)
            pieces.append(jnp.where(lo, result[:CBLK], result[CBLK:]) + dw_later[:, cols])
            zero = jnp.zeros_like(dy_pair)
            parted = jnp.concatenate([jnp.where(lo, dy_pair, zero), jnp.where(lo, zero, dy_pair)], 0)
            dweights = mm_nt(parted, w_pair)
            dinner = dinner + dweights[:CBLK] * left + dweights[CBLK:] * right
        dw = jnp.concatenate(pieces, 1)
        dinner_low = dinner.astype(low)
        dread = dread + mm(dinner_low, entry)
        dentry = dentry + mm_tn(dinner_low, read)
        dlogs = collect(dy * y_ref[rows, :] - w * dw, spread)
        dtotal = jnp.sum(w * dw_later, 0, keepdims=True) + last * jnp.sum(
            dstate * state, 0, keepdims=True
        )
        dtotal = collect(jnp.broadcast_to(dtotal, (8, channels)), spread)[0:1, :]
        dfall = (
            lax.dot_general(
                triangle, dlogs, (((0,), (0,)), ((), ())),
                precision=highest, preferred_element_type=f32,
            )
            + dtotal
        )
        dsteps = collect(xs * dw, spread) - rate * dfall
        ddecay = ddecay - rate * jnp.sum(steps * dfall, 0, keepdims=True)
        live = iota(raw.shape, 1) < heads
        draw = jnp.where(live, dsteps * sigmoid(raw), 0.0)
        dbias = dbias + jnp.sum(draw, 0, keepdims=True)
        dstep_ref[rows, :] = draw.astype(low)
        dve[8 + CBLK * c : 8 + CBLK * c + CBLK, :] = (steps_wide * dw + skip * dy) * silu_grad(v, sig)
        dbce[8 + CBLK * c : 8 + CBLK * c + CBLK, :] = jnp.concatenate(
            [dentry, dread], 1
        ) * silu_grad(vbc, sig_bc)
        dstate = last * dstate + mm_tn(read, faded)
    gh_ref[0:1, :] = dbias
    gh_ref[1:2, :] = ddecay
    gh_ref[2:, :] = jnp.zeros((gh_ref.shape[0] - 2, 128), f32)

    def conv_back(ext, taps, out_ref, cols, grads_ref, pre_ref, tail_ref):
        def spread_rows(start, count):
            total = taps[0:1, :] * ext[start + KC - 1 : start + KC - 1 + count, :]
            for k in range(1, KC):
                at = start + KC - 1 - k
                total = total + taps[k : k + 1, :] * ext[at : at + count, :]
            return total

        head_ref[0:8, cols] = jnp.zeros((8, ext.shape[1]), f32)
        head_ref[8:16, cols] = spread_rows(0, 8)
        grads = [0.0] * (KC + 1)
        for c in range(chunks):
            at = CBLK * c
            dpre = spread_rows(8 + at, CBLK)
            out_ref[at : at + CBLK, :] = dpre.astype(low)
            if c == chunks - 1:
                edge_ref[:, cols] = dpre[CBLK - 16 :, :]
        for k in range(KC):
            shift = KC - 1 - k
            main = jnp.sum(pre_ref[...] * ext[8 + shift : 8 + shift + tokens, :], 0, keepdims=True)
            edge = jnp.sum(tail_ref[...] * ext[shift : shift + 8, :], 0, keepdims=True)
            grads[k] = main + edge
        grads[KC] = jnp.sum(ext[8 : 8 + tokens, :], 0, keepdims=True)
        for k in range(KC + 1):
            grads_ref[k : k + 1, :] = grads[k]
        grads_ref[KC + 1 :, :] = jnp.zeros((grads_ref.shape[0] - KC - 1, ext.shape[1]), f32)

    conv_back(dve, taps_ref, dx_ref, slice(0, channels), gx_ref, x_ref, xt_ref)
    bc_cols = slice(channels, channels + 2 * NS)
    conv_back(dbce, taps_bc_ref, dbc_ref, bc_cols, gbc_ref, bc_ref, bct_ref)


def block(height, width, col=0, first=0):
    return pl.BlockSpec((height, width), lambda s: (first + s, col))


def whole(shape):
    return pl.BlockSpec(shape, lambda s: (0, 0))


def shaped(rows, cols, dtype):
    return jax.ShapeDtypeStruct((rows, cols), dtype)


def run(body, seqs, inputs, outputs, scratch=(), at=None, flops=0, shared=()):
    arrays = [a for a, _ in inputs]
    specs = [s for _, s in inputs]
    if at is not None:
        arrays = [at] + arrays
        specs = [pl.BlockSpec(memory_space=pltpu.SMEM)] + specs
    moved = sum(a.size * a.dtype.itemsize for a in arrays)
    out_specs = [block(r, c) for r, c, _ in outputs]
    out_shape = [shaped(seqs * r, c, d) for r, c, d in outputs]
    aliases, count = {}, len(arrays)
    for r, c, d, total, first, previous in shared:
        if previous is not None:
            aliases[len(arrays)] = len(out_shape)
            arrays.append(previous)
            specs.append(pl.BlockSpec(memory_space=pl.ANY))
        out_specs.append(block(r, c, 0, first))
        out_shape.append(shaped(total * r, c, d))
    kept = len(aliases)

    def inner(*refs):
        body(*refs[:count], *refs[count + kept :])

    return pl.pallas_call(
        inner,
        grid=(seqs,),
        in_specs=specs,
        out_specs=out_specs,
        out_shape=out_shape,
        scratch_shapes=list(scratch),
        input_output_aliases=aliases,
        compiler_params=vmem_params(),
        cost_estimate=pl.CostEstimate(flops=flops, bytes_accessed=moved, transcendentals=0),
    )(*arrays)


def prep(pre, cosine, sine, seqs, tokens, q_at, q_cols, kv_at):
    return run(
        prep_body,
        seqs,
        [
            (pre, block(tokens, q_cols, q_at // q_cols)),
            (pre, block(tokens, 128, kv_at // 128)),
            (cosine, block(tokens, 128)),
            (sine, block(tokens, 128)),
        ],
        [(tokens, q_cols, low), (tokens, 128, low)],
    )


def attend(queries, keyvals, at, seqs, tokens):
    hops, cols = len(keyvals), queries.shape[1]
    work = 4 * seqs * tokens * tokens * hops * (cols // HEAD_SIZE) * 256
    return run(
        functools.partial(attend_body, hops=hops),
        seqs,
        [(queries, block(tokens, cols))] + [(kv, block(tokens, 128)) for kv in keyvals],
        [(tokens, cols, low), (tokens, 128, f32)],
        at=at,
        flops=work,
    )


def attend_back(
    queries, keyvals, grads, grad_at, outs, lse, cosine, sine, at, first, seqs, tokens, previous
):
    hops, cols = len(keyvals), queries.shape[1]
    work = 10 * tokens * tokens * hops * (cols // HEAD_SIZE) * 256
    return run(
        functools.partial(attend_back_body, hops=hops),
        1,
        [
            (queries, block(tokens, cols, 0, first)),
            (grads, block(tokens, cols, grad_at // cols)),
            (outs, block(tokens, cols, 0, first)),
            (lse, block(tokens, 128, 0, first)),
            (cosine, block(tokens, 128, 0, first)),
            (sine, block(tokens, 128, 0, first)),
        ]
        + [(kv, block(tokens, 128, 0, first)) for kv in keyvals],
        [(tokens, cols, low)],
        at=at,
        flops=work,
        shared=[(tokens, 128, low, seqs, first, p) for p in previous],
    )


SENT = NS + 16


class Columns:
    def __init__(self, channels, q_cols):
        self.channels = channels
        self.x, self.z, self.q = 0, channels, 2 * channels
        self.bc = self.q + q_cols
        self.kv = self.bc + 2 * NS
        self.step = self.kv + 128
        self.total = self.step + 128

    def x_block(self, tokens, first=0):
        return block(tokens, self.channels, 0, first)

    def z_block(self, tokens, first=0):
        return block(tokens, self.channels, 1, first)

    def bc_block(self, tokens, first=0):
        return block(tokens, 2 * NS, self.bc // (2 * NS), first)

    def step_block(self, tokens, first=0):
        return block(tokens, 128, self.step // 128, first)


def scan(pre, cols, tails, taps, taps_bc, per_head, seqs, tokens, heads):
    channels = cols.channels
    return run(
        functools.partial(scan_body, heads=heads),
        seqs,
        [
            (pre, cols.x_block(tokens)),
            (pre, cols.bc_block(tokens)),
            (pre, cols.step_block(tokens)),
            (tails, block(8, channels)),
            (tails, block(8, 2 * NS, channels // (2 * NS))),
            (taps, whole(taps.shape)),
            (taps_bc, whole(taps_bc.shape)),
            (per_head, whole(per_head.shape)),
        ],
        [
            (tokens, channels, f32),
            (tokens, 2 * NS, f32),
            (tokens, channels, f32),
            (tokens, 128, f32),
            (tokens // CBLK * NS, channels, f32),
            (SENT, channels, low),
        ],
        scratch=[pltpu.VMEM((tokens + 8, channels), f32), pltpu.VMEM((tokens + 8, 2 * NS), f32)],
        flops=8 * seqs * tokens * CBLK * channels,
    )


def gate(pre, cols, y, v, vbc, logs, per_head, earlier, first, tokens):
    channels = cols.channels
    return run(
        gate_body,
        1,
        [
            (pre, cols.z_block(tokens, first)),
            (y, block(tokens, channels, 0, first)),
            (v, block(tokens, channels, 0, first)),
            (vbc, block(tokens, 2 * NS, 0, first)),
            (logs, block(tokens, 128, 0, first)),
            (per_head, whole(per_head.shape)),
        ]
        + [(a, block(SENT, channels, 0, first)) for a in earlier],
        [(tokens, channels, low), (tokens, channels, f32), (NS, channels, f32)],
        flops=4 * tokens * CBLK * channels,
    )


def gate_back(grads, pre, cols, y, v, vbc, logs, per_head, sent, first, seqs, tokens, previous):
    channels = cols.channels
    return run(
        gate_back_body,
        1,
        [
            (grads, block(tokens, channels)),
            (pre, cols.z_block(tokens, first)),
            (y, block(tokens, channels)),
            (v, block(tokens, channels, 0, first)),
            (vbc, block(tokens, 2 * NS, 0, first)),
            (logs, block(tokens, 128, 0, first)),
            (per_head, whole(per_head.shape)),
            (sent, block(SENT, channels, 0, first)),
        ],
        [
            (tokens, channels, f32),
            (tokens, channels, low),
            (8, channels, f32),
        ],
        flops=4 * tokens * CBLK * channels,
        shared=[(SENT, channels, low, seqs, first, previous)],
    )


def scan_back(
    dy, y, v, vbc, pre, cols, tails, taps, taps_bc, per_head, logs, states, carried, later,
    first, tokens, heads,
):
    channels = cols.channels
    return run(
        functools.partial(scan_back_body, heads=heads),
        1,
        [
            (dy, block(tokens, channels)),
            (y, block(tokens, channels)),
            (v, block(tokens, channels, 0, first)),
            (vbc, block(tokens, 2 * NS, 0, first)),
            (pre, cols.x_block(tokens, first)),
            (pre, cols.bc_block(tokens, first)),
            (pre, cols.step_block(tokens, first)),
            (tails, block(8, channels, 0, first)),
            (tails, block(8, 2 * NS, channels // (2 * NS), first)),
            (taps, whole(taps.shape)),
            (taps_bc, whole(taps_bc.shape)),
            (per_head, whole(per_head.shape)),
            (logs, block(tokens, 128, 0, first)),
            (states, block(tokens // CBLK * NS, channels, 0, first)),
            (carried, block(NS, channels)),
        ]
        + [(a, block(SENT, channels, 0, first)) for a in later],
        [
            (tokens, channels, low),
            (tokens, 2 * NS, low),
            (tokens, 128, low),
            (16, channels + 2 * NS, f32),
            (16, channels + 2 * NS, f32),
            (8, channels, f32),
            (8, 2 * NS, f32),
            (8, 128, f32),
        ],
        scratch=[
            pltpu.VMEM((tokens + 16, channels), f32),
            pltpu.VMEM((tokens + 16, 2 * NS), f32),
        ],
        flops=30 * tokens * CBLK * channels,
    )


TILE = 256


def wide(rows, col=0, width=None):
    return pl.BlockSpec((TILE, rows if width is None else width), lambda t: (t, col))


def tall(array):
    return pl.BlockSpec((array.shape[0], TILE), lambda t: (0, t))


def tiled(body, width, arrays, specs, outputs, scratch, flops):
    return pl.pallas_call(
        body,
        grid=(width // TILE,),
        in_specs=specs,
        out_specs=[spec for _, _, spec in outputs],
        out_shape=[jax.ShapeDtypeStruct(shape, dtype) for shape, dtype, _ in outputs],
        scratch_shapes=scratch,
        compiler_params=vmem_params(),
        cost_estimate=pl.CostEstimate(
            flops=flops,
            bytes_accessed=sum(a.size * a.dtype.itemsize for a in arrays),
            transcendentals=0,
        ),
    )(*arrays)


def early_grads_body(left_ref, wz_ref, wq_ref, *refs, seqs):
    dz, dq, grads, gated = (refs[seqs * i : seqs * i + seqs] for i in range(4))
    attended, ready, out_ref, part_ref, held = refs[-5:]
    tokens = held.shape[0] // seqs
    z_cols = dz[0].shape[1]

    @pl.when(pl.program_id(0) == 0)
    def _():
        for s in range(seqs):
            held[tokens * s : tokens * (s + 1), :z_cols] = dz[s][...]
            held[tokens * s : tokens * (s + 1), z_cols:] = dq[s][...]

    split = held.shape[1]
    out_ref[:, :split] = mm(left_ref[...], held[...]).astype(low)
    first = split + ready.shape[1]
    middle = first + z_cols
    out_ref[:, split:first] = ready[...]
    from_gated, from_attended = 0.0, 0.0
    for s in range(seqs):
        grad = grads[s][...]
        from_gated = from_gated + mm_tn(grad, gated[s][...])
        from_attended = from_attended + mm_tn(grad, attended[tokens * s : tokens * (s + 1), :])
    out_ref[:, first:middle] = from_gated.astype(low)
    out_ref[:, middle:] = from_attended.astype(low)
    part_ref[...] = mm_nt(held[:, :z_cols], wz_ref[...]) + mm_nt(held[:, z_cols:], wq_ref[...])


def early_grads(left, weight, cols, dz, dq, grads, gated, attended, ready):
    width, rows = left.shape
    own = cols.bc - cols.z
    out_cols = own + ready.shape[1] + gated[0].shape[1] + attended.shape[1]
    q_cols = cols.bc - cols.q
    return tiled(
        functools.partial(early_grads_body, seqs=len(dz)),
        width,
        [left, weight, weight, *dz, *dq, *grads, *gated, attended, ready],
        [
            wide(rows),
            wide(cols.channels, cols.z // cols.channels),
            wide(q_cols, cols.q // q_cols),
        ]
        + [whole(a.shape) for a in (*dz, *dq)]
        + [tall(a) for a in grads]
        + [whole(a.shape) for a in (*gated, attended)]
        + [wide(ready.shape[1])],
        [
            ((width, out_cols), low, wide(out_cols)),
            ((rows, width), f32, pl.BlockSpec((rows, TILE), lambda t: (0, t))),
        ],
        [pltpu.VMEM((rows, own), low)],
        2 * rows * width * (own + out_cols),
    )


def late_grads_body(
    left_ref, wx_ref, wbc_ref, wrest_ref, start_ref, head_ref, cos_ref, sin_ref, *refs, seqs, owned
):
    dx, dbc, dstep, edge = (refs[seqs * i : seqs * i + seqs] for i in range(4))
    keyvals, (out_ref, part_ref, held) = refs[4 * seqs : -3], refs[-3:]
    tokens = held.shape[0] // seqs
    channels = dx[0].shape[1]
    conv_cols = channels + dbc[0].shape[1]

    @pl.when(pl.program_id(0) == 0)
    def _():
        for s in range(seqs):
            rows = slice(tokens * s, tokens * (s + 1))
            held[rows, :channels] = dx[s][...]
            held[rows, channels:conv_cols] = dbc[s][...]
            held[rows, conv_cols : conv_cols + 128] = keyval_total(
                cos_ref[rows, :], sin_ref[rows, :], [ref[rows, :] for ref in keyvals]
            )
            held[rows, conv_cols + 128 :] = dstep[s][...]
            held[tokens * (s + 1) - 16 : tokens * (s + 1), :conv_cols] = (
                edge[s][...] + head_ref[16 * s : 16 * s + 16, :]
            ).astype(low)

    terms = mm(left_ref[...], held[...])
    for core in range(2):
        blocks = [terms[at : at + owned] for at in range(core * owned, TILE, 2 * owned)]
        out_ref[core] = jnp.concatenate(blocks, 0).astype(low)
    part_ref[...] = (
        start_ref[...]
        + mm_nt(held[:, :channels], wx_ref[...])
        + mm_nt(held[:, channels:conv_cols], wbc_ref[...])
        + mm_nt(held[:, conv_cols:], wrest_ref[...])
    ).astype(low)


def late_grads(
    left, weight, cols, start, head, cosine, sine, owned, dx, dbc, dstep, edge, keyvals
):
    width, rows = left.shape
    own = cols.total - (cols.bc - cols.z)
    bc_cols, rest = cols.kv - cols.bc, cols.total - cols.kv
    return tiled(
        functools.partial(late_grads_body, seqs=len(dx), owned=owned),
        width,
        [left, weight, weight, weight, start, head, cosine, sine, *dx, *dbc, *dstep, *edge, *keyvals],
        [
            wide(rows),
            wide(cols.channels, 0),
            wide(bc_cols, cols.bc // bc_cols),
            wide(rest, cols.kv // rest),
            tall(start),
        ]
        + [whole(a.shape) for a in (head, cosine, sine, *dx, *dbc, *dstep, *edge, *keyvals)],
        [
            (
                (2, width // 2, own),
                low,
                pl.BlockSpec((2, TILE // 2, own), lambda t: (0, t, 0)),
            ),
            ((rows, width), low, pl.BlockSpec((rows, TILE), lambda t: (0, t))),
        ],
        [pltpu.VMEM((rows, own), low)],
        4 * rows * width * own,
    )


def passed_along(array, axis, distance):
    devices = range(lax.axis_size(axis))
    route = [(i - distance, i) for i in devices if i - distance in devices]
    return lax.ppermute(array, axis, route)


def after(array, *others):
    return lax.optimization_barrier((array, *others))[0]


def swapped(array, axis, distance):
    devices = range(lax.axis_size(axis))
    return lax.ppermute(array, axis, [(i, i ^ distance) for i in devices])


def offer(part):
    mine = part.astype(low)
    return mine, swapped(mine, "tp", 1)


def summed_pair(mine, other):
    return mine.astype(f32) + other.astype(f32)


def sum_over(array, axes):
    for axis in axes:
        distance = 1
        while distance < lax.axis_size(axis):
            array = array + swapped(array, axis, distance)
            distance *= 2
    return array


def place(axis, distance=0):
    return lax.axis_index(axis).astype(jnp.uint32) ^ jnp.uint32(distance)


def place(axis, distance=0):
    return lax.axis_index(axis).astype(jnp.uint32) ^ jnp.uint32(distance)


def picked(array, at, dim):
    return lax.dynamic_index_in_dim(array, at, dim, False)


def states_beside(sent, seqs, side):
    chips = range(lax.axis_size("ctx") // 2)
    near, far = (1, 0) if side < 0 else (0, 1)
    got = lax.ppermute(sent, "ctx", [(2 * k + far, 2 * k + near) for k in chips])
    own, got = (a.reshape(seqs, SENT, -1).astype(f32) for a in (sent, got))
    is_decay = lax.broadcasted_iota(jnp.int32, (1, SENT, 1), 1) >= NS
    got = jnp.where((lax.axis_index("ctx") & 1) == near, got, jnp.where(is_decay, 1.0, 0.0))
    both = jnp.where(is_decay, own * got, own + own[:, NS : NS + 1] * got)
    first, both = (a.astype(low).reshape(sent.shape) for a in (got, both))
    beside = [first]
    for d in chips[1:]:
        for core in range(2):
            route = [(2 * k + near, 2 * (k - side * d) + core) for k in chips if k - side * d in chips]
            beside.append(lax.ppermute(both, "ctx", route))
    return beside


def core_sum(terms):
    dp, ctx = lax.axis_size("dp"), lax.axis_size("ctx")
    one = jnp.uint32(1)
    got = swapped(picked(terms, place("ctx", 1) & one, 0), "ctx", 1)
    total = picked(terms, place("ctx") & one, 0).astype(f32) + got.astype(f32)
    return total.astype(low).reshape(dp, ctx // 2, -1, terms.shape[2])


def spread(held, axis, dim, shift):
    own = picked(held, place(axis) >> jnp.uint32(shift), dim)
    sends = [
        picked(held, place(axis, d << shift) >> jnp.uint32(shift), dim)
        for d in range(1, held.shape[dim])
    ]
    return own, sends, [swapped(a, axis, (d + 1) << shift) for d, a in enumerate(sends)]


def added(own, got):
    total = own.astype(f32)
    for block_in in got:
        total = total + block_in.astype(f32)
    return total


def rms_norm(values, gain):
    return values * lax.rsqrt(jnp.mean(values * values, -1, keepdims=True) + eps_norm) * gain


def angle_tables(positions):
    half = HEAD_SIZE // 2
    freqs = rope_base ** (-2.0 * jnp.arange(half, dtype=f32) / HEAD_SIZE)
    angles = positions.reshape(-1, 1).astype(f32) * freqs
    cosine, sine = jnp.cos(angles), jnp.sin(angles)
    return jnp.tile(cosine, (1, 4)), jnp.concatenate([-sine, sine, -sine, sine], 1)


def per_device(
    hidden_in,
    positions,
    valid_mask,
    teacher,
    cotangent,
    mixer_gain,
    query_weight,
    keyvalue_projection_weight,
    attnout_weight,
    stream_weight,
    state_weight,
    step_weight,
    conv_stream,
    bias_stream,
    conv_state,
    bias_state,
    step_bias,
    decay_log,
    skip_scale,
    mambaout_weight,
    ffn_gain,
    gateup_weight,
    down_weight,
):
    seqs, tokens, width = hidden_in.shape
    owners = ("dp", "ctx")
    rows = query_weight.shape[0]
    q_cols = query_weight.shape[1]
    kv_cols = keyvalue_projection_weight.shape[2]
    channels = stream_weight.shape[2]
    bc_cols = state_weight.shape[1]
    heads = step_weight.shape[1]
    hidden_units = gateup_weight.shape[2]
    step_cols = 128
    hops = lax.axis_size("ctx")
    each = range(seqs)

    tallies = jnp.sum(valid_mask.reshape(seqs * tokens // CBLK, CBLK), -1).astype(low)
    spare = jnp.zeros((rows, step_cols - heads), low)
    spare = spare.at[0, : tallies.shape[0]].set(tallies)
    mixer_shard = jnp.concatenate(
        [
            stream_weight[:, 1],
            stream_weight[:, 0],
            query_weight,
            state_weight,
            keyvalue_projection_weight.reshape(rows, 2 * kv_cols),
            step_weight,
            spare,
            mambaout_weight.T,
            attnout_weight.T,
        ],
        1,
    )
    cols = Columns(channels, q_cols)
    all_cols = cols.total
    mixer_both = lax.all_gather(mixer_shard, owners, axis=0, tiled=True)
    mixer_full, out_full_w = mixer_both[:, :all_cols], mixer_both[:, all_cols:]
    ffn_shard = jnp.concatenate(
        [gateup_weight.reshape(rows, 2 * hidden_units), down_weight.T], 1
    )
    ffn_full = lax.all_gather(ffn_shard, owners, axis=0, tiled=True)
    gateup_full = ffn_full[:, : 2 * hidden_units]
    down_full = ffn_full[:, 2 * hidden_units :]

    counts = mixer_both.reshape(-1, rows, mixer_both.shape[1])
    counts = counts[:, 0, cols.step + heads : cols.step + heads + tallies.shape[0]]
    valid_total = jnp.sum(counts.astype(f32))

    at = lax.axis_index("ctx").astype(jnp.int32).reshape(1)
    cosine, sine = angle_tables(positions)

    def taps_of(taps, bias):
        spare_rows = jnp.zeros((8 - KC - 1, taps.shape[1]), f32)
        return jnp.concatenate([taps, bias[None], spare_rows], 0)

    taps, taps_bc = taps_of(conv_stream, bias_stream), taps_of(conv_state, bias_state)
    per_head = jnp.pad(
        jnp.stack([step_bias, jnp.exp(decay_log), skip_scale]), ((0, 5), (0, 128 - heads))
    )

    hidden = hidden_in.astype(f32)
    normed = rms_norm(hidden, mixer_gain).astype(low).reshape(seqs * tokens, width)
    normed, normed_t = lax.optimization_barrier((normed, normed.T))
    pre = jnp.dot(normed, mixer_full, preferred_element_type=f32)

    def last_rows(array):
        return array.reshape(seqs, tokens, -1)[:, tokens - 8 :].reshape(seqs * 8, -1)

    ends = last_rows(pre)
    ends = jnp.concatenate([ends[:, : cols.z], ends[:, cols.bc : cols.kv]], 1)
    tails = passed_along(ends, "ctx", 1)
    queries, keyval = prep(pre, cosine, sine, seqs, tokens, cols.q, q_cols, cols.kv)
    keyvals = [keyval] + [passed_along(keyval, "ctx", d) for d in range(1, hops)]
    v, vbc, y_own, logs, states, sent = scan(
        after(pre, keyval), cols, tails, taps, taps_bc, per_head, seqs, tokens, heads
    )
    earlier = states_beside(after(sent, *keyvals[1:]), seqs, -1)
    attended, lse = attend(after(queries, earlier[0]), keyvals, at, seqs, tokens)
    gated, y, carried, offers = [], [], [], []
    for s in each:
        here = gate(pre, cols, y_own, v, vbc, logs, per_head, earlier, s, tokens)
        y.append(here[1])
        carried.append(here[2])
        gated.append(here[0])
        mixers = jnp.concatenate([here[0], attended[tokens * s : tokens * (s + 1)]], -1)
        offers.append(
            offer(jnp.einsum("ti,di->td", mixers, out_full_w, preferred_element_type=f32))
        )

    mask_float = valid_mask.astype(f32)[..., None]
    loss_scale = 1.0 / (valid_total * width)
    squares_local = jnp.zeros((), f32)
    resid, normed_two, gateup, inner = [], [], [], []
    down_offers = []
    for s in each:
        mine, other = offers[s]
        other = after(other, offers[-1][0], *(d[0] for d in down_offers))
        resid.append(hidden[s] + summed_pair(mine, other))
        normed_two.append(rms_norm(resid[s], ffn_gain).astype(low))
        gateup.append(jnp.dot(normed_two[s], gateup_full, preferred_element_type=f32))
        inner.append(
            (jax.nn.silu(gateup[s][:, :hidden_units]) * gateup[s][:, hidden_units:]).astype(low)
        )
        down_offers.append(
            offer(jnp.einsum("tf,df->td", inner[s], down_full, preferred_element_type=f32))
        )
    out_full, out_grad, down_in, gateup_low, back_offers = [], [], [], [], []

    def swiglu_flat(both):
        return jax.nn.silu(both[:, :hidden_units]) * both[:, hidden_units:]

    for s in each:
        mine, other = down_offers[s]
        other = after(other, down_offers[-1][0], *(d[0] for d in back_offers))
        out_full.append(resid[s] + summed_pair(mine, other))
        diff = out_full[s] - teacher[s].astype(f32)
        squares_local = squares_local + jnp.sum(mask_float[s] * diff * diff)
        out_grad.append(cotangent[s].astype(f32) + mask_float[s] * 2.0 * diff * loss_scale)
        down_in.append(out_grad[s].astype(low))
        inner_grad = jnp.einsum("td,df->tf", down_in[s], down_full, preferred_element_type=f32)
        gateup_low.append(jax.vjp(swiglu_flat, gateup[s])[1](inner_grad)[0].astype(low))
        mine = jnp.einsum("tc,dc->td", gateup_low[s], gateup_full, preferred_element_type=f32)
        back_offers.append(offer(mine) if s == 0 else (mine.astype(low),))
    block_out = jnp.stack(out_full).astype(low)

    join = lambda parts: jnp.concatenate(parts, 0)
    def wgrad(left, right):
        left, right = join(left), join(right)
        return jnp.einsum("td,tc->dc", left, right, preferred_element_type=f32).astype(low)

    gateup_terms = wgrad(normed_two, gateup_low)

    resid_grad, mixed_low, ffn_gain_grad = [], [], 0.0
    dy, dz, skip_rows, mixers_grads = [], [], [], []
    sent_back = None
    for s in each:
        mine = back_offers[s][0]
        if s == 0:
            other = after(back_offers[s][1], gateup_terms, back_offers[-1][0])
            gateup_reduced = lax.psum_scatter(
                after(gateup_terms, other), owners, scatter_dimension=0, tiled=True
            )
        else:
            other = after(swapped(after(mine, other), "tp", 1), sent_back)
        back = jax.vjp(rms_norm, resid[s], ffn_gain)[1](summed_pair(mine, other))
        resid_grad.append(out_grad[s] + back[0])
        ffn_gain_grad = ffn_gain_grad + back[1]
        mixed_low.append(resid_grad[s].astype(low))
        mixers_grads.append(
            jnp.dot(mixed_low[s], out_full_w, preferred_element_type=f32).astype(low)
        )
        *here, sent_back = gate_back(
            mixers_grads[s], pre, cols, y[s], v, vbc, logs, per_head, sent, s, seqs, tokens,
            sent_back,
        )
        dy.append(here[0])
        dz.append(here[1])
        skip_rows.append(here[2])
    later = states_beside(sent_back, seqs, 1)
    query_back, keyval_parts = [], [None] * hops
    for s in each:
        gq, *keyval_parts = attend_back(
            queries, keyvals, after(mixers_grads[s], later[0]), channels, attended, lse,
            cosine, sine, at, s, seqs, tokens, keyval_parts,
        )
        query_back.append(gq)
    early_terms, part = early_grads(
        after(normed_t, *later), mixer_both, cols, dz, query_back, mixed_low, gated, attended,
        wgrad(down_in, inner),
    )
    early_reduced = lax.psum_scatter(early_terms, owners, scatter_dimension=0, tiled=True)
    keyval_parts = [keyval_parts[0]] + [
        passed_along(keyval_parts[d], "ctx", -d) for d in range(1, hops)
    ]
    scan_backs = []
    for s in each:
        scan_backs.append(
            scan_back(
                after(dy[s], early_terms), y[s], v, vbc, pre, cols, tails, taps, taps_bc, per_head,
                logs, states, carried[s], later, s, tokens, heads,
            )
        )
    head = passed_along(join([scan_backs[s][4] for s in each]), "ctx", -1)
    dx, dbc, dstep, edge = (list(a) for a in list(zip(*scan_backs))[:4])
    late_terms, part = late_grads(
        normed_t, mixer_both, cols, after(part, gateup_reduced), head, cosine, sine, rows,
        dx, dbc, dstep, edge, keyval_parts,
    )
    part = [part[tokens * s : tokens * (s + 1)] for s in each]
    own, sends, got = spread(core_sum(late_terms), "ctx", 1, 1)

    hidden_rows = [hidden[s] for s in each]
    norm_one_back = [jax.vjp(rms_norm, hidden_rows[s], mixer_gain)[1] for s in each]
    mixer_gain_grad = sum(norm_one_back[s](part[s].astype(f32))[1] for s in each)

    tp_index = lax.axis_index("tp")
    tp_count = lax.axis_size("tp")

    def widen(piece, axis_dim):
        shape_full = list(piece.shape)
        shape_full[axis_dim] = piece.shape[axis_dim] * tp_count
        blank = jnp.zeros(tuple(shape_full), f32)
        return lax.dynamic_update_slice_in_dim(
            blank, piece, tp_index * piece.shape[axis_dim], axis_dim
        )

    def narrow(wide, axis_dim, piece_size):
        return lax.dynamic_slice_in_dim(wide, tp_index * piece_size, piece_size, axis_dim)

    conv_sum, conv_bc_sum, head_sum = (
        sum(scan_backs[s][i] for s in each) for i in (5, 6, 7)
    )
    skip_grad = jnp.sum(sum(skip_rows[s][0] for s in each).reshape(heads, MP), -1)
    small = [
        mixer_gain_grad,
        ffn_gain_grad / tp_count,
        widen(conv_sum[: KC + 1], 1),
        conv_bc_sum[: KC + 1],
        widen(jnp.stack([head_sum[0, :heads], head_sum[1, :heads], skip_grad]), 1),
        (squares_local / tp_count).reshape(1),
    ]
    flat = jnp.concatenate([a.reshape(-1) for a in small])
    fill = -flat.shape[0] % 1024
    flat = after(jnp.pad(flat, (0, fill)).reshape(-1, 128), *sends)
    flat = sum_over(flat, ("tp",))
    part_other = [swapped(after(p, flat), "tp", 1) for p in part]
    flat = sum_over(flat, ("dp", "ctx"))
    held = after(added(own, got).astype(low), part_other[0], flat)
    own, sends, got = spread(held, "dp", 0, 0)
    flat = after(flat, *sends).reshape(-1)
    summed, start = [], 0
    for a in small:
        summed.append(flat[start : start + a.size].reshape(a.shape))
        start += a.size
    conv_total = narrow(summed[2], 1, channels)
    head_total = narrow(summed[4], 1, heads)
    loss = summed[5][0] * loss_scale
    small_outs = (summed[0], summed[1], summed[3], conv_total, head_total)
    other = [after(part_other[s], *(small_outs if s else sends)) for s in each]
    normed_grad = join([summed_pair(part[s], other[s]) for s in each])
    norm_back = jax.vjp(rms_norm, hidden.reshape(seqs * tokens, width), mixer_gain)[1]
    input_grad = (join(resid_grad) + norm_back(normed_grad)[0]).astype(low)
    last, early_reduced, _ = lax.optimization_barrier((got[0], early_reduced, input_grad))
    late_reduced = added(own, [last, *got[1:]])
    gateup_reduced = gateup_reduced.astype(f32)
    early_reduced = early_reduced.astype(f32)
    down_reduced = early_reduced[:, channels + q_cols : channels + q_cols + hidden_units]
    out_reduced = early_reduced[:, channels + q_cols + hidden_units :]
    state_reduced = summed_pair(*offer(late_reduced[:, channels : channels + bc_cols]))
    rest = late_reduced[:, channels + bc_cols :]
    return (
        block_out,
        loss,
        input_grad.reshape(seqs, tokens, width),
        summed[0],
        early_reduced[:, channels : channels + q_cols],
        jnp.stack([rest[:, :kv_cols], rest[:, kv_cols : 2 * kv_cols]], 1),
        out_reduced[:, channels:].T,
        jnp.stack([early_reduced[:, :channels], late_reduced[:, :channels]], 1),
        state_reduced,
        rest[:, 2 * kv_cols : 2 * kv_cols + heads],
        conv_total[:KC],
        conv_total[KC],
        summed[3][:KC],
        summed[3][KC],
        head_total[0],
        head_total[1],
        head_total[2],
        out_reduced[:, :channels].T,
        summed[1],
        gateup_reduced.reshape(rows, 2, hidden_units),
        down_reduced.T,
    )


def solution(mesh):
    return jax.shard_map(
        per_device,
        mesh=mesh,
        in_specs=(
            P("dp", "ctx", None),
            P("dp", "ctx"),
            P("dp", "ctx"),
            P("dp", "ctx", None),
            P("dp", "ctx", None),
            P(),
            P(("dp", "ctx"), "tp"),
            P(("dp", "ctx"), None, "tp"),
            P("tp", ("dp", "ctx")),
            P(("dp", "ctx"), None, "tp"),
            P(("dp", "ctx"), None),
            P(("dp", "ctx"), "tp"),
            P(None, "tp"),
            P("tp"),
            P(),
            P(),
            P("tp"),
            P("tp"),
            P("tp"),
            P("tp", ("dp", "ctx")),
            P(),
            P(("dp", "ctx"), None, "tp"),
            P("tp", ("dp", "ctx")),
        ),
        out_specs=(
            P("dp", "ctx", None),
            P(),
            P("dp", "ctx", None),
            P(),
            P(("dp", "ctx"), "tp"),
            P(("dp", "ctx"), None, "tp"),
            P("tp", ("dp", "ctx")),
            P(("dp", "ctx"), None, "tp"),
            P(("dp", "ctx"), None),
            P(("dp", "ctx"), "tp"),
            P(None, "tp"),
            P("tp"),
            P(),
            P(),
            P("tp"),
            P("tp"),
            P("tp"),
            P("tp", ("dp", "ctx")),
            P(),
            P(("dp", "ctx"), None, "tp"),
            P("tp", ("dp", "ctx")),
        ),
        check_vma=False,
    )
```
